32 devices in a mesh: dp: 4 (over z), sp: 8 (over y, x, core).
Axes of the slice: x: 2, y: 2, z: 4, core: 2. Of those that a mesh axis runs over, the one named last changes fastest.
Arguments:
- token_ids: int32 [8, 2048], P('dp'), may hold values from 0 to 50303
- targets: int32 [8, 2048], P('dp'), may hold values from 0 to 50303
- stream_ids: int32 [8], replicated, may hold values 0 or 1
- embed_table: float32 [50304, 1024], P('sp', 'dp'), may hold values from -6 to 6
- embed_first: float32 [50304, 1024], P('sp', 'dp'), may hold values from -2.9802322e-08 to 2.9802322e-08
- embed_second: float32 [50304, 1024], P('sp', 'dp'), may hold values from 9.47911e-17 to 3.791644e-16
- unembed: float32 [1024, 50304], P('dp', 'sp'), may hold values from -0.25 to 0.25
- unembed_first: float32 [1024, 50304], P('dp', 'sp'), may hold values from -5.9604645e-07 to 5.9604645e-07
- unembed_second: float32 [1024, 50304], P('dp', 'sp'), may hold values from 4.3245172e-14 to 1.7298069e-13
- proj_in: float32 [1024, 7168], P(('dp', 'sp')), may hold values from -0.1875 to 0.1875
- proj_in_first: float32 [1024, 7168], P(('dp', 'sp')), may hold values from -5.9604645e-07 to 5.9604645e-07
- proj_in_second: float32 [1024, 7168], P(('dp', 'sp')), may hold values from 4.3245172e-14 to 1.7298069e-13
- proj_out: float32 [5120, 1024], P(('dp', 'sp')), may hold values from -1.25 to 1.25
- proj_out_first: float32 [5120, 1024], P(('dp', 'sp')), may hold values from -5.9604645e-07 to 5.9604645e-07
- proj_out_second: float32 [5120, 1024], P(('dp', 'sp')), may hold values from 4.3245172e-14 to 1.7298069e-13
- norm_params: float32 [6, 1024], P(None, ('dp', 'sp')), may hold values from -0.6 to 1.3
- norm_first: float32 [6, 1024], P(None, ('dp', 'sp')), may hold values from -5.722046e-06 to 5.722046e-06
- norm_second: float32 [6, 1024], P(None, ('dp', 'sp')), may hold values from 4.3245173e-12 to 1.729807e-11
- biases: float32 [8192], P(('dp', 'sp')), may hold values from -1.25 to 1.25
- bias_first: float32 [8192], P(('dp', 'sp')), may hold values from -5.722046e-06 to 5.722046e-06
- bias_second: float32 [8192], P(('dp', 'sp')), may hold values from 4.3245173e-12 to 1.729807e-11
Outputs:
- mean_loss: float32 [], replicated
- grad_norm: float32 [], replicated
- embed_new: float32 [50304, 1024], P('sp', 'dp')
- embed_first_new: float32 [50304, 1024], P('sp', 'dp')
- embed_second_new: float32 [50304, 1024], P('sp', 'dp')
- unembed_new: float32 [1024, 50304], P('dp', 'sp')
- unembed_first_new: float32 [1024, 50304], P('dp', 'sp')
- unembed_second_new: float32 [1024, 50304], P('dp', 'sp')
- proj_in_new: float32 [1024, 7168], P(('dp', 'sp'))
- proj_in_first_new: float32 [1024, 7168], P(('dp', 'sp'))
- proj_in_second_new: float32 [1024, 7168], P(('dp', 'sp'))
- proj_out_new: float32 [5120, 1024], P(('dp', 'sp'))
- proj_out_first_new: float32 [5120, 1024], P(('dp', 'sp'))
- proj_out_second_new: float32 [5120, 1024], P(('dp', 'sp'))
- norm_new: float32 [6, 1024], P(None, ('dp', 'sp'))
- norm_first_new: float32 [6, 1024], P(None, ('dp', 'sp'))
- norm_second_new: float32 [6, 1024], P(None, ('dp', 'sp'))
- bias_new: float32 [8192], P(('dp', 'sp'))
- bias_first_new: float32 [8192], P(('dp', 'sp'))
- bias_second_new: float32 [8192], P(('dp', 'sp'))
The draws below stay inside these ranges and needn't reach their ends.
All inputs are finite; a program needn't handle non-finite values.
Results may differ from the reference program's by a relative error of at most 0.018.
Values may be sent and summed in bfloat16 or wider, within the bound.
A program may use at most 320 MiB of HBM per device.

```python
import math
import jax
import jax.numpy as jnp
from jax import lax

D = 1024
HEADS = 16
HD = 64
ROT = 16
FF = 4096
V = 50304
LEN = 2048
STEP_COUNT = 10
SEQS = 8
NPARAM = 115619840


def draw_proj_out(key, part):
    sample = jnp.clip(jax.random.normal(key, (D + FF, D), jnp.float32), -4.0, 4.0)
    row_place = jnp.arange(D + FF)[:, None]
    factor = jnp.where(row_place < D, 10.0, 0.5) * D ** (-0.5)
    return sample * factor


def draw_norm_params(key, part):
    sample = jnp.clip(jax.random.normal(key, (6, D), jnp.float32), -3.0, 3.0)
    row_place = jnp.arange(6)[:, None]
    return jnp.where(row_place % 2 == 0, 1.0 + 0.1 * sample, 0.2 * sample)


def plant(values, own_key, smallest, top_value):
    extent = values.shape
    spot = [jax.random.randint(jax.random.fold_in(own_key, axis), (), 0, extent[axis]) for axis in range(len(extent))]
    values = values.at[tuple(spot)].set(smallest)
    longest = extent.index(max(extent))
    spot[longest] = (spot[longest] + 1) % extent[longest]
    return values.at[tuple(spot)].set(top_value)


def steps_of(key, extent, split, smallest, largest):
    def one(axis_at, parts):
        heights = jax.random.uniform(jax.random.fold_in(jax.random.fold_in(key, 6), axis_at), (parts,), jnp.float32, smallest / len(split), largest / len(split))
        return jnp.repeat(jnp.exp(heights), extent[axis_at] // parts).reshape((-1,) + (1,) * (len(extent) - axis_at - 1))

    factor_of = one(*split[0])
    for cut in split[1:]:
        factor_of = factor_of * one(*cut)
    return factor_of


def bell_draw(stream_key, extent, spread, reach, shards=(), kind=jnp.bfloat16):
    factor_of = steps_of(stream_key, extent, shards, -0.22, 0.18) if shards else 1.0
    result = jax.random.normal(stream_key, extent, jnp.float32) * spread * factor_of
    return jnp.minimum(jnp.maximum(result, -reach), reach).astype(kind)


def setup_inputs(seed: int = 0) -> dict:
    arg_keys = jax.random.split(jax.random.key(seed), 22)
    token_ids = plant(jax.random.randint(arg_keys[0], (SEQS, LEN), 0, V), jax.random.fold_in(arg_keys[0], 1), 0, V - 1).astype(jnp.int32)
    targets = plant(jax.random.randint(arg_keys[1], (SEQS, LEN), 0, V), jax.random.fold_in(arg_keys[1], 1), 0, V - 1).astype(jnp.int32)
    stream_ids = plant((jax.random.randint(arg_keys[2], (SEQS,), 0, 4) < 1).astype(jnp.int32), jax.random.fold_in(arg_keys[2], 1), 0, 1)
    embed_table = bell_draw(arg_keys[3], (V, D), 1.0, 6.0, ((0, 8), (1, 4)), jnp.float32)
    embed_first = bell_draw(arg_keys[4], (V, D), (0.0011 * D ** -1 * V ** -0.5), 2.9802322387695312e-08, ((0, 8), (1, 4)), jnp.float32)
    embed_second = jnp.clip(jnp.exp(math.log(3.791643991408165e-16) - 1.3862944 * jax.random.uniform(arg_keys[5], (V, D), jnp.float32) ** steps_of(arg_keys[5], (V, D), ((0, 8), (1, 4)), -0.2, 0.2)), 9.479109978520413e-17, 3.791643991408165e-16)
    unembed = bell_draw(arg_keys[6], (D, V), (D // 2) ** -0.5, 0.25, ((0, 4), (1, 8)), jnp.float32)
    unembed_first = bell_draw(arg_keys[7], (D, V), (0.0011 * NPARAM ** -0.5), 5.960464477539062e-07, ((0, 4), (1, 8)), jnp.float32)
    unembed_second = jnp.clip(jnp.exp(math.log(1.7298068901751285e-13) - 1.3862944 * jax.random.uniform(arg_keys[8], (D, V), jnp.float32) ** steps_of(arg_keys[8], (D, V), ((0, 4), (1, 8)), -0.2, 0.2)), 4.324517225437821e-14, 1.7298068901751285e-13)
    proj_in = bell_draw(arg_keys[9], (D, 3 * D + FF), D ** -0.5, 0.1875, ((0, 32),), jnp.float32)
    proj_in_first = bell_draw(arg_keys[10], (D, 3 * D + FF), (0.0011 * NPARAM ** -0.5), 5.960464477539062e-07, ((0, 32),), jnp.float32)
    proj_in_second = jnp.clip(jnp.exp(math.log(1.7298068901751285e-13) - 1.3862944 * jax.random.uniform(arg_keys[11], (D, 3 * D + FF), jnp.float32) ** steps_of(arg_keys[11], (D, 3 * D + FF), ((0, 32),), -0.2, 0.2)), 4.324517225437821e-14, 1.7298068901751285e-13)
    proj_out = draw_proj_out(jax.random.fold_in(arg_keys[21], 71), 0)
    proj_out_first = bell_draw(arg_keys[13], (D + FF, D), (0.0011 * NPARAM ** -0.5), 5.960464477539062e-07, ((0, 32),), jnp.float32)
    proj_out_second = jnp.clip(jnp.exp(math.log(1.7298068901751285e-13) - 1.3862944 * jax.random.uniform(arg_keys[14], (D + FF, D), jnp.float32) ** steps_of(arg_keys[14], (D + FF, D), ((0, 32),), -0.2, 0.2)), 4.324517225437821e-14, 1.7298068901751285e-13)
    norm_params = draw_norm_params(jax.random.fold_in(arg_keys[21], 71), 0)
    norm_first = bell_draw(arg_keys[16], (6, D), (0.011 * NPARAM ** -0.5), 5.7220458984375e-06, ((1, 32),), jnp.float32)
    norm_second = jnp.clip(jnp.exp(math.log(1.7298069227011936e-11) - 1.3862944 * jax.random.uniform(arg_keys[17], (6, D), jnp.float32) ** steps_of(arg_keys[17], (6, D), ((1, 32),), -0.2, 0.2)), 4.324517306752984e-12, 1.7298069227011936e-11)
    biases = bell_draw(arg_keys[18], (4 * D + FF,), 0.2, 1.25, ((0, 32),), jnp.float32)
    bias_first = bell_draw(arg_keys[19], (4 * D + FF,), (0.011 * NPARAM ** -0.5), 5.7220458984375e-06, ((0, 32),), jnp.float32)
    bias_second = jnp.clip(jnp.exp(math.log(1.7298069227011936e-11) - 1.3862944 * jax.random.uniform(arg_keys[20], (4 * D + FF,), jnp.float32) ** steps_of(arg_keys[20], (4 * D + FF,), ((0, 32),), -0.2, 0.2)), 4.324517306752984e-12, 1.7298069227011936e-11)
    return {"token_ids": token_ids, "targets": targets, "stream_ids": stream_ids, "embed_table": embed_table, "embed_first": embed_first, "embed_second": embed_second, "unembed": unembed, "unembed_first": unembed_first, "unembed_second": unembed_second, "proj_in": proj_in, "proj_in_first": proj_in_first, "proj_in_second": proj_in_second, "proj_out": proj_out, "proj_out_first": proj_out_first, "proj_out_second": proj_out_second, "norm_params": norm_params, "norm_first": norm_first, "norm_second": norm_second, "biases": biases, "bias_first": bias_first, "bias_second": bias_second}


@jax.custom_vjp
def low(v):
    return lax.optimization_barrier(v.astype(jnp.bfloat16)).astype(jnp.float32)

@jax.custom_vjp
def low_back(v):
    return v

def low_keep(v):
    return (low(v), None)

def low_pass(kept, grad):
    return (grad,)

def back_keep(v):
    return (v, None)

def back_low(kept, grad):
    return (low(grad),)
low.defvjp(low_keep, low_pass)
low_back.defvjp(back_keep, back_low)
NORM_EPS = 1e-05
BETA_ONE = 0.9
BETA_TWO = 0.95
ADAM_EPS = 1e-08
WEIGHT_DECAY = 0.01
CLIP_LEVEL = 0.01
REPLAY_WEIGHT = 4.0
NEGATIVE_FILL = -1e+30
HIGHEST = lax.Precision.HIGHEST

def layer_norm(values, gain_row, shift_row):
    average = lax.optimization_barrier(jnp.mean(values, axis=-1, keepdims=True))
    centered = values - average
    variance = lax.optimization_barrier(jnp.mean(centered * centered, axis=-1, keepdims=True))
    return centered * lax.rsqrt(variance + NORM_EPS) * gain_row + shift_row

def rotary_tables(positions):
    halfway = ROT // 2
    frequency = 10000.0 ** (-2.0 * jnp.arange(halfway, dtype=jnp.float32) / ROT)
    angles = positions.astype(jnp.float32)[:, None] * frequency[None, :]
    angles = jnp.concatenate([angles, angles], axis=-1)
    return (jnp.cos(angles), jnp.sin(angles))

def rotate(values, cosine, sine_part):
    halfway = ROT // 2
    turned_part = values[..., :ROT]
    turned = jnp.concatenate([-turned_part[..., halfway:], turned_part[..., :halfway]], axis=-1)
    rotated = turned_part * cosine[:, None, :] + turned * sine_part[:, None, :]
    return jnp.concatenate([rotated, values[..., ROT:]], axis=-1)

def sequence_loss(weights, tokens, labels):
    table, head_table, wide_in, wide_out, norm_rows, bias_all = weights
    width = D
    hidden0 = low_back(jnp.take(table, tokens, axis=0))
    normed_one = low(layer_norm(hidden0, norm_rows[0], norm_rows[1]))
    normed_two = low(layer_norm(hidden0, norm_rows[2], norm_rows[3]))
    joint_proj = low_back(jnp.dot(normed_one, wide_in[:, :3 * width], precision=HIGHEST) + bias_all[:3 * width])
    joint_proj = joint_proj.reshape(LEN, HEADS, 3, HD)
    cosine, sine_part = rotary_tables(jnp.arange(LEN))
    queries = low_back(low(rotate(joint_proj[:, :, 0], cosine, sine_part)))
    keys_all = low_back(low(rotate(joint_proj[:, :, 1], cosine, sine_part)))
    values_all = low_back(low(joint_proj[:, :, 2]))
    scores = low_back(jnp.einsum('qhd,khd->hqk', queries, keys_all, precision=HIGHEST) * HD ** (-0.5))
    causal = jnp.arange(LEN)[:, None] >= jnp.arange(LEN)[None, :]
    scores = jnp.where(causal[None], scores, NEGATIVE_FILL)
    probs = low(jax.nn.softmax(scores, axis=-1))
    attended = jnp.einsum('hqk,khd->qhd', probs, values_all, precision=HIGHEST)
    attended = low_back(low(attended)).reshape(LEN, width)
    up_values = low_back(jnp.dot(normed_two, wide_in[:, 3 * width:], precision=HIGHEST) + bias_all[3 * width:3 * width + FF])
    act = low(jax.nn.gelu(up_values, approximate=False))
    joined = jnp.concatenate([attended, act], axis=-1)
    branch = low_back(jnp.dot(joined, wide_out, precision=HIGHEST) + bias_all[3 * width + FF:])
    hidden1 = hidden0 + branch
    final = low(layer_norm(hidden1, norm_rows[4], norm_rows[5]))
    logits = low_back(jnp.dot(final, head_table, precision=HIGHEST))
    log_sum = jax.nn.logsumexp(logits, axis=-1)
    chosen = jnp.take_along_axis(logits, labels[:, None], axis=-1)[:, 0]
    return jnp.mean(log_sum - chosen)

def total_loss(weights, token_ids, targets, stream_ids):

    def one_sequence(sequence_pair):
        return jax.checkpoint(sequence_loss)(weights, sequence_pair[0], sequence_pair[1])
    per_sequence = lax.map(one_sequence, (token_ids, targets))
    seq_weight = 1.0 + (REPLAY_WEIGHT - 1.0) * stream_ids.astype(jnp.float32)
    return jnp.sum(seq_weight * per_sequence) / jnp.sum(seq_weight)

def adam_update(weight, first, second, grad, clip_factor, rate, decay):
    grad = grad * clip_factor
    first_new = BETA_ONE * first + (1.0 - BETA_ONE) * grad
    second_new = BETA_TWO * second + (1.0 - BETA_TWO) * grad * grad
    fix_one = 1.0 - BETA_ONE ** STEP_COUNT
    fix_two = 1.0 - BETA_TWO ** STEP_COUNT
    direction = first_new / fix_one / (jnp.sqrt(second_new / fix_two) + ADAM_EPS)
    return (weight - rate * (direction + decay * weight), first_new, second_new)

def reference(token_ids, targets, stream_ids, embed_table, embed_first, embed_second, unembed, unembed_first, unembed_second, proj_in, proj_in_first, proj_in_second, proj_out, proj_out_first, proj_out_second, norm_params, norm_first, norm_second, biases, bias_first, bias_second):
    masters = (embed_table, unembed, proj_in, proj_out, norm_params, biases)

    def forward(table, head_table, wide_in, wide_out, norm_rows, bias_all):
        lowered = (low(table), low(head_table), low(wide_in), low(wide_out), low(norm_rows), low(bias_all))
        return total_loss(lowered, token_ids, targets, stream_ids)
    mean_loss, pull_back = jax.vjp(forward, *masters)
    grads = pull_back(jnp.ones_like(mean_loss))
    squares = jnp.float32(0.0)
    for grad in grads:
        squares = squares + jnp.sum(grad * grad)
    grad_norm = jnp.sqrt(squares)
    clip_factor = jnp.minimum(1.0, CLIP_LEVEL / (grad_norm + 1e-06))
    firsts = (embed_first, unembed_first, proj_in_first, proj_out_first, norm_first, bias_first)
    seconds = (embed_second, unembed_second, proj_in_second, proj_out_second, norm_second, bias_second)
    rates = (1.0, 0.05, 0.05, 0.1, 0.5, 0.5)
    decays = (WEIGHT_DECAY, WEIGHT_DECAY, WEIGHT_DECAY, WEIGHT_DECAY, 0.0, 0.0)
    results = []
    for index in range(6):
        results.extend(adam_update(masters[index], firsts[index], seconds[index], grads[index], clip_factor, rates[index], decays[index]))
    return (mean_loss, grad_norm, results[0], results[1], results[2], results[3], results[4], results[5], results[6], results[7], results[8], results[9], results[10], results[11], results[12], results[13], results[14], results[15], results[16], results[17])
```

```python
from functools import partial

import jax
import jax.numpy as jnp
from jax import lax
from jax.experimental import pallas as pl
from jax.experimental.pallas import tpu as pltpu
from jax.sharding import PartitionSpec as P

HEADS = 16
ROT = 16
STEP_COUNT = 10


NORM_EPS = 1e-05
BETA_ONE = 0.9
BETA_TWO = 0.95
ADAM_EPS = 1e-08
WEIGHT_DECAY = 0.01
CLIP_LEVEL = 0.01
REPLAY_WEIGHT = 4.0
NEGATIVE_FILL = -1e30
LOW = jnp.bfloat16
WIDE = jnp.float32
CHUNKS = 5
LANES = 128
HEAD_ROWS = 512
ATTEND_ROWS = 1024
VMEM_LIMIT = 60 * 1024 * 1024


def lane_of(shape):
    return lax.broadcasted_iota(jnp.int32, shape, 1)


def head_forward_kernel(real, rows_ref, table_ref, label_ref, powers_ref, stats_ref, lines_ref):
    padded = table_ref.shape[0]
    part = padded // CHUNKS
    rows = rows_ref[...]
    count = rows.shape[0]
    label = label_ref[...]
    lane = lane_of((count, LANES))
    stats = jnp.zeros((count, LANES), WIDE)
    tops, sums = [], []
    chosen = jnp.zeros((count, 1), WIDE)
    for c in range(CHUNKS):
        logits = lax.dot_general(
            rows,
            table_ref[c * part : (c + 1) * part, :],
            (((1,), (1,)), ((), ())),
            preferred_element_type=WIDE,
        )
        column = lane_of(logits.shape) + c * part
        chosen = chosen + jnp.sum(jnp.where(column == label, logits, 0.0), axis=1, keepdims=True)
        if (c + 1) * part > real:
            logits = jnp.where(column < real, logits, NEGATIVE_FILL)
        top = jnp.max(logits, axis=1, keepdims=True)
        powers = jnp.exp(logits - top)
        sums.append(jnp.sum(powers, axis=1, keepdims=True))
        tops.append(top)
        powers_ref[:, c * part : (c + 1) * part] = powers.astype(LOW)
        stats = jnp.where(lane == 8 + c, top, stats)
    highest = tops[0]
    for c in range(1, CHUNKS):
        highest = jnp.maximum(highest, tops[c])
    total = jnp.zeros((count, 1), WIDE)
    for c in range(CHUNKS):
        total = total + sums[c] * jnp.exp(tops[c] - highest)
    stats = jnp.where(lane == 0, highest, stats)
    stats = jnp.where(lane == 1, total, stats)
    stats = jnp.where(lane == 2, chosen, stats)
    stats_ref[...] = stats
    lines_ref[...] = jnp.transpose(stats)[0:8, :]


def head_forward(rows, table, label, real):
    total, width = rows.shape
    padded = table.shape[0]
    count = min(HEAD_ROWS, total)
    return pl.pallas_call(
        partial(head_forward_kernel, real),
        grid=(total // count,),
        in_specs=[
            pl.BlockSpec((count, width), lambda i: (i, 0)),
            pl.BlockSpec((padded, width), lambda i: (0, 0), pipeline_mode=pl.Buffered(1)),
            pl.BlockSpec((count, 1), lambda i: (i, 0)),
        ],
        out_specs=[
            pl.BlockSpec((count, padded), lambda i: (i, 0)),
            pl.BlockSpec((count, LANES), lambda i: (i, 0)),
            pl.BlockSpec((8, count), lambda i: (0, i)),
        ],
        out_shape=[
            jax.ShapeDtypeStruct((total, padded), LOW),
            jax.ShapeDtypeStruct((total, LANES), WIDE),
            jax.ShapeDtypeStruct((8, total), WIDE),
        ],
        cost_estimate=pl.CostEstimate(
            flops=2 * total * width * padded,
            bytes_accessed=2 * (total * (width + padded) + width * padded),
            transcendentals=total * padded,
        ),
        compiler_params=pltpu.CompilerParams(vmem_limit_bytes=VMEM_LIMIT),
        name="head_forward",
    )(rows, table, label)


def head_backward_kernel(stats_ref, lines_ref, label_ref, powers_ref, table_ref, slope_ref, grad_ref):
    padded = table_ref.shape[0]
    part = padded // CHUNKS
    stats = stats_ref[...]
    label = label_ref[...]
    lines = lines_ref[...]
    lines = jnp.transpose(jnp.concatenate([lines] * (LANES // 8), axis=0))
    lse = lines[:, 0:1]
    scale = lines[:, 1:2]
    total = None
    for c in range(CHUNKS):
        ratio = scale * jnp.exp(stats[:, 8 + c : 9 + c] - lse)
        slope = powers_ref[:, c * part : (c + 1) * part].astype(WIDE) * ratio
        column = lane_of(slope.shape) + c * part
        slope = jnp.where(column == label, slope - scale, slope).astype(LOW)
        slope_ref[:, c * part : (c + 1) * part] = slope
        piece = jnp.dot(
            slope, table_ref[c * part : (c + 1) * part, :], preferred_element_type=WIDE
        )
        total = piece if total is None else total + piece
    grad_ref[...] = total.astype(LOW)


def head_backward(stats, lines, label, powers, table):
    total, padded = powers.shape
    width = table.shape[1]
    count = min(HEAD_ROWS, total)
    return pl.pallas_call(
        head_backward_kernel,
        grid=(total // count,),
        in_specs=[
            pl.BlockSpec((count, LANES), lambda i: (i, 0)),
            pl.BlockSpec((8, count), lambda i: (0, i)),
            pl.BlockSpec((count, 1), lambda i: (i, 0)),
            pl.BlockSpec((count, padded), lambda i: (i, 0)),
            pl.BlockSpec((padded, width), lambda i: (0, 0), pipeline_mode=pl.Buffered(1)),
        ],
        out_specs=[
            pl.BlockSpec((count, padded), lambda i: (i, 0)),
            pl.BlockSpec((count, width), lambda i: (i, 0)),
        ],
        out_shape=[
            jax.ShapeDtypeStruct((total, padded), LOW),
            jax.ShapeDtypeStruct((total, width), LOW),
        ],
        cost_estimate=pl.CostEstimate(
            flops=2 * total * width * padded,
            bytes_accessed=2 * (total * (width + 2 * padded) + width * padded),
            transcendentals=0,
        ),
        compiler_params=pltpu.CompilerParams(vmem_limit_bytes=VMEM_LIMIT),
        name="head_backward",
    )(stats, lines, label, powers, table)


def attend_forward_kernel(heads, scale, query_ref, key_ref, value_ref, out_ref, lse_ref):
    pieces, stretch, wide = query_ref.shape
    block = pieces * stretch
    head = wide // heads
    index = pl.program_id(1)
    query = query_ref[...].reshape(block, wide) * jnp.asarray(scale, LOW)
    lane = lane_of((block, wide))
    mine = [(lane >= h * head) & (lane < (h + 1) * head) for h in range(heads)]
    own = [jnp.where(mine[h], query, jnp.zeros_like(query)) for h in range(heads)]

    def step(c, state, masked):
        spots = pl.ds(c * pieces, pieces)
        keys = key_ref[spots].reshape(block, wide)
        values = value_ref[spots].reshape(block, wide)
        fresh = []
        for h in range(heads):
            top, total, summed = state[h]
            scores = lax.dot_general(
                own[h], keys, (((1,), (1,)), ((), ())), preferred_element_type=WIDE
            )
            if masked:
                here = lax.broadcasted_iota(jnp.int32, scores.shape, 0)
                scores = jnp.where(here >= lane_of(scores.shape), scores, NEGATIVE_FILL)
            higher = jnp.maximum(top, jnp.max(scores, axis=1, keepdims=True))
            powers = jnp.exp(scores - higher)
            shrink = jnp.exp(top - higher)
            total = total * shrink + jnp.sum(powers, axis=1, keepdims=True)
            summed = summed * shrink + jnp.dot(
                powers.astype(LOW), values, preferred_element_type=WIDE
            )
            fresh.append((higher, total, summed))
        return tuple(fresh)

    state = tuple(
        (
            jnp.full((block, 1), NEGATIVE_FILL, WIDE),
            jnp.zeros((block, 1), WIDE),
            jnp.zeros((block, wide), WIDE),
        )
        for _ in range(heads)
    )
    state = lax.fori_loop(0, index, lambda c, s: step(c, s, False), state)
    state = step(index, state, True)
    result = None
    spot = lane_of((block, LANES))
    logs = jnp.zeros((block, LANES), WIDE)
    for h in range(heads):
        top, total, summed = state[h]
        piece = summed / total
        result = piece if result is None else jnp.where(mine[h], piece, result)
        logs = jnp.where(spot == h, top + jnp.log(total), logs)
    out_ref[...] = result.astype(LOW).reshape(pieces, stretch, wide)
    lse_ref[...] = jnp.transpose(logs)[0:8, :]


def attend_specs(triple, block):
    span, _, seqs, stretch, wide = triple.shape
    pieces = min(block, span * stretch) // stretch
    part = pl.BlockSpec((pieces, None, stretch, wide), lambda s, i: (i, s, 0, 0))
    query = pl.BlockSpec((pieces, None, None, stretch, wide), lambda s, i: (i, 0, s, 0, 0))
    keys = pl.BlockSpec((span, None, None, stretch, wide), lambda s, i: (0, 1, s, 0, 0))
    values = pl.BlockSpec((span, None, None, stretch, wide), lambda s, i: (0, 2, s, 0, 0))
    logs = pl.BlockSpec((None, 8, pieces * stretch), lambda s, i: (s, 0, i))
    return (seqs, span // pieces), part, query, keys, values, logs


def attend_forward(triple, heads, block, scale):
    span, _, seqs, stretch, wide = triple.shape
    length = span * stretch
    grid, part, query, keys, values, logs = attend_specs(triple, block)
    pairs = seqs * heads * length * length // 2
    return pl.pallas_call(
        partial(attend_forward_kernel, heads, scale),
        grid=grid,
        in_specs=[query, keys, values],
        out_specs=[part, logs],
        out_shape=[
            jax.ShapeDtypeStruct((span, seqs, stretch, wide), LOW),
            jax.ShapeDtypeStruct((seqs, 8, length), WIDE),
        ],
        cost_estimate=pl.CostEstimate(
            flops=pairs, bytes_accessed=seqs * length * wide, transcendentals=0
        ),
        compiler_params=pltpu.CompilerParams(vmem_limit_bytes=VMEM_LIMIT),
        name="attend_forward",
    )(triple, triple, triple)


def attend_backward_kernel(
    heads, scale, query_ref, key_ref, value_ref, out_ref, grad_ref, lse_ref, triple_ref, dk_sum, dv_sum
):
    pieces, stretch, wide = query_ref.shape
    block = pieces * stretch
    span = key_ref.shape[0]
    head = wide // heads
    index = pl.program_id(1)

    @pl.when(index == 0)
    def _():
        dk_sum[...] = jnp.zeros_like(dk_sum)
        dv_sum[...] = jnp.zeros_like(dv_sum)

    query = query_ref[...].reshape(block, wide) * jnp.asarray(scale, LOW)
    grad = grad_ref[...].reshape(block, wide)
    lane = lane_of((block, wide))
    mine = [(lane >= h * head) & (lane < (h + 1) * head) for h in range(heads)]
    zero = jnp.zeros_like(query)
    own_query = [jnp.where(mine[h], query, zero) for h in range(heads)]
    own_grad = [jnp.where(mine[h], grad, zero) for h in range(heads)]
    product = out_ref[...].reshape(block, wide).astype(WIDE) * grad.astype(WIDE)
    spot = lane_of((block, LANES))
    centres = jnp.zeros((block, LANES), WIDE)
    for h in range(heads):
        centre = jnp.sum(jnp.where(mine[h], product, 0.0), axis=1, keepdims=True)
        centres = jnp.where(spot == h, centre, centres)
    centres = jnp.transpose(centres)
    logs = lse_ref[...]

    def step(c, state, masked):
        spots = pl.ds(c * pieces, pieces)
        rows = pl.ds(pl.multiple_of(c * block, block), block)
        keys = key_ref[spots].reshape(block, wide)
        values = value_ref[spots].reshape(block, wide)
        fresh = []
        key_part, value_part = None, None
        for h in range(heads):
            scores = lax.dot_general(
                keys, own_query[h], (((1,), (1,)), ((), ())), preferred_element_type=WIDE
            )
            probs = jnp.exp(scores - logs[h : h + 1, :])
            if masked:
                here = lax.broadcasted_iota(jnp.int32, scores.shape, 0)
                probs = jnp.where(here <= lane_of(scores.shape), probs, 0.0)
            grad_probs = lax.dot_general(
                values, own_grad[h], (((1,), (1,)), ((), ())), preferred_element_type=WIDE
            )
            slope = (probs * (grad_probs - centres[h : h + 1, :])).astype(LOW)
            a = jnp.dot(slope, own_query[h], preferred_element_type=WIDE)
            b = jnp.dot(probs.astype(LOW), own_grad[h], preferred_element_type=WIDE)
            key_part = a if key_part is None else key_part + a
            value_part = b if value_part is None else value_part + b
            fresh.append(
                state[h]
                + lax.dot_general(slope, keys, (((0,), (0,)), ((), ())), preferred_element_type=WIDE)
            )
        dk_sum[rows, :] += key_part
        dv_sum[rows, :] += value_part
        return tuple(fresh)

    state = tuple(jnp.zeros((block, wide), WIDE) for _ in range(heads))
    state = lax.fori_loop(0, index, lambda c, s: step(c, s, False), state)
    state = step(index, state, True)
    result = state[0]
    for h in range(1, heads):
        result = jnp.where(mine[h], state[h], result)
    triple_ref[pl.ds(index * pieces, pieces), 0] = (
        (result * scale).astype(LOW).reshape(pieces, stretch, wide)
    )

    @pl.when(index == pl.num_programs(1) - 1)
    def _():
        triple_ref[:, 1] = dk_sum[...].astype(LOW).reshape(span, stretch, wide)
        triple_ref[:, 2] = dv_sum[...].astype(LOW).reshape(span, stretch, wide)


def attend_backward(triple, attended, grad, lse, heads, block, scale):
    span, _, seqs, stretch, wide = triple.shape
    length = span * stretch
    grid, part, query, keys, values, logs = attend_specs(triple, block)
    pairs = seqs * heads * length * length // 2
    return pl.pallas_call(
        partial(attend_backward_kernel, heads, scale),
        grid=grid,
        in_specs=[query, keys, values, part, part, logs],
        out_specs=pl.BlockSpec((span, 3, None, stretch, wide), lambda s, i: (0, 0, s, 0, 0)),
        out_shape=jax.ShapeDtypeStruct((span, 3, seqs, stretch, wide), LOW),
        scratch_shapes=[pltpu.VMEM((length, wide), WIDE), pltpu.VMEM((length, wide), WIDE)],
        cost_estimate=pl.CostEstimate(
            flops=pairs, bytes_accessed=seqs * length * wide, transcendentals=0
        ),
        compiler_params=pltpu.CompilerParams(vmem_limit_bytes=VMEM_LIMIT),
        name="attend_backward",
    )(triple, triple, triple, attended, grad, lse)


def turn_tables(positions, repeats, parts, wide, head):
    halfway = ROT // 2
    place = jnp.arange(parts * wide)
    entry = place % head
    turned = (place // wide < 2) & (entry < ROT)
    frequency = 10000.0 ** (-2.0 * (entry % halfway).astype(WIDE) / ROT)
    angles = positions.astype(WIDE)[:, None] * frequency[None, :]
    sine = jnp.where(turned, jnp.sin(angles), 0.0)
    cosine = jnp.where(turned, jnp.cos(angles), 1.0)
    later = jnp.where(entry < halfway, -sine, 0.0)
    earlier = jnp.where(entry < halfway, 0.0, sine)
    return tuple(jnp.tile(table, (1, repeats)) for table in (cosine, later, earlier))


def turn_packs(span, wide):
    return 1 if (3 * wide) % LANES == 0 else 2


def queries_kernel(seqs, wide, rows_ref, table_ref, bias_ref, cosine_ref, later_ref, earlier_ref, out_ref):
    halfway = ROT // 2
    columns = table_ref.shape[1]
    values = jnp.dot(rows_ref[...], table_ref[...], preferred_element_type=WIDE) + bias_ref[...]
    stretch = cosine_ref.shape[0]
    for s in range(seqs):
        part = values[s * stretch : (s + 1) * stretch]
        part = (
            part * cosine_ref[...]
            + pltpu.roll(part, columns - halfway, 1) * later_ref[...]
            + pltpu.roll(part, halfway, 1) * earlier_ref[...]
        ).astype(LOW)
        for j in range(columns // wide):
            out_ref[j // 3, j % 3, s] = part[:, j * wide : (j + 1) * wide]


def project_queries(rows, table, bias, tables, span, seqs, wide):
    total, width = rows.shape
    stretch = total // seqs
    packs = turn_packs(span, wide)
    columns = packs * 3 * wide
    fixed = pl.BlockSpec((stretch, columns), lambda g: (0, 0))
    return pl.pallas_call(
        partial(queries_kernel, seqs, wide),
        grid=(span // packs,),
        in_specs=[
            pl.BlockSpec((total, width), lambda g: (0, 0)),
            pl.BlockSpec((width, columns), lambda g: (0, g)),
            pl.BlockSpec((1, columns), lambda g: (0, g)),
            fixed,
            fixed,
            fixed,
        ],
        out_specs=pl.BlockSpec((packs, 3, seqs, stretch, wide), lambda g: (g, 0, 0, 0, 0)),
        out_shape=jax.ShapeDtypeStruct((span, 3, seqs, stretch, wide), LOW),
        cost_estimate=pl.CostEstimate(
            flops=2 * total * width * span * 3 * wide,
            bytes_accessed=2 * width * span * 3 * wide,
            transcendentals=0,
        ),
        compiler_params=pltpu.CompilerParams(vmem_limit_bytes=VMEM_LIMIT),
        name="project_queries",
    )(rows, table, bias, *tables)


def unturn_kernel(seqs, wide, triple_ref, cosine_ref, later_ref, earlier_ref, out_ref):
    halfway = ROT // 2
    columns = out_ref.shape[1]
    stretch = cosine_ref.shape[0]
    for s in range(seqs):
        part = jnp.concatenate(
            [triple_ref[j // 3, j % 3, s].astype(WIDE) for j in range(columns // wide)], axis=1
        )
        part = (
            part * cosine_ref[...]
            - pltpu.roll(part, columns - halfway, 1) * later_ref[...]
            - pltpu.roll(part, halfway, 1) * earlier_ref[...]
        )
        out_ref[s * stretch : (s + 1) * stretch, :] = part.astype(LOW)


def unturn(triple, tables):
    span, _, seqs, stretch, wide = triple.shape
    packs = turn_packs(span, wide)
    columns = packs * 3 * wide
    fixed = pl.BlockSpec((stretch, columns), lambda g: (0, 0))
    return pl.pallas_call(
        partial(unturn_kernel, seqs, wide),
        grid=(span // packs,),
        in_specs=[
            pl.BlockSpec((packs, 3, seqs, stretch, wide), lambda g: (g, 0, 0, 0, 0)),
            fixed,
            fixed,
            fixed,
        ],
        out_specs=pl.BlockSpec((seqs * stretch, columns), lambda g: (0, g)),
        out_shape=jax.ShapeDtypeStruct((seqs * stretch, span * 3 * wide), LOW),
        compiler_params=pltpu.CompilerParams(vmem_limit_bytes=VMEM_LIMIT),
        name="unturn",
    )(triple, *tables)


def gelu_exact(values):
    return jax.nn.gelu(values, approximate=False)


def standardize(values):
    average = jnp.mean(values, axis=-1, keepdims=True)
    centered = values - average
    variance = jnp.mean(centered * centered, axis=-1, keepdims=True)
    inverse = lax.rsqrt(variance + NORM_EPS)
    return centered * inverse, inverse


def standardize_pull(scaled, normal, inverse):
    return inverse * (
        scaled
        - jnp.mean(scaled, axis=-1, keepdims=True)
        - normal * jnp.mean(scaled * normal, axis=-1, keepdims=True)
    )


def adam_update(weight, first, second, grad, clip_factor, rate, decay):
    grad = grad * clip_factor
    first_new = BETA_ONE * first + (1.0 - BETA_ONE) * grad
    second_new = BETA_TWO * second + (1.0 - BETA_TWO) * grad * grad
    fix_one = 1.0 - BETA_ONE**STEP_COUNT
    fix_two = 1.0 - BETA_TWO**STEP_COUNT
    direction = first_new / fix_one / (jnp.sqrt(second_new / fix_two) + ADAM_EPS)
    return (weight - rate * (direction + decay * weight), first_new, second_new)


def summed_over(vector, axes):
    for axis in axes:
        vector = jnp.sum(lax.all_gather(vector, axis), axis=0)
    return vector


def scattered(gradient):
    return lax.psum_scatter(gradient, ("dp", "sp"), scatter_dimension=0, tiled=True).astype(WIDE)


def local(
    token_ids,
    targets,
    stream_ids,
    embed_table,
    embed_first,
    embed_second,
    unembed,
    unembed_first,
    unembed_second,
    proj_in,
    proj_in_first,
    proj_in_second,
    proj_out,
    proj_out_first,
    proj_out_second,
    norm_params,
    norm_first,
    norm_second,
    biases,
    bias_first,
    bias_second,
):
    span = lax.axis_size("sp")
    teams = lax.axis_size("dp")
    sp_index = lax.axis_index("sp")
    dp_index = lax.axis_index("dp")
    seq_here, length = token_ids.shape
    stretch = length // span
    vocab_local = embed_table.shape[0]
    slab, in_columns = proj_in.shape
    width = proj_out.shape[1]
    triple_columns = 3 * width
    hidden_units = in_columns - triple_columns
    heads_here = HEADS // span
    head_dim = width // HEADS
    wide = heads_here * head_dim
    scale = head_dim ** (-0.5)
    tokens_here = seq_here * stretch
    offset = sp_index * vocab_local

    ids_all = lax.all_gather(token_ids, "dp")
    ids_all = ids_all.reshape(teams, seq_here, span, stretch).transpose(2, 0, 1, 3).reshape(-1)
    local_ids = ids_all - offset
    in_slice = (local_ids >= 0) & (local_ids < vocab_local)
    safe_ids = jnp.clip(local_ids, 0, vocab_local - 1)
    picked = jnp.where(
        in_slice[:, None],
        embed_table.astype(LOW).at[safe_ids].get(mode="promise_in_bounds"),
        jnp.zeros((), LOW),
    )
    hidden0 = lax.psum_scatter(picked, "sp", scatter_dimension=0, tiled=True)
    hidden0 = lax.all_to_all(hidden0, "dp", split_axis=0, concat_axis=1, tiled=True).astype(WIDE)

    bias_rows = biases.shape[0] // slab
    norm_rows = norm_params.shape[0]
    shard_triple = proj_in[:, :triple_columns].astype(LOW)
    shard_triple = shard_triple.reshape(slab, span, heads_here, 3, head_dim).transpose(0, 1, 3, 2, 4)
    shard_triple = shard_triple.reshape(slab, triple_columns)
    extras = jnp.concatenate([norm_params.T, biases.reshape(slab, bias_rows)], axis=1).astype(LOW)
    extras = jnp.pad(extras, ((0, 0), (0, LANES - extras.shape[1])))
    wide_in = lax.all_gather(
        jnp.concatenate([shard_triple, proj_in[:, triple_columns:].astype(LOW), extras], axis=1),
        ("dp", "sp"),
        axis=0,
        tiled=True,
    )
    wide_out = lax.all_gather(proj_out.astype(LOW), ("dp", "sp"), axis=0, tiled=True)
    vocab_step = CHUNKS * LANES
    vocab_padded = -(-vocab_local // vocab_step) * vocab_step
    head_table = lax.all_gather(
        jnp.pad(unembed.T.astype(LOW), ((0, vocab_padded - vocab_local), (0, 0))),
        "dp",
        axis=1,
        tiled=True,
    )
    norm_vals = wide_in[:, in_columns : in_columns + norm_rows].astype(WIDE).T
    bias_vals = wide_in[:, in_columns + norm_rows : in_columns + norm_rows + bias_rows]
    bias_vals = bias_vals.astype(WIDE).reshape(-1)
    triple_bias = bias_vals[:triple_columns].reshape(span, heads_here, 3, head_dim)
    triple_bias = triple_bias.transpose(0, 2, 1, 3).reshape(1, triple_columns)

    normal0, inverse0 = standardize(hidden0)
    normed_one = (normal0 * norm_vals[0] + norm_vals[1]).astype(LOW)
    normed_two = (normal0 * norm_vals[2] + norm_vals[3]).astype(LOW)
    positions = sp_index * stretch + jnp.arange(stretch)
    tables = turn_tables(positions, turn_packs(span, wide), 3, wide, head_dim)
    packed = project_queries(normed_one, wide_in, triple_bias, tables, span, seq_here, wide)
    triple = lax.all_to_all(packed, "sp", split_axis=0, concat_axis=0, tiled=True)
    attended_heads, log_totals = attend_forward(triple, heads_here, ATTEND_ROWS, scale)
    attended = lax.all_to_all(attended_heads, "sp", split_axis=0, concat_axis=0, tiled=True)
    attended = attended.reshape(span, tokens_here, wide).transpose(1, 0, 2).reshape(tokens_here, width)
    up_values = (
        jnp.dot(
            normed_two, wide_in[:, triple_columns:in_columns], preferred_element_type=WIDE
        )
        + bias_vals[triple_columns:in_columns]
    )
    act_f, pull_gelu = jax.vjp(gelu_exact, up_values)
    joined = jnp.concatenate([attended, act_f.astype(LOW)], axis=-1)
    hidden1 = (
        hidden0 + jnp.dot(joined, wide_out, preferred_element_type=WIDE) + bias_vals[in_columns:]
    )
    normal1, inverse1 = standardize(hidden1)
    final = (normal1 * norm_vals[4] + norm_vals[5]).astype(LOW)
    rows_all = lax.all_gather(final.reshape(seq_here, stretch, width), "sp", axis=1, tiled=True)
    rows_all = rows_all.reshape(-1, width)
    grand = rows_all.shape[0]
    labels = targets.reshape(-1, 1) - offset
    powers, stats, lines = head_forward(rows_all, head_table, labels, vocab_local)
    merged = lax.all_gather(lines[0:3], "sp")
    highest = jnp.max(merged[:, 0], axis=0)
    summed = jnp.sum(merged[:, 1] * jnp.exp(merged[:, 0] - highest), axis=0)
    log_sum = highest + jnp.log(summed)
    token_loss = (log_sum - jnp.sum(merged[:, 2], axis=0)).reshape(seq_here, length)
    weight_all = 1.0 + (REPLAY_WEIGHT - 1.0) * stream_ids.astype(WIDE)
    total_weight = jnp.sum(weight_all)
    seq_weight = lax.dynamic_slice_in_dim(weight_all, dp_index * seq_here, seq_here, 0)
    loss_local = jnp.sum(seq_weight * jnp.mean(token_loss, axis=1))
    token_scale = jnp.broadcast_to(
        (seq_weight / (total_weight * length))[:, None], (seq_here, length)
    ).reshape(-1)
    guide = jnp.concatenate(
        [log_sum[None], token_scale[None], jnp.zeros((6, grand), WIDE)], axis=0
    )
    slopes, grad_rows = head_backward(stats, guide, labels, powers, head_table)
    final_grad = lax.psum_scatter(
        grad_rows.reshape(seq_here, length, width), "sp", scatter_dimension=1, tiled=True
    ).astype(WIDE)
    final_grad = final_grad.reshape(tokens_here, width)
    unembed_grad = lax.dot_general(
        slopes, rows_all, (((0,), (0,)), ((), ())), preferred_element_type=WIDE
    ).astype(LOW)
    final_grad, unembed_grad = lax.optimization_barrier((final_grad, unembed_grad))
    r_unembed = lax.psum_scatter(unembed_grad, "dp", scatter_dimension=1, tiled=True)

    g_gain_final = jnp.sum(final_grad * normal1, axis=0)
    g_shift_final = jnp.sum(final_grad, axis=0)
    d_hidden1 = standardize_pull(final_grad * norm_vals[4], normal1, inverse1)
    d_branch = d_hidden1.astype(LOW)
    g_out = lax.dot_general(
        joined, d_branch, (((0,), (0,)), ((), ())), preferred_element_type=WIDE
    ).astype(LOW)
    g_bias_out = jnp.sum(d_branch.astype(WIDE), axis=0)
    contract_last = (((1,), (1,)), ((), ()))
    d_attended = lax.dot_general(
        d_branch, wide_out[:width], contract_last, preferred_element_type=WIDE
    ).astype(LOW)
    d_attended = d_attended.reshape(seq_here, stretch, span, wide).transpose(2, 0, 1, 3)
    d_heads = lax.all_to_all(d_attended, "sp", split_axis=0, concat_axis=0, tiled=True)
    d_act = lax.dot_general(d_branch, wide_out[width:], contract_last, preferred_element_type=WIDE)
    d_up = pull_gelu(d_act)[0].astype(LOW)
    g_up = lax.dot_general(
        normed_two, d_up, (((0,), (0,)), ((), ())), preferred_element_type=WIDE
    ).astype(LOW)
    d_normed_two = lax.dot_general(
        d_up, wide_in[:, triple_columns:in_columns], contract_last, preferred_element_type=WIDE
    )
    d_heads, g_out, g_up, d_normed_two = lax.optimization_barrier(
        (d_heads, g_out, g_up, d_normed_two)
    )
    r_out = scattered(g_out)
    r_up = scattered(g_up)
    d_triple = attend_backward(
        triple, attended_heads, d_heads, log_totals, heads_here, ATTEND_ROWS, scale
    )
    d_triple = lax.all_to_all(d_triple, "sp", split_axis=0, concat_axis=0, tiled=True)
    d_joint = unturn(d_triple, tables)
    g_triple = lax.dot_general(
        normed_one, d_joint, (((0,), (0,)), ((), ())), preferred_element_type=WIDE
    ).astype(LOW)
    d_normed_one = lax.dot_general(
        d_joint, wide_in[:, :triple_columns], contract_last, preferred_element_type=WIDE
    )
    g_gain_one = jnp.sum(d_normed_one * normal0, axis=0)
    g_shift_one = jnp.sum(d_normed_one, axis=0)
    g_gain_two = jnp.sum(d_normed_two * normal0, axis=0)
    g_shift_two = jnp.sum(d_normed_two, axis=0)
    d_sum = d_normed_one * norm_vals[0] + d_normed_two * norm_vals[2]
    d_hidden0 = (d_hidden1 + standardize_pull(d_sum, normal0, inverse0)).astype(LOW)
    d_hidden0, r_unembed, r_out, r_up = lax.optimization_barrier(
        (d_hidden0, r_unembed, r_out, r_up)
    )
    grad_all = lax.all_to_all(d_hidden0, "dp", split_axis=1, concat_axis=0, tiled=True)
    grad_all = lax.all_gather(grad_all, "sp", axis=0, tiled=True)
    target_ids = jnp.where(in_slice, local_ids, vocab_local)
    r_embed = (
        jnp.zeros(embed_table.shape, WIDE).at[target_ids].add(grad_all.astype(WIDE), mode="drop")
    )

    g_bias_triple = jnp.sum(d_joint.astype(WIDE), axis=0).reshape(span, 3, heads_here, head_dim)
    g_bias = jnp.concatenate(
        [
            g_bias_triple.transpose(0, 2, 1, 3).reshape(-1),
            jnp.sum(d_up.astype(WIDE), axis=0),
            g_bias_out,
        ]
    )
    g_norm = jnp.stack(
        [g_gain_one, g_shift_one, g_gain_two, g_shift_two, g_gain_final, g_shift_final], axis=1
    )
    g_extra = jnp.concatenate([g_norm, g_bias.reshape(width, bias_rows)], axis=1).astype(LOW)
    g_extra = jnp.pad(g_extra, ((0, 0), (0, LANES - g_extra.shape[1])))
    r_triple = scattered(jnp.concatenate([g_triple, g_extra], axis=1))
    r_norm = r_triple[:, triple_columns : triple_columns + norm_rows].T
    r_bias = r_triple[
        :, triple_columns + norm_rows : triple_columns + norm_rows + bias_rows
    ].reshape(-1)
    r_triple = r_triple[:, :triple_columns].reshape(slab, span, 3, heads_here, head_dim)
    r_triple = r_triple.transpose(0, 1, 3, 2, 4).reshape(slab, triple_columns)
    r_in = jnp.concatenate([r_triple, r_up], axis=1)
    r_unembed = r_unembed[:vocab_local].astype(WIDE).T

    reduced = (r_embed, r_unembed, r_in, r_out, r_norm, r_bias)
    squares = jnp.float32(0.0)
    for grad_piece in reduced:
        squares = squares + jnp.sum(grad_piece * grad_piece)
    loss_term = jnp.where(sp_index == 0, loss_local, 0.0)
    totals = summed_over(jnp.stack([squares, loss_term]), ("sp", "dp"))
    squares_total, loss_total = totals[0], totals[1]
    grad_norm = jnp.sqrt(squares_total)
    mean_loss = loss_total / total_weight
    clip_factor = jnp.minimum(1.0, CLIP_LEVEL / (grad_norm + 1e-06))
    masters = (embed_table, unembed, proj_in, proj_out, norm_params, biases)
    firsts = (embed_first, unembed_first, proj_in_first, proj_out_first, norm_first, bias_first)
    seconds = (
        embed_second,
        unembed_second,
        proj_in_second,
        proj_out_second,
        norm_second,
        bias_second,
    )
    rates = (1.0, 0.05, 0.05, 0.1, 0.5, 0.5)
    decays = (WEIGHT_DECAY, WEIGHT_DECAY, WEIGHT_DECAY, WEIGHT_DECAY, 0.0, 0.0)
    results = []
    for index in range(6):
        results.extend(
            adam_update(
                masters[index],
                firsts[index],
                seconds[index],
                reduced[index],
                clip_factor,
                rates[index],
                decays[index],
            )
        )
    return (
        mean_loss,
        grad_norm,
        results[0],
        results[1],
        results[2],
        results[3],
        results[4],
        results[5],
        results[6],
        results[7],
        results[8],
        results[9],
        results[10],
        results[11],
        results[12],
        results[13],
        results[14],
        results[15],
        results[16],
        results[17],
    )


def solution(mesh):
    in_specs = (
        P("dp", None),
        P("dp", None),
        P(),
        P("sp", "dp"),
        P("sp", "dp"),
        P("sp", "dp"),
        P("dp", "sp"),
        P("dp", "sp"),
        P("dp", "sp"),
        P(("dp", "sp"), None),
        P(("dp", "sp"), None),
        P(("dp", "sp"), None),
        P(("dp", "sp"), None),
        P(("dp", "sp"), None),
        P(("dp", "sp"), None),
        P(None, ("dp", "sp")),
        P(None, ("dp", "sp")),
        P(None, ("dp", "sp")),
        P(("dp", "sp")),
        P(("dp", "sp")),
        P(("dp", "sp")),
    )
    out_specs = (
        P(),
        P(),
        P("sp", "dp"),
        P("sp", "dp"),
        P("sp", "dp"),
        P("dp", "sp"),
        P("dp", "sp"),
        P("dp", "sp"),
        P(("dp", "sp"), None),
        P(("dp", "sp"), None),
        P(("dp", "sp"), None),
        P(("dp", "sp"), None),
        P(("dp", "sp"), None),
        P(("dp", "sp"), None),
        P(None, ("dp", "sp")),
        P(None, ("dp", "sp")),
        P(None, ("dp", "sp")),
        P(("dp", "sp")),
        P(("dp", "sp")),
        P(("dp", "sp")),
    )
    return jax.shard_map(local, mesh=mesh, in_specs=in_specs, out_specs=out_specs, check_vma=False)
```

```python
from functools import partial

import jax
import jax.numpy as jnp
from jax import lax
from jax.experimental import pallas as pl
from jax.experimental.pallas import tpu as pltpu
from jax.sharding import PartitionSpec as P

HEADS = 16
ROT = 16
STEP_COUNT = 10


NORM_EPS = 1e-05
BETA_ONE = 0.9
BETA_TWO = 0.95
ADAM_EPS = 1e-08
WEIGHT_DECAY = 0.01
CLIP_LEVEL = 0.01
REPLAY_WEIGHT = 4.0
NEGATIVE_FILL = -1e30
LOW = jnp.bfloat16
WIDE = jnp.float32
CHUNKS = 5
LANES = 128
HEAD_ROWS = 512
ATTEND_ROWS = 1024
VMEM_LIMIT = 60 * 1024 * 1024


def lane_of(shape):
    return lax.broadcasted_iota(jnp.int32, shape, 1)


def fetch_table(parts, table_ref, arrivals):
    @pl.when(pl.program_id(0) == 0)
    def _():
        share = table_ref.shape[1] // len(parts)
        copies = [
            pltpu.make_async_copy(
                parts[k], table_ref.at[:, k * share : (k + 1) * share], arrivals.at[k]
            )
            for k in range(len(parts))
        ]
        for copy in copies:
            copy.start()
        for copy in copies:
            copy.wait()


def head_forward_kernel(teams, real, rows_ref, label_ref, *refs):
    powers_ref, stats_ref, lines_ref, table_ref, arrivals = refs[teams:]
    fetch_table(refs[:teams], table_ref, arrivals)
    padded = table_ref.shape[0]
    part = padded // CHUNKS
    rows = rows_ref[...]
    count = rows.shape[0]
    label = label_ref[...]
    lane = lane_of((count, LANES))
    stats = jnp.zeros((count, LANES), WIDE)
    tops, sums = [], []
    chosen = jnp.zeros((count, 1), WIDE)
    for c in range(CHUNKS):
        logits = lax.dot_general(
            rows,
            table_ref[c * part : (c + 1) * part, :],
            (((1,), (1,)), ((), ())),
            preferred_element_type=WIDE,
        )
        column = lane_of(logits.shape) + c * part
        chosen = chosen + jnp.sum(jnp.where(column == label, logits, 0.0), axis=1, keepdims=True)
        if (c + 1) * part > real:
            logits = jnp.where(column < real, logits, NEGATIVE_FILL)
        top = jnp.max(logits, axis=1, keepdims=True)
        powers = jnp.exp(logits - top)
        sums.append(jnp.sum(powers, axis=1, keepdims=True))
        tops.append(top)
        powers_ref[:, c * part : (c + 1) * part] = powers.astype(LOW)
        stats = jnp.where(lane == 8 + c, top, stats)
    highest = tops[0]
    for c in range(1, CHUNKS):
        highest = jnp.maximum(highest, tops[c])
    total = jnp.zeros((count, 1), WIDE)
    for c in range(CHUNKS):
        total = total + sums[c] * jnp.exp(tops[c] - highest)
    stats = jnp.where(lane == 0, highest, stats)
    stats = jnp.where(lane == 1, total, stats)
    stats = jnp.where(lane == 2, chosen, stats)
    stats_ref[...] = stats
    lines_ref[...] = jnp.transpose(stats)[0:8, :]


def head_forward(rows, tables, label, real):
    total, width = rows.shape
    padded = tables[0].shape[0]
    teams = len(tables)
    count = min(HEAD_ROWS, total)
    return pl.pallas_call(
        partial(head_forward_kernel, teams, real),
        grid=(total // count,),
        in_specs=[
            pl.BlockSpec((count, width), lambda i: (i, 0)),
            pl.BlockSpec((count, 1), lambda i: (i, 0)),
        ]
        + [pl.BlockSpec(memory_space=pl.ANY)] * teams,
        out_specs=[
            pl.BlockSpec((count, padded), lambda i: (i, 0)),
            pl.BlockSpec((count, LANES), lambda i: (i, 0)),
            pl.BlockSpec((8, count), lambda i: (0, i)),
        ],
        out_shape=[
            jax.ShapeDtypeStruct((total, padded), LOW),
            jax.ShapeDtypeStruct((total, LANES), WIDE),
            jax.ShapeDtypeStruct((8, total), WIDE),
        ],
        scratch_shapes=[pltpu.VMEM((padded, width), LOW), pltpu.SemaphoreType.DMA((teams,))],
        cost_estimate=pl.CostEstimate(
            flops=2 * total * width * padded,
            bytes_accessed=2 * (total * (width + padded) + width * padded),
            transcendentals=total * padded,
        ),
        compiler_params=pltpu.CompilerParams(vmem_limit_bytes=VMEM_LIMIT),
        name="head_forward",
    )(rows, label, *tables)


def head_backward_kernel(teams, stats_ref, lines_ref, label_ref, powers_ref, *refs):
    slope_ref, grad_ref, table_ref, arrivals = refs[teams:]
    fetch_table(refs[:teams], table_ref, arrivals)
    padded = table_ref.shape[0]
    part = padded // CHUNKS
    stats = stats_ref[...]
    label = label_ref[...]
    lines = lines_ref[...]
    lines = jnp.transpose(jnp.concatenate([lines] * (LANES // 8), axis=0))
    lse = lines[:, 0:1]
    scale = lines[:, 1:2]
    total = None
    for c in range(CHUNKS):
        ratio = scale * jnp.exp(stats[:, 8 + c : 9 + c] - lse)
        slope = powers_ref[:, c * part : (c + 1) * part].astype(WIDE) * ratio
        column = lane_of(slope.shape) + c * part
        slope = jnp.where(column == label, slope - scale, slope).astype(LOW)
        slope_ref[:, c * part : (c + 1) * part] = slope
        piece = jnp.dot(
            slope, table_ref[c * part : (c + 1) * part, :], preferred_element_type=WIDE
        )
        total = piece if total is None else total + piece
    grad_ref[...] = total.astype(LOW)


def head_backward(stats, lines, label, powers, tables):
    total, padded = powers.shape
    teams = len(tables)
    width = teams * tables[0].shape[1]
    count = min(HEAD_ROWS, total)
    return pl.pallas_call(
        partial(head_backward_kernel, teams),
        grid=(total // count,),
        in_specs=[
            pl.BlockSpec((count, LANES), lambda i: (i, 0)),
            pl.BlockSpec((8, count), lambda i: (0, i)),
            pl.BlockSpec((count, 1), lambda i: (i, 0)),
            pl.BlockSpec((count, padded), lambda i: (i, 0)),
        ]
        + [pl.BlockSpec(memory_space=pl.ANY)] * teams,
        out_specs=[
            pl.BlockSpec((count, padded), lambda i: (i, 0)),
            pl.BlockSpec((count, width), lambda i: (i, 0)),
        ],
        out_shape=[
            jax.ShapeDtypeStruct((total, padded), LOW),
            jax.ShapeDtypeStruct((total, width), LOW),
        ],
        scratch_shapes=[pltpu.VMEM((padded, width), LOW), pltpu.SemaphoreType.DMA((teams,))],
        cost_estimate=pl.CostEstimate(
            flops=2 * total * width * padded,
            bytes_accessed=2 * (total * (width + 2 * padded) + width * padded),
            transcendentals=0,
        ),
        compiler_params=pltpu.CompilerParams(vmem_limit_bytes=VMEM_LIMIT),
        name="head_backward",
    )(stats, lines, label, powers, *tables)


def attend_forward_kernel(heads, scale, query_ref, key_ref, value_ref, out_ref, lse_ref):
    pieces, stretch, wide = query_ref.shape
    block = pieces * stretch
    head = wide // heads
    index = pl.program_id(1)
    query = query_ref[...].reshape(block, wide) * jnp.asarray(scale, LOW)
    lane = lane_of((block, wide))
    mine = [(lane >= h * head) & (lane < (h + 1) * head) for h in range(heads)]
    own = [jnp.where(mine[h], query, jnp.zeros_like(query)) for h in range(heads)]

    def step(c, state, masked):
        spots = pl.ds(c * pieces, pieces)
        keys = key_ref[spots].reshape(block, wide)
        values = value_ref[spots].reshape(block, wide)
        fresh = []
        for h in range(heads):
            top, total, summed = state[h]
            scores = lax.dot_general(
                own[h], keys, (((1,), (1,)), ((), ())), preferred_element_type=WIDE
            )
            if masked:
                here = lax.broadcasted_iota(jnp.int32, scores.shape, 0)
                scores = jnp.where(here >= lane_of(scores.shape), scores, NEGATIVE_FILL)
            higher = jnp.maximum(top, jnp.max(scores, axis=1, keepdims=True))
            powers = jnp.exp(scores - higher)
            shrink = jnp.exp(top - higher)
            total = total * shrink + jnp.sum(powers, axis=1, keepdims=True)
            summed = summed * shrink + jnp.dot(
                powers.astype(LOW), values, preferred_element_type=WIDE
            )
            fresh.append((higher, total, summed))
        return tuple(fresh)

    state = tuple(
        (
            jnp.full((block, 1), NEGATIVE_FILL, WIDE),
            jnp.zeros((block, 1), WIDE),
            jnp.zeros((block, wide), WIDE),
        )
        for _ in range(heads)
    )
    state = lax.fori_loop(0, index, lambda c, s: step(c, s, False), state)
    state = step(index, state, True)
    result = None
    spot = lane_of((block, LANES))
    logs = jnp.zeros((block, LANES), WIDE)
    for h in range(heads):
        top, total, summed = state[h]
        piece = summed / total
        result = piece if result is None else jnp.where(mine[h], piece, result)
        logs = jnp.where(spot == h, top + jnp.log(total), logs)
    out_ref[...] = result.astype(LOW).reshape(pieces, stretch, wide)
    lse_ref[...] = jnp.transpose(logs)[0:8, :]


def attend_specs(triple, block):
    span, _, seqs, stretch, wide = triple.shape
    pieces = min(block, span * stretch) // stretch
    part = pl.BlockSpec((pieces, None, stretch, wide), lambda s, i: (i, s, 0, 0))
    query = pl.BlockSpec((pieces, None, None, stretch, wide), lambda s, i: (i, 0, s, 0, 0))
    keys = pl.BlockSpec((span, None, None, stretch, wide), lambda s, i: (0, 1, s, 0, 0))
    values = pl.BlockSpec((span, None, None, stretch, wide), lambda s, i: (0, 2, s, 0, 0))
    logs = pl.BlockSpec((None, 8, pieces * stretch), lambda s, i: (s, 0, i))
    return (seqs, span // pieces), part, query, keys, values, logs


def attend_forward(triple, heads, block, scale):
    span, _, seqs, stretch, wide = triple.shape
    length = span * stretch
    grid, part, query, keys, values, logs = attend_specs(triple, block)
    pairs = seqs * heads * length * length // 2
    return pl.pallas_call(
        partial(attend_forward_kernel, heads, scale),
        grid=grid,
        in_specs=[query, keys, values],
        out_specs=[part, logs],
        out_shape=[
            jax.ShapeDtypeStruct((span, seqs, stretch, wide), LOW),
            jax.ShapeDtypeStruct((seqs, 8, length), WIDE),
        ],
        cost_estimate=pl.CostEstimate(
            flops=pairs, bytes_accessed=seqs * length * wide, transcendentals=0
        ),
        compiler_params=pltpu.CompilerParams(vmem_limit_bytes=VMEM_LIMIT),
        name="attend_forward",
    )(triple, triple, triple)


def attend_backward_kernel(
    heads, scale, query_ref, key_ref, value_ref, out_ref, grad_ref, lse_ref, triple_ref, dk_sum, dv_sum
):
    pieces, stretch, wide = query_ref.shape
    block = pieces * stretch
    span = key_ref.shape[0]
    head = wide // heads
    index = pl.program_id(1)

    @pl.when(index == 0)
    def _():
        dk_sum[...] = jnp.zeros_like(dk_sum)
        dv_sum[...] = jnp.zeros_like(dv_sum)

    query = query_ref[...].reshape(block, wide) * jnp.asarray(scale, LOW)
    grad = grad_ref[...].reshape(block, wide)
    lane = lane_of((block, wide))
    mine = [(lane >= h * head) & (lane < (h + 1) * head) for h in range(heads)]
    zero = jnp.zeros_like(query)
    own_query = [jnp.where(mine[h], query, zero) for h in range(heads)]
    own_grad = [jnp.where(mine[h], grad, zero) for h in range(heads)]
    product = out_ref[...].reshape(block, wide).astype(WIDE) * grad.astype(WIDE)
    spot = lane_of((block, LANES))
    centres = jnp.zeros((block, LANES), WIDE)
    for h in range(heads):
        centre = jnp.sum(jnp.where(mine[h], product, 0.0), axis=1, keepdims=True)
        centres = jnp.where(spot == h, centre, centres)
    centres = jnp.transpose(centres)
    logs = lse_ref[...]

    def step(c, state, masked):
        spots = pl.ds(c * pieces, pieces)
        rows = pl.ds(pl.multiple_of(c * block, block), block)
        keys = key_ref[spots].reshape(block, wide)
        values = value_ref[spots].reshape(block, wide)
        fresh = []
        key_part, value_part = None, None
        for h in range(heads):
            scores = lax.dot_general(
                keys, own_query[h], (((1,), (1,)), ((), ())), preferred_element_type=WIDE
            )
            probs = jnp.exp(scores - logs[h : h + 1, :])
            if masked:
                here = lax.broadcasted_iota(jnp.int32, scores.shape, 0)
                probs = jnp.where(here <= lane_of(scores.shape), probs, 0.0)
            grad_probs = lax.dot_general(
                values, own_grad[h], (((1,), (1,)), ((), ())), preferred_element_type=WIDE
            )
            slope = (probs * (grad_probs - centres[h : h + 1, :])).astype(LOW)
            a = jnp.dot(slope, own_query[h], preferred_element_type=WIDE)
            b = jnp.dot(probs.astype(LOW), own_grad[h], preferred_element_type=WIDE)
            key_part = a if key_part is None else key_part + a
            value_part = b if value_part is None else value_part + b
            fresh.append(
                state[h]
                + lax.dot_general(slope, keys, (((0,), (0,)), ((), ())), preferred_element_type=WIDE)
            )
        dk_sum[rows, :] += key_part
        dv_sum[rows, :] += value_part
        return tuple(fresh)

    state = tuple(jnp.zeros((block, wide), WIDE) for _ in range(heads))
    state = lax.fori_loop(0, index, lambda c, s: step(c, s, False), state)
    state = step(index, state, True)
    result = state[0]
    for h in range(1, heads):
        result = jnp.where(mine[h], state[h], result)
    triple_ref[pl.ds(index * pieces, pieces), 0] = (
        (result * scale).astype(LOW).reshape(pieces, stretch, wide)
    )

    @pl.when(index == pl.num_programs(1) - 1)
    def _():
        triple_ref[:, 1] = dk_sum[...].astype(LOW).reshape(span, stretch, wide)
        triple_ref[:, 2] = dv_sum[...].astype(LOW).reshape(span, stretch, wide)


def attend_backward(triple, attended, grad, lse, heads, block, scale):
    span, _, seqs, stretch, wide = triple.shape
    length = span * stretch
    grid, part, query, keys, values, logs = attend_specs(triple, block)
    pairs = seqs * heads * length * length // 2
    return pl.pallas_call(
        partial(attend_backward_kernel, heads, scale),
        grid=grid,
        in_specs=[query, keys, values, part, part, logs],
        out_specs=pl.BlockSpec((span, 3, None, stretch, wide), lambda s, i: (0, 0, s, 0, 0)),
        out_shape=jax.ShapeDtypeStruct((span, 3, seqs, stretch, wide), LOW),
        scratch_shapes=[pltpu.VMEM((length, wide), WIDE), pltpu.VMEM((length, wide), WIDE)],
        cost_estimate=pl.CostEstimate(
            flops=pairs, bytes_accessed=seqs * length * wide, transcendentals=0
        ),
        compiler_params=pltpu.CompilerParams(vmem_limit_bytes=VMEM_LIMIT),
        name="attend_backward",
    )(triple, triple, triple, attended, grad, lse)


def turn_tables(positions, repeats, parts, wide, head):
    halfway = ROT // 2
    place = jnp.arange(parts * wide)
    entry = place % head
    turned = (place // wide < 2) & (entry < ROT)
    frequency = 10000.0 ** (-2.0 * (entry % halfway).astype(WIDE) / ROT)
    angles = positions.astype(WIDE)[:, None] * frequency[None, :]
    sine = jnp.where(turned, jnp.sin(angles), 0.0)
    cosine = jnp.where(turned, jnp.cos(angles), 1.0)
    later = jnp.where(entry < halfway, -sine, 0.0)
    earlier = jnp.where(entry < halfway, 0.0, sine)
    return tuple(jnp.tile(table, (1, repeats)) for table in (cosine, later, earlier))


def turn_packs(span, wide):
    return 1 if (3 * wide) % LANES == 0 else 2


def queries_kernel(seqs, wide, rows_ref, table_ref, bias_ref, cosine_ref, later_ref, earlier_ref, out_ref):
    halfway = ROT // 2
    columns = table_ref.shape[1]
    values = jnp.dot(rows_ref[...], table_ref[...], preferred_element_type=WIDE) + bias_ref[...]
    stretch = cosine_ref.shape[0]
    for s in range(seqs):
        part = values[s * stretch : (s + 1) * stretch]
        part = (
            part * cosine_ref[...]
            + pltpu.roll(part, columns - halfway, 1) * later_ref[...]
            + pltpu.roll(part, halfway, 1) * earlier_ref[...]
        ).astype(LOW)
        for j in range(columns // wide):
            out_ref[j // 3, j % 3, s] = part[:, j * wide : (j + 1) * wide]


def project_queries(rows, table, bias, tables, span, seqs, wide):
    total, width = rows.shape
    stretch = total // seqs
    packs = turn_packs(span, wide)
    columns = packs * 3 * wide
    fixed = pl.BlockSpec((stretch, columns), lambda g: (0, 0))
    return pl.pallas_call(
        partial(queries_kernel, seqs, wide),
        grid=(span // packs,),
        in_specs=[
            pl.BlockSpec((total, width), lambda g: (0, 0)),
            pl.BlockSpec((width, columns), lambda g: (0, g)),
            pl.BlockSpec((1, columns), lambda g: (0, g)),
            fixed,
            fixed,
            fixed,
        ],
        out_specs=pl.BlockSpec((packs, 3, seqs, stretch, wide), lambda g: (g, 0, 0, 0, 0)),
        out_shape=jax.ShapeDtypeStruct((span, 3, seqs, stretch, wide), LOW),
        cost_estimate=pl.CostEstimate(
            flops=2 * total * width * span * 3 * wide,
            bytes_accessed=2 * width * span * 3 * wide,
            transcendentals=0,
        ),
        compiler_params=pltpu.CompilerParams(vmem_limit_bytes=VMEM_LIMIT),
        name="project_queries",
    )(rows, table, bias, *tables)


def unturn_kernel(seqs, wide, triple_ref, cosine_ref, later_ref, earlier_ref, out_ref):
    halfway = ROT // 2
    columns = out_ref.shape[1]
    stretch = cosine_ref.shape[0]
    for s in range(seqs):
        part = jnp.concatenate(
            [triple_ref[j // 3, j % 3, s].astype(WIDE) for j in range(columns // wide)], axis=1
        )
        part = (
            part * cosine_ref[...]
            - pltpu.roll(part, columns - halfway, 1) * later_ref[...]
            - pltpu.roll(part, halfway, 1) * earlier_ref[...]
        )
        out_ref[s * stretch : (s + 1) * stretch, :] = part.astype(LOW)


def unturn(triple, tables):
    span, _, seqs, stretch, wide = triple.shape
    packs = turn_packs(span, wide)
    columns = packs * 3 * wide
    fixed = pl.BlockSpec((stretch, columns), lambda g: (0, 0))
    return pl.pallas_call(
        partial(unturn_kernel, seqs, wide),
        grid=(span // packs,),
        in_specs=[
            pl.BlockSpec((packs, 3, seqs, stretch, wide), lambda g: (g, 0, 0, 0, 0)),
            fixed,
            fixed,
            fixed,
        ],
        out_specs=pl.BlockSpec((seqs * stretch, columns), lambda g: (0, g)),
        out_shape=jax.ShapeDtypeStruct((seqs * stretch, span * 3 * wide), LOW),
        compiler_params=pltpu.CompilerParams(vmem_limit_bytes=VMEM_LIMIT),
        name="unturn",
    )(triple, *tables)


def gelu_exact(values):
    return jax.nn.gelu(values, approximate=False)


def standardize(values):
    average = jnp.mean(values, axis=-1, keepdims=True)
    centered = values - average
    variance = jnp.mean(centered * centered, axis=-1, keepdims=True)
    inverse = lax.rsqrt(variance + NORM_EPS)
    return centered * inverse, inverse


def standardize_pull(scaled, normal, inverse):
    return inverse * (
        scaled
        - jnp.mean(scaled, axis=-1, keepdims=True)
        - normal * jnp.mean(scaled * normal, axis=-1, keepdims=True)
    )


def adam_update(weight, first, second, grad, clip_factor, rate, decay):
    grad = grad * clip_factor
    first_new = BETA_ONE * first + (1.0 - BETA_ONE) * grad
    second_new = BETA_TWO * second + (1.0 - BETA_TWO) * grad * grad
    fix_one = 1.0 - BETA_ONE**STEP_COUNT
    fix_two = 1.0 - BETA_TWO**STEP_COUNT
    direction = first_new / fix_one / (jnp.sqrt(second_new / fix_two) + ADAM_EPS)
    return (weight - rate * (direction + decay * weight), first_new, second_new)


def summed_over(vector, axes):
    for axis in axes:
        vector = jnp.sum(lax.all_gather(vector, axis), axis=0)
    return vector


def scattered(gradient):
    dp, sp = lax.axis_size("dp"), lax.axis_size("sp")
    rows, columns = gradient.shape
    gradient = gradient.reshape(dp, sp, rows // (dp * sp), columns).transpose(1, 0, 2, 3)
    gradient = gradient.reshape(rows, columns)
    return lax.psum_scatter(gradient, "sp", scatter_dimension=0, tiled=True)


def joined_teams(gradient):
    dp = lax.axis_size("dp")
    rows, columns = gradient.shape
    gradient = lax.all_to_all(gradient, "dp", split_axis=0, concat_axis=0, tiled=True)
    return jnp.sum(gradient.reshape(dp, rows // dp, columns).astype(WIDE), axis=0)


def moved(array, axis, step):
    size = lax.axis_size(axis)
    return lax.ppermute(array, axis, [(i, (i + step) % size) for i in range(size)])


def turned(values, teams, team):
    share = values.shape[1] // teams
    blocks = [values[:, b * share : (b + 1) * share] for b in range(teams)]
    order = [blocks[(teams - 1 - m) % teams] for m in range(2 * teams - 1)]
    row = jnp.concatenate(order, axis=1)
    return lax.dynamic_slice_in_dim(row, (teams - 1 - team) * share, teams * share, 1)


def local(
    token_ids,
    targets,
    stream_ids,
    embed_table,
    embed_first,
    embed_second,
    unembed,
    unembed_first,
    unembed_second,
    proj_in,
    proj_in_first,
    proj_in_second,
    proj_out,
    proj_out_first,
    proj_out_second,
    norm_params,
    norm_first,
    norm_second,
    biases,
    bias_first,
    bias_second,
):
    span = lax.axis_size("sp")
    teams = lax.axis_size("dp")
    sp_index = lax.axis_index("sp")
    dp_index = lax.axis_index("dp")
    seq_here, length = token_ids.shape
    stretch = length // span
    vocab_local = embed_table.shape[0]
    slab, in_columns = proj_in.shape
    width = proj_out.shape[1]
    triple_columns = 3 * width
    hidden_units = in_columns - triple_columns
    heads_here = HEADS // span
    head_dim = width // HEADS
    wide = heads_here * head_dim
    scale = head_dim ** (-0.5)
    tokens_here = seq_here * stretch
    offset = sp_index * vocab_local

    bias_rows = biases.shape[0] // slab
    norm_rows = norm_params.shape[0]
    shard_triple = proj_in[:, :triple_columns].astype(LOW)
    shard_triple = shard_triple.reshape(slab, span, heads_here, 3, head_dim).transpose(0, 1, 3, 2, 4)
    shard_triple = shard_triple.reshape(slab, triple_columns)
    extras = jnp.concatenate([norm_params.T, biases.reshape(slab, bias_rows)], axis=1).astype(LOW)
    extras = jnp.pad(extras, ((0, 0), (0, LANES - extras.shape[1])))
    shard_triple = jnp.concatenate([shard_triple, extras], axis=1)
    vocab_step = CHUNKS * LANES
    vocab_padded = -(-vocab_local // vocab_step) * vocab_step
    own_table = jnp.pad(unembed.T.astype(LOW), ((0, vocab_padded - vocab_local), (0, 0)))
    token_ids, shard_triple, own_table = lax.optimization_barrier(
        (token_ids, shard_triple, own_table)
    )
    wide_triple = lax.all_gather(shard_triple, ("dp", "sp"), axis=0, tiled=True)
    half = vocab_padded // 2
    middle = teams // 2
    far_first = moved(own_table[:half], "dp", middle)

    ids_all = lax.all_gather(token_ids, "dp")
    ids_all = ids_all.reshape(teams, seq_here, span, stretch).transpose(2, 0, 1, 3).reshape(-1)
    local_ids = ids_all - offset
    in_slice = (local_ids >= 0) & (local_ids < vocab_local)
    safe_ids = jnp.clip(local_ids, 0, vocab_local - 1)
    picked = jnp.where(
        in_slice[:, None],
        embed_table.astype(LOW).at[safe_ids].get(mode="promise_in_bounds"),
        jnp.zeros((), LOW),
    )
    picked, wide_triple, far_first, own_table = lax.optimization_barrier(
        (picked, wide_triple, far_first, own_table)
    )
    tables = {k: moved(own_table, "dp", k) for k in range(1, middle)}
    wide_up = lax.all_gather(proj_in[:, triple_columns:].astype(LOW), ("dp", "sp"), axis=0, tiled=True)
    wide_out = lax.all_gather(proj_out.astype(LOW), ("dp", "sp"), axis=0, tiled=True)
    hidden0 = lax.psum_scatter(picked, "sp", scatter_dimension=0, tiled=True)
    hidden0, tables = lax.optimization_barrier((hidden0, tables))
    hidden0 = lax.all_to_all(hidden0, "dp", split_axis=0, concat_axis=1, tiled=True)
    hidden0, later_table = lax.optimization_barrier((hidden0, own_table))
    hidden0 = hidden0.astype(WIDE)
    for k in range(middle + 1, teams):
        tables[k] = moved(later_table, "dp", k)
    norm_vals = wide_triple[:, triple_columns : triple_columns + norm_rows].astype(WIDE).T
    bias_vals = wide_triple[
        :, triple_columns + norm_rows : triple_columns + norm_rows + bias_rows
    ]
    bias_vals = bias_vals.astype(WIDE).reshape(-1)
    triple_bias = bias_vals[:triple_columns].reshape(span, heads_here, 3, head_dim)
    triple_bias = triple_bias.transpose(0, 2, 1, 3).reshape(1, triple_columns)

    normal0, inverse0 = standardize(hidden0)
    normed_one = (normal0 * norm_vals[0] + norm_vals[1]).astype(LOW)
    normed_two = (normal0 * norm_vals[2] + norm_vals[3]).astype(LOW)
    positions = sp_index * stretch + jnp.arange(stretch)
    angles = turn_tables(positions, turn_packs(span, wide), 3, wide, head_dim)
    packed = project_queries(normed_one, wide_triple, triple_bias, angles, span, seq_here, wide)
    triple = lax.all_to_all(packed, "sp", split_axis=0, concat_axis=0, tiled=True)
    triple, tables, later_table = lax.optimization_barrier((triple, tables, later_table))
    far_last = moved(later_table[half:], "dp", middle)
    attended_heads, log_totals = attend_forward(triple, heads_here, ATTEND_ROWS, scale)
    attended = lax.all_to_all(attended_heads, "sp", split_axis=0, concat_axis=0, tiled=True)
    attended, far_last = lax.optimization_barrier((attended, far_last))
    tables[middle] = jnp.concatenate([far_first, far_last], axis=0)
    tables = [own_table] + [tables[k] for k in range(1, teams)]
    attended = attended.reshape(span, tokens_here, wide).transpose(1, 0, 2).reshape(tokens_here, width)
    up_values = (
        jnp.dot(normed_two, wide_up, preferred_element_type=WIDE)
        + bias_vals[triple_columns:in_columns]
    )
    act_f, pull_gelu = jax.vjp(gelu_exact, up_values)
    joined = jnp.concatenate([attended, act_f.astype(LOW)], axis=-1)
    hidden1 = (
        hidden0 + jnp.dot(joined, wide_out, preferred_element_type=WIDE) + bias_vals[in_columns:]
    )
    normal1, inverse1 = standardize(hidden1)
    final = (normal1 * norm_vals[4] + norm_vals[5]).astype(LOW)
    final = turned(final, teams, dp_index)
    rows_all = lax.all_gather(final.reshape(seq_here, stretch, width), "sp", axis=1, tiled=True)
    rows_all = rows_all.reshape(-1, width)
    grand = rows_all.shape[0]
    labels = targets.reshape(-1, 1) - offset
    powers, stats, lines = head_forward(rows_all, tables, labels, vocab_local)
    merged = lax.all_gather(lines[0:3], "sp")
    highest = jnp.max(merged[:, 0], axis=0)
    summed = jnp.sum(merged[:, 1] * jnp.exp(merged[:, 0] - highest), axis=0)
    log_sum = highest + jnp.log(summed)
    token_loss = (log_sum - jnp.sum(merged[:, 2], axis=0)).reshape(seq_here, length)
    weight_all = 1.0 + (REPLAY_WEIGHT - 1.0) * stream_ids.astype(WIDE)
    total_weight = jnp.sum(weight_all)
    seq_weight = lax.dynamic_slice_in_dim(weight_all, dp_index * seq_here, seq_here, 0)
    loss_local = jnp.sum(seq_weight * jnp.mean(token_loss, axis=1))
    token_scale = jnp.broadcast_to(
        (seq_weight / (total_weight * length))[:, None], (seq_here, length)
    ).reshape(-1)
    guide = jnp.concatenate(
        [log_sum[None], token_scale[None], jnp.zeros((6, grand), WIDE)], axis=0
    )
    slopes, grad_rows = head_backward(stats, guide, labels, powers, tables)
    final_grad = lax.psum_scatter(
        grad_rows.reshape(seq_here, length, width), "sp", scatter_dimension=1, tiled=True
    ).astype(WIDE)
    final_grad = final_grad.reshape(tokens_here, width)
    share = width // teams
    unembed_parts = [
        lax.dot_general(
            slopes,
            rows_all[:, k * share : (k + 1) * share],
            (((0,), (0,)), ((), ())),
            preferred_element_type=WIDE,
        ).astype(LOW)
        for k in range(teams)
    ]
    arrived = [moved(unembed_parts[k], "dp", teams - k) for k in range(1, middle)]
    final_grad, unembed_parts = lax.optimization_barrier((final_grad, unembed_parts))
    final_grad = turned(final_grad, teams, dp_index)

    g_gain_final = jnp.sum(final_grad * normal1, axis=0)
    g_shift_final = jnp.sum(final_grad, axis=0)
    d_hidden1 = standardize_pull(final_grad * norm_vals[4], normal1, inverse1)
    d_branch = d_hidden1.astype(LOW)
    g_out = lax.dot_general(
        joined, d_branch, (((0,), (0,)), ((), ())), preferred_element_type=WIDE
    ).astype(LOW)
    g_bias_out = jnp.sum(d_branch.astype(WIDE), axis=0)
    contract_last = (((1,), (1,)), ((), ()))
    d_attended = lax.dot_general(
        d_branch, wide_out[:width], contract_last, preferred_element_type=WIDE
    ).astype(LOW)
    d_attended = d_attended.reshape(seq_here, stretch, span, wide).transpose(2, 0, 1, 3)
    d_heads = lax.all_to_all(d_attended, "sp", split_axis=0, concat_axis=0, tiled=True)
    d_act = lax.dot_general(d_branch, wide_out[width:], contract_last, preferred_element_type=WIDE)
    d_up = pull_gelu(d_act)[0].astype(LOW)
    g_up = lax.dot_general(
        normed_two, d_up, (((0,), (0,)), ((), ())), preferred_element_type=WIDE
    ).astype(LOW)
    d_normed_two = lax.dot_general(
        d_up, wide_up, contract_last, preferred_element_type=WIDE
    )
    d_heads, g_out, g_up, d_normed_two, arrived, unembed_parts = lax.optimization_barrier(
        (d_heads, g_out, g_up, d_normed_two, arrived, unembed_parts)
    )
    far_first = moved(unembed_parts[middle][:half], "dp", middle)
    r_out = scattered(g_out)
    r_up = scattered(g_up)
    d_triple = attend_backward(
        triple, attended_heads, d_heads, log_totals, heads_here, ATTEND_ROWS, scale
    )
    d_triple = lax.all_to_all(d_triple, "sp", split_axis=0, concat_axis=0, tiled=True)
    d_joint = unturn(d_triple, angles)
    g_triple = lax.dot_general(
        normed_one, d_joint, (((0,), (0,)), ((), ())), preferred_element_type=WIDE
    ).astype(LOW)
    d_normed_one = lax.dot_general(
        d_joint, wide_triple[:, :triple_columns], contract_last, preferred_element_type=WIDE
    )
    d_normed_one, far_first, unembed_parts = lax.optimization_barrier(
        (d_normed_one, far_first, unembed_parts)
    )
    late = [moved(unembed_parts[k], "dp", teams - k) for k in range(middle + 1, teams)]
    g_gain_one = jnp.sum(d_normed_one * normal0, axis=0)
    g_shift_one = jnp.sum(d_normed_one, axis=0)
    g_gain_two = jnp.sum(d_normed_two * normal0, axis=0)
    g_shift_two = jnp.sum(d_normed_two, axis=0)
    d_sum = d_normed_one * norm_vals[0] + d_normed_two * norm_vals[2]
    d_hidden0 = (d_hidden1 + standardize_pull(d_sum, normal0, inverse0)).astype(LOW)
    d_hidden0, r_out, r_up = lax.optimization_barrier((d_hidden0, r_out, r_up))
    grad_all = lax.all_to_all(d_hidden0, "dp", split_axis=1, concat_axis=0, tiled=True)
    grad_all, late, far_part = lax.optimization_barrier((grad_all, late, unembed_parts[middle]))
    far_last = moved(far_part[half:], "dp", middle)
    r_unembed = [unembed_parts[0], *arrived, *late, jnp.concatenate([far_first, far_last], axis=0)]
    grad_all = lax.all_gather(grad_all, "sp", axis=0, tiled=True)
    target_ids = jnp.where(in_slice, local_ids, vocab_local)
    r_embed = (
        jnp.zeros(embed_table.shape, WIDE).at[target_ids].add(grad_all.astype(WIDE), mode="drop")
    )

    g_bias_triple = jnp.sum(d_joint.astype(WIDE), axis=0).reshape(span, 3, heads_here, head_dim)
    g_bias = jnp.concatenate(
        [
            g_bias_triple.transpose(0, 2, 1, 3).reshape(-1),
            jnp.sum(d_up.astype(WIDE), axis=0),
            g_bias_out,
        ]
    )
    g_norm = jnp.stack(
        [g_gain_one, g_shift_one, g_gain_two, g_shift_two, g_gain_final, g_shift_final], axis=1
    )
    g_extra = jnp.concatenate([g_norm, g_bias.reshape(width, bias_rows)], axis=1).astype(LOW)
    g_extra = jnp.pad(g_extra, ((0, 0), (0, LANES - g_extra.shape[1])))
    r_triple = scattered(jnp.concatenate([g_triple, g_extra], axis=1))
    r_triple, r_up, r_out = joined_teams(r_triple), joined_teams(r_up), joined_teams(r_out)
    r_norm = r_triple[:, triple_columns : triple_columns + norm_rows].T
    r_bias = r_triple[
        :, triple_columns + norm_rows : triple_columns + norm_rows + bias_rows
    ].reshape(-1)
    r_triple = r_triple[:, :triple_columns].reshape(slab, span, 3, heads_here, head_dim)
    r_triple = r_triple.transpose(0, 1, 3, 2, 4).reshape(slab, triple_columns)
    r_in = jnp.concatenate([r_triple, r_up], axis=1)
    r_unembed = sum(part[:vocab_local].astype(WIDE) for part in r_unembed).T

    reduced = (r_embed, r_unembed, r_in, r_out, r_norm, r_bias)
    squares = jnp.float32(0.0)
    for grad_piece in reduced:
        squares = squares + jnp.sum(grad_piece * grad_piece)
    loss_term = jnp.where(sp_index == 0, loss_local, 0.0)
    totals = summed_over(jnp.stack([squares, loss_term]), ("sp", "dp"))
    squares_total, loss_total = totals[0], totals[1]
    grad_norm = jnp.sqrt(squares_total)
    mean_loss = loss_total / total_weight
    clip_factor = jnp.minimum(1.0, CLIP_LEVEL / (grad_norm + 1e-06))
    masters = (embed_table, unembed, proj_in, proj_out, norm_params, biases)
    firsts = (embed_first, unembed_first, proj_in_first, proj_out_first, norm_first, bias_first)
    seconds = (
        embed_second,
        unembed_second,
        proj_in_second,
        proj_out_second,
        norm_second,
        bias_second,
    )
    rates = (1.0, 0.05, 0.05, 0.1, 0.5, 0.5)
    decays = (WEIGHT_DECAY, WEIGHT_DECAY, WEIGHT_DECAY, WEIGHT_DECAY, 0.0, 0.0)
    results = []
    for index in range(6):
        results.extend(
            adam_update(
                masters[index],
                firsts[index],
                seconds[index],
                reduced[index],
                clip_factor,
                rates[index],
                decays[index],
            )
        )
    return (
        mean_loss,
        grad_norm,
        results[0],
        results[1],
        results[2],
        results[3],
        results[4],
        results[5],
        results[6],
        results[7],
        results[8],
        results[9],
        results[10],
        results[11],
        results[12],
        results[13],
        results[14],
        results[15],
        results[16],
        results[17],
    )


def solution(mesh):
    in_specs = (
        P("dp", None),
        P("dp", None),
        P(),
        P("sp", "dp"),
        P("sp", "dp"),
        P("sp", "dp"),
        P("dp", "sp"),
        P("dp", "sp"),
        P("dp", "sp"),
        P(("dp", "sp"), None),
        P(("dp", "sp"), None),
        P(("dp", "sp"), None),
        P(("dp", "sp"), None),
        P(("dp", "sp"), None),
        P(("dp", "sp"), None),
        P(None, ("dp", "sp")),
        P(None, ("dp", "sp")),
        P(None, ("dp", "sp")),
        P(("dp", "sp")),
        P(("dp", "sp")),
        P(("dp", "sp")),
    )
    out_specs = (
        P(),
        P(),
        P("sp", "dp"),
        P("sp", "dp"),
        P("sp", "dp"),
        P("dp", "sp"),
        P("dp", "sp"),
        P("dp", "sp"),
        P(("dp", "sp"), None),
        P(("dp", "sp"), None),
        P(("dp", "sp"), None),
        P(("dp", "sp"), None),
        P(("dp", "sp"), None),
        P(("dp", "sp"), None),
        P(None, ("dp", "sp")),
        P(None, ("dp", "sp")),
        P(None, ("dp", "sp")),
        P(("dp", "sp")),
        P(("dp", "sp")),
        P(("dp", "sp")),
    )
    return jax.shard_map(local, mesh=mesh, in_specs=in_specs, out_specs=out_specs, check_vma=False)
```

```python
from functools import partial

import jax
import jax.numpy as jnp
from jax import lax
from jax.experimental import pallas as pl
from jax.experimental.pallas import tpu as pltpu
from jax.sharding import PartitionSpec as P

HEADS = 16
ROT = 16
STEP_COUNT = 10


NORM_EPS = 1e-05
BETA_ONE = 0.9
BETA_TWO = 0.95
ADAM_EPS = 1e-08
WEIGHT_DECAY = 0.01
CLIP_LEVEL = 0.01
REPLAY_WEIGHT = 4.0
NEGATIVE_FILL = -1e30
LOW = jnp.bfloat16
WIDE = jnp.float32
CHUNKS = 5
LANES = 128
HEAD_ROWS = 512
ATTEND_ROWS = 1024
VMEM_LIMIT = 60 * 1024 * 1024


def lane_of(shape):
    return lax.broadcasted_iota(jnp.int32, shape, 1)


def fetch_table(parts, table_ref, arrivals):
    @pl.when(pl.program_id(0) == 0)
    def _():
        share = table_ref.shape[1] // len(parts)
        copies = [
            pltpu.make_async_copy(
                parts[k], table_ref.at[:, k * share : (k + 1) * share], arrivals.at[k]
            )
            for k in range(len(parts))
        ]
        for copy in copies:
            copy.start()
        for copy in copies:
            copy.wait()


def head_forward_kernel(teams, real, rows_ref, label_ref, *refs):
    powers_ref, stats_ref, lines_ref, table_ref, arrivals = refs[teams:]
    fetch_table(refs[:teams], table_ref, arrivals)
    padded = table_ref.shape[0]
    part = padded // CHUNKS
    rows = rows_ref[...]
    count = rows.shape[0]
    label = label_ref[...]
    lane = lane_of((count, LANES))
    stats = jnp.zeros((count, LANES), WIDE)
    tops, sums = [], []
    chosen = jnp.zeros((count, 1), WIDE)
    for c in range(CHUNKS):
        logits = lax.dot_general(
            rows,
            table_ref[c * part : (c + 1) * part, :],
            (((1,), (1,)), ((), ())),
            preferred_element_type=WIDE,
        )
        column = lane_of(logits.shape) + c * part
        chosen = chosen + jnp.sum(jnp.where(column == label, logits, 0.0), axis=1, keepdims=True)
        if (c + 1) * part > real:
            logits = jnp.where(column < real, logits, NEGATIVE_FILL)
        top = jnp.max(logits, axis=1, keepdims=True)
        powers = jnp.exp(logits - top)
        sums.append(jnp.sum(powers, axis=1, keepdims=True))
        tops.append(top)
        powers_ref[:, c * part : (c + 1) * part] = powers.astype(LOW)
        stats = jnp.where(lane == 8 + c, top, stats)
    highest = tops[0]
    for c in range(1, CHUNKS):
        highest = jnp.maximum(highest, tops[c])
    total = jnp.zeros((count, 1), WIDE)
    for c in range(CHUNKS):
        total = total + sums[c] * jnp.exp(tops[c] - highest)
    stats = jnp.where(lane == 0, highest, stats)
    stats = jnp.where(lane == 1, total, stats)
    stats = jnp.where(lane == 2, chosen, stats)
    stats_ref[...] = stats
    lines_ref[...] = jnp.transpose(stats)[0:8, :]


def head_forward(rows, tables, label, real):
    total, width = rows.shape
    padded = tables[0].shape[0]
    teams = len(tables)
    count = min(HEAD_ROWS, total)
    return pl.pallas_call(
        partial(head_forward_kernel, teams, real),
        grid=(total // count,),
        in_specs=[
            pl.BlockSpec((count, width), lambda i: (i, 0)),
            pl.BlockSpec((count, 1), lambda i: (i, 0)),
        ]
        + [pl.BlockSpec(memory_space=pl.ANY)] * teams,
        out_specs=[
            pl.BlockSpec((count, padded), lambda i: (i, 0)),
            pl.BlockSpec((count, LANES), lambda i: (i, 0)),
            pl.BlockSpec((8, count), lambda i: (0, i)),
        ],
        out_shape=[
            jax.ShapeDtypeStruct((total, padded), LOW),
            jax.ShapeDtypeStruct((total, LANES), WIDE),
            jax.ShapeDtypeStruct((8, total), WIDE),
        ],
        scratch_shapes=[pltpu.VMEM((padded, width), LOW), pltpu.SemaphoreType.DMA((teams,))],
        cost_estimate=pl.CostEstimate(
            flops=2 * total * width * padded,
            bytes_accessed=2 * (total * (width + padded) + width * padded),
            transcendentals=total * padded,
        ),
        compiler_params=pltpu.CompilerParams(vmem_limit_bytes=VMEM_LIMIT),
        name="head_forward",
    )(rows, label, *tables)


def head_backward_kernel(teams, stats_ref, lines_ref, label_ref, powers_ref, *refs):
    slope_ref, grad_ref, table_ref, arrivals = refs[teams:]
    fetch_table(refs[:teams], table_ref, arrivals)
    padded = table_ref.shape[0]
    part = padded // CHUNKS
    stats = stats_ref[...]
    label = label_ref[...]
    lines = lines_ref[...]
    lines = jnp.transpose(jnp.concatenate([lines] * (LANES // 8), axis=0))
    lse = lines[:, 0:1]
    scale = lines[:, 1:2]
    total = None
    for c in range(CHUNKS):
        ratio = scale * jnp.exp(stats[:, 8 + c : 9 + c] - lse)
        slope = powers_ref[:, c * part : (c + 1) * part].astype(WIDE) * ratio
        column = lane_of(slope.shape) + c * part
        slope = jnp.where(column == label, slope - scale, slope).astype(LOW)
        slope_ref[:, c * part : (c + 1) * part] = slope
        piece = jnp.dot(
            slope, table_ref[c * part : (c + 1) * part, :], preferred_element_type=WIDE
        )
        total = piece if total is None else total + piece
    grad_ref[...] = total.astype(LOW)


def head_backward(stats, lines, label, powers, tables):
    total, padded = powers.shape
    teams = len(tables)
    width = teams * tables[0].shape[1]
    count = min(HEAD_ROWS, total)
    return pl.pallas_call(
        partial(head_backward_kernel, teams),
        grid=(total // count,),
        in_specs=[
            pl.BlockSpec((count, LANES), lambda i: (i, 0)),
            pl.BlockSpec((8, count), lambda i: (0, i)),
            pl.BlockSpec((count, 1), lambda i: (i, 0)),
            pl.BlockSpec((count, padded), lambda i: (i, 0)),
        ]
        + [pl.BlockSpec(memory_space=pl.ANY)] * teams,
        out_specs=[
            pl.BlockSpec((count, padded), lambda i: (i, 0)),
            pl.BlockSpec((count, width), lambda i: (i, 0)),
        ],
        out_shape=[
            jax.ShapeDtypeStruct((total, padded), LOW),
            jax.ShapeDtypeStruct((total, width), LOW),
        ],
        scratch_shapes=[pltpu.VMEM((padded, width), LOW), pltpu.SemaphoreType.DMA((teams,))],
        cost_estimate=pl.CostEstimate(
            flops=2 * total * width * padded,
            bytes_accessed=2 * (total * (width + 2 * padded) + width * padded),
            transcendentals=0,
        ),
        compiler_params=pltpu.CompilerParams(vmem_limit_bytes=VMEM_LIMIT),
        name="head_backward",
    )(stats, lines, label, powers, *tables)


def attend_forward_kernel(heads, scale, query_ref, key_ref, value_ref, out_ref, lse_ref):
    pieces, stretch, wide = query_ref.shape
    block = pieces * stretch
    head = wide // heads
    index = pl.program_id(1)
    query = query_ref[...].reshape(block, wide) * jnp.asarray(scale, LOW)
    lane = lane_of((block, wide))
    mine = [(lane >= h * head) & (lane < (h + 1) * head) for h in range(heads)]
    own = [jnp.where(mine[h], query, jnp.zeros_like(query)) for h in range(heads)]

    def step(c, state, masked):
        spots = pl.ds(c * pieces, pieces)
        keys = key_ref[spots].reshape(block, wide)
        values = value_ref[spots].reshape(block, wide)
        fresh = []
        for h in range(heads):
            top, total, summed = state[h]
            scores = lax.dot_general(
                own[h], keys, (((1,), (1,)), ((), ())), preferred_element_type=WIDE
            )
            if masked:
                here = lax.broadcasted_iota(jnp.int32, scores.shape, 0)
                scores = jnp.where(here >= lane_of(scores.shape), scores, NEGATIVE_FILL)
            higher = jnp.maximum(top, jnp.max(scores, axis=1, keepdims=True))
            powers = jnp.exp(scores - higher)
            shrink = jnp.exp(top - higher)
            total = total * shrink + jnp.sum(powers, axis=1, keepdims=True)
            summed = summed * shrink + jnp.dot(
                powers.astype(LOW), values, preferred_element_type=WIDE
            )
            fresh.append((higher, total, summed))
        return tuple(fresh)

    state = tuple(
        (
            jnp.full((block, 1), NEGATIVE_FILL, WIDE),
            jnp.zeros((block, 1), WIDE),
            jnp.zeros((block, wide), WIDE),
        )
        for _ in range(heads)
    )
    state = lax.fori_loop(0, index, lambda c, s: step(c, s, False), state)
    state = step(index, state, True)
    result = None
    spot = lane_of((block, LANES))
    logs = jnp.zeros((block, LANES), WIDE)
    for h in range(heads):
        top, total, summed = state[h]
        piece = summed / total
        result = piece if result is None else jnp.where(mine[h], piece, result)
        logs = jnp.where(spot == h, top + jnp.log(total), logs)
    out_ref[...] = result.astype(LOW).reshape(pieces, stretch, wide)
    lse_ref[...] = jnp.transpose(logs)[0:8, :]


def attend_specs(triple, block):
    span, _, seqs, stretch, wide = triple.shape
    pieces = min(block, span * stretch) // stretch
    part = pl.BlockSpec((pieces, None, stretch, wide), lambda s, i: (i, s, 0, 0))
    query = pl.BlockSpec((pieces, None, None, stretch, wide), lambda s, i: (i, 0, s, 0, 0))
    keys = pl.BlockSpec((span, None, None, stretch, wide), lambda s, i: (0, 1, s, 0, 0))
    values = pl.BlockSpec((span, None, None, stretch, wide), lambda s, i: (0, 2, s, 0, 0))
    logs = pl.BlockSpec((None, 8, pieces * stretch), lambda s, i: (s, 0, i))
    return (seqs, span // pieces), part, query, keys, values, logs


def attend_forward(triple, heads, block, scale):
    span, _, seqs, stretch, wide = triple.shape
    length = span * stretch
    grid, part, query, keys, values, logs = attend_specs(triple, block)
    pairs = seqs * heads * length * length // 2
    return pl.pallas_call(
        partial(attend_forward_kernel, heads, scale),
        grid=grid,
        in_specs=[query, keys, values],
        out_specs=[part, logs],
        out_shape=[
            jax.ShapeDtypeStruct((span, seqs, stretch, wide), LOW),
            jax.ShapeDtypeStruct((seqs, 8, length), WIDE),
        ],
        cost_estimate=pl.CostEstimate(
            flops=pairs, bytes_accessed=seqs * length * wide, transcendentals=0
        ),
        compiler_params=pltpu.CompilerParams(vmem_limit_bytes=VMEM_LIMIT),
        name="attend_forward",
    )(triple, triple, triple)


def attend_backward_kernel(
    heads, scale, query_ref, key_ref, value_ref, out_ref, grad_ref, lse_ref, triple_ref, dk_sum, dv_sum
):
    pieces, stretch, wide = query_ref.shape
    block = pieces * stretch
    span = key_ref.shape[0]
    head = wide // heads
    index = pl.program_id(1)

    @pl.when(index == 0)
    def _():
        dk_sum[...] = jnp.zeros_like(dk_sum)
        dv_sum[...] = jnp.zeros_like(dv_sum)

    query = query_ref[...].reshape(block, wide) * jnp.asarray(scale, LOW)
    grad = grad_ref[...].reshape(block, wide)
    lane = lane_of((block, wide))
    mine = [(lane >= h * head) & (lane < (h + 1) * head) for h in range(heads)]
    zero = jnp.zeros_like(query)
    own_query = [jnp.where(mine[h], query, zero) for h in range(heads)]
    own_grad = [jnp.where(mine[h], grad, zero) for h in range(heads)]
    product = out_ref[...].reshape(block, wide).astype(WIDE) * grad.astype(WIDE)
    spot = lane_of((block, LANES))
    centres = jnp.zeros((block, LANES), WIDE)
    for h in range(heads):
        centre = jnp.sum(jnp.where(mine[h], product, 0.0), axis=1, keepdims=True)
        centres = jnp.where(spot == h, centre, centres)
    centres = jnp.transpose(centres)
    logs = lse_ref[...]

    def step(c, state, masked):
        spots = pl.ds(c * pieces, pieces)
        rows = pl.ds(pl.multiple_of(c * block, block), block)
        keys = key_ref[spots].reshape(block, wide)
        values = value_ref[spots].reshape(block, wide)
        fresh = []
        key_part, value_part = None, None
        for h in range(heads):
            scores = lax.dot_general(
                keys, own_query[h], (((1,), (1,)), ((), ())), preferred_element_type=WIDE
            )
            probs = jnp.exp(scores - logs[h : h + 1, :])
            if masked:
                here = lax.broadcasted_iota(jnp.int32, scores.shape, 0)
                probs = jnp.where(here <= lane_of(scores.shape), probs, 0.0)
            grad_probs = lax.dot_general(
                values, own_grad[h], (((1,), (1,)), ((), ())), preferred_element_type=WIDE
            )
            slope = (probs * (grad_probs - centres[h : h + 1, :])).astype(LOW)
            a = jnp.dot(slope, own_query[h], preferred_element_type=WIDE)
            b = jnp.dot(probs.astype(LOW), own_grad[h], preferred_element_type=WIDE)
            key_part = a if key_part is None else key_part + a
            value_part = b if value_part is None else value_part + b
            fresh.append(
                state[h]
                + lax.dot_general(slope, keys, (((0,), (0,)), ((), ())), preferred_element_type=WIDE)
            )
        dk_sum[rows, :] += key_part
        dv_sum[rows, :] += value_part
        return tuple(fresh)

    state = tuple(jnp.zeros((block, wide), WIDE) for _ in range(heads))
    state = lax.fori_loop(0, index, lambda c, s: step(c, s, False), state)
    state = step(index, state, True)
    result = state[0]
    for h in range(1, heads):
        result = jnp.where(mine[h], state[h], result)
    triple_ref[pl.ds(index * pieces, pieces), 0] = (
        (result * scale).astype(LOW).reshape(pieces, stretch, wide)
    )

    @pl.when(index == pl.num_programs(1) - 1)
    def _():
        triple_ref[:, 1] = dk_sum[...].astype(LOW).reshape(span, stretch, wide)
        triple_ref[:, 2] = dv_sum[...].astype(LOW).reshape(span, stretch, wide)


def attend_backward(triple, attended, grad, lse, heads, block, scale):
    span, _, seqs, stretch, wide = triple.shape
    length = span * stretch
    grid, part, query, keys, values, logs = attend_specs(triple, block)
    pairs = seqs * heads * length * length // 2
    return pl.pallas_call(
        partial(attend_backward_kernel, heads, scale),
        grid=grid,
        in_specs=[query, keys, values, part, part, logs],
        out_specs=pl.BlockSpec((span, 3, None, stretch, wide), lambda s, i: (0, 0, s, 0, 0)),
        out_shape=jax.ShapeDtypeStruct((span, 3, seqs, stretch, wide), LOW),
        scratch_shapes=[pltpu.VMEM((length, wide), WIDE), pltpu.VMEM((length, wide), WIDE)],
        cost_estimate=pl.CostEstimate(
            flops=pairs, bytes_accessed=seqs * length * wide, transcendentals=0
        ),
        compiler_params=pltpu.CompilerParams(vmem_limit_bytes=VMEM_LIMIT),
        name="attend_backward",
    )(triple, triple, triple, attended, grad, lse)


def turn_tables(positions, repeats, parts, wide, head):
    halfway = ROT // 2
    place = jnp.arange(parts * wide)
    entry = place % head
    turned = (place // wide < 2) & (entry < ROT)
    frequency = 10000.0 ** (-2.0 * (entry % halfway).astype(WIDE) / ROT)
    angles = positions.astype(WIDE)[:, None] * frequency[None, :]
    sine = jnp.where(turned, jnp.sin(angles), 0.0)
    cosine = jnp.where(turned, jnp.cos(angles), 1.0)
    later = jnp.where(entry < halfway, -sine, 0.0)
    earlier = jnp.where(entry < halfway, 0.0, sine)
    return tuple(jnp.tile(table, (1, repeats)) for table in (cosine, later, earlier))


def turn_packs(span, wide):
    return 1 if (3 * wide) % LANES == 0 else 2


def queries_kernel(seqs, wide, rows_ref, table_ref, bias_ref, cosine_ref, later_ref, earlier_ref, out_ref):
    halfway = ROT // 2
    columns = table_ref.shape[1]
    values = jnp.dot(rows_ref[...], table_ref[...], preferred_element_type=WIDE) + bias_ref[...]
    stretch = cosine_ref.shape[0]
    for s in range(seqs):
        part = values[s * stretch : (s + 1) * stretch]
        part = (
            part * cosine_ref[...]
            + pltpu.roll(part, columns - halfway, 1) * later_ref[...]
            + pltpu.roll(part, halfway, 1) * earlier_ref[...]
        ).astype(LOW)
        for j in range(columns // wide):
            out_ref[j // 3, j % 3, s] = part[:, j * wide : (j + 1) * wide]


def project_queries(rows, table, bias, tables, span, seqs, wide):
    total, width = rows.shape
    stretch = total // seqs
    packs = turn_packs(span, wide)
    columns = packs * 3 * wide
    fixed = pl.BlockSpec((stretch, columns), lambda g: (0, 0))
    return pl.pallas_call(
        partial(queries_kernel, seqs, wide),
        grid=(span // packs,),
        in_specs=[
            pl.BlockSpec((total, width), lambda g: (0, 0)),
            pl.BlockSpec((width, columns), lambda g: (0, g)),
            pl.BlockSpec((1, columns), lambda g: (0, g)),
            fixed,
            fixed,
            fixed,
        ],
        out_specs=pl.BlockSpec((packs, 3, seqs, stretch, wide), lambda g: (g, 0, 0, 0, 0)),
        out_shape=jax.ShapeDtypeStruct((span, 3, seqs, stretch, wide), LOW),
        cost_estimate=pl.CostEstimate(
            flops=2 * total * width * span * 3 * wide,
            bytes_accessed=2 * width * span * 3 * wide,
            transcendentals=0,
        ),
        compiler_params=pltpu.CompilerParams(vmem_limit_bytes=VMEM_LIMIT),
        name="project_queries",
    )(rows, table, bias, *tables)


def unturn_kernel(seqs, wide, triple_ref, cosine_ref, later_ref, earlier_ref, out_ref):
    halfway = ROT // 2
    columns = out_ref.shape[1]
    stretch = cosine_ref.shape[0]
    for s in range(seqs):
        part = jnp.concatenate(
            [triple_ref[j // 3, j % 3, s].astype(WIDE) for j in range(columns // wide)], axis=1
        )
        part = (
            part * cosine_ref[...]
            - pltpu.roll(part, columns - halfway, 1) * later_ref[...]
            - pltpu.roll(part, halfway, 1) * earlier_ref[...]
        )
        out_ref[s * stretch : (s + 1) * stretch, :] = part.astype(LOW)


def unturn(triple, tables):
    span, _, seqs, stretch, wide = triple.shape
    packs = turn_packs(span, wide)
    columns = packs * 3 * wide
    fixed = pl.BlockSpec((stretch, columns), lambda g: (0, 0))
    return pl.pallas_call(
        partial(unturn_kernel, seqs, wide),
        grid=(span // packs,),
        in_specs=[
            pl.BlockSpec((packs, 3, seqs, stretch, wide), lambda g: (g, 0, 0, 0, 0)),
            fixed,
            fixed,
            fixed,
        ],
        out_specs=pl.BlockSpec((seqs * stretch, columns), lambda g: (0, g)),
        out_shape=jax.ShapeDtypeStruct((seqs * stretch, span * 3 * wide), LOW),
        compiler_params=pltpu.CompilerParams(vmem_limit_bytes=VMEM_LIMIT),
        name="unturn",
    )(triple, *tables)


def gelu_exact(values):
    return jax.nn.gelu(values, approximate=False)


def standardize(values):
    average = jnp.mean(values, axis=-1, keepdims=True)
    centered = values - average
    variance = jnp.mean(centered * centered, axis=-1, keepdims=True)
    inverse = lax.rsqrt(variance + NORM_EPS)
    return centered * inverse, inverse


def standardize_pull(scaled, normal, inverse):
    return inverse * (
        scaled
        - jnp.mean(scaled, axis=-1, keepdims=True)
        - normal * jnp.mean(scaled * normal, axis=-1, keepdims=True)
    )


def adam_update(weight, first, second, grad, clip_factor, rate, decay):
    grad = grad * clip_factor
    first_new = BETA_ONE * first + (1.0 - BETA_ONE) * grad
    second_new = BETA_TWO * second + (1.0 - BETA_TWO) * grad * grad
    fix_one = 1.0 - BETA_ONE**STEP_COUNT
    fix_two = 1.0 - BETA_TWO**STEP_COUNT
    direction = first_new / fix_one / (jnp.sqrt(second_new / fix_two) + ADAM_EPS)
    return (weight - rate * (direction + decay * weight), first_new, second_new)


def summed_over(vector, axes):
    for axis in axes:
        vector = jnp.sum(lax.all_gather(vector, axis), axis=0)
    return vector


def gathered(shard):
    rows = lax.all_gather(shard, "dp")
    rows = lax.all_gather(rows, "sp", axis=1, tiled=True)
    return rows.reshape(-1, shard.shape[1])


def scattered(gradient):
    dp, sp = lax.axis_size("dp"), lax.axis_size("sp")
    rows, columns = gradient.shape
    gradient = gradient.reshape(dp, sp, rows // (dp * sp), columns).transpose(1, 0, 2, 3)
    gradient = gradient.reshape(rows, columns)
    return lax.psum_scatter(gradient, "sp", scatter_dimension=0, tiled=True)


def joined_teams(gradient):
    dp = lax.axis_size("dp")
    rows, columns = gradient.shape
    gradient = lax.all_to_all(gradient, "dp", split_axis=0, concat_axis=0, tiled=True)
    return jnp.sum(gradient.reshape(dp, rows // dp, columns).astype(WIDE), axis=0)


def moved(array, axis, step):
    size = lax.axis_size(axis)
    return lax.ppermute(array, axis, [(i, (i + step) % size) for i in range(size)])


def turned(values, teams, team):
    share = values.shape[1] // teams
    blocks = [values[:, b * share : (b + 1) * share] for b in range(teams)]
    order = [blocks[(teams - 1 - m) % teams] for m in range(2 * teams - 1)]
    row = jnp.concatenate(order, axis=1)
    return lax.dynamic_slice_in_dim(row, (teams - 1 - team) * share, teams * share, 1)


def local(
    token_ids,
    targets,
    stream_ids,
    embed_table,
    embed_first,
    embed_second,
    unembed,
    unembed_first,
    unembed_second,
    proj_in,
    proj_in_first,
    proj_in_second,
    proj_out,
    proj_out_first,
    proj_out_second,
    norm_params,
    norm_first,
    norm_second,
    biases,
    bias_first,
    bias_second,
):
    span = lax.axis_size("sp")
    teams = lax.axis_size("dp")
    sp_index = lax.axis_index("sp")
    dp_index = lax.axis_index("dp")
    seq_here, length = token_ids.shape
    stretch = length // span
    vocab_local = embed_table.shape[0]
    slab, in_columns = proj_in.shape
    width = proj_out.shape[1]
    triple_columns = 3 * width
    hidden_units = in_columns - triple_columns
    heads_here = HEADS // span
    head_dim = width // HEADS
    wide = heads_here * head_dim
    scale = head_dim ** (-0.5)
    tokens_here = seq_here * stretch
    offset = sp_index * vocab_local

    bias_rows = biases.shape[0] // slab
    norm_rows = norm_params.shape[0]
    shard_triple = proj_in[:, :triple_columns].astype(LOW)
    shard_triple = shard_triple.reshape(slab, span, heads_here, 3, head_dim).transpose(0, 1, 3, 2, 4)
    shard_triple = shard_triple.reshape(slab, triple_columns)
    extras = jnp.concatenate([norm_params.T, biases.reshape(slab, bias_rows)], axis=1).astype(LOW)
    extras = jnp.pad(extras, ((0, 0), (0, LANES - extras.shape[1])))
    shard_triple = jnp.concatenate([shard_triple, extras], axis=1)
    vocab_step = CHUNKS * LANES
    vocab_padded = -(-vocab_local // vocab_step) * vocab_step
    own_table = jnp.pad(unembed.T.astype(LOW), ((0, vocab_padded - vocab_local), (0, 0)))
    token_ids, shard_triple, own_table = lax.optimization_barrier(
        (token_ids, shard_triple, own_table)
    )
    wide_triple = lax.all_gather(shard_triple, ("dp", "sp"), axis=0, tiled=True)
    half = vocab_padded // 2
    middle = teams // 2
    ids_all = lax.all_gather(token_ids, "dp")
    ids_all, own_table = lax.optimization_barrier((ids_all, own_table))
    far_first = moved(own_table[:half], "dp", middle)
    ids_all = ids_all.reshape(teams, seq_here, span, stretch).transpose(2, 0, 1, 3).reshape(-1)
    local_ids = ids_all - offset
    in_slice = (local_ids >= 0) & (local_ids < vocab_local)
    safe_ids = jnp.clip(local_ids, 0, vocab_local - 1)
    picked = jnp.where(
        in_slice[:, None],
        embed_table.astype(LOW).at[safe_ids].get(mode="promise_in_bounds"),
        jnp.zeros((), LOW),
    )
    shard_up, shard_out = proj_in[:, triple_columns:].astype(LOW), proj_out.astype(LOW)
    picked, wide_triple, far_first, own_table = lax.optimization_barrier(
        (picked, wide_triple, far_first, own_table)
    )
    tables = {k: moved(own_table, "dp", k) for k in range(1, middle)}
    hidden0 = lax.psum_scatter(picked, "sp", scatter_dimension=0, tiled=True)
    hidden0, tables, shard_up, shard_out = lax.optimization_barrier(
        (hidden0, tables, shard_up, shard_out)
    )
    wide_up = gathered(shard_up)
    wide_out = gathered(shard_out)
    hidden0 = lax.all_to_all(hidden0, "dp", split_axis=0, concat_axis=1, tiled=True)
    hidden0, later_table = lax.optimization_barrier((hidden0, own_table))
    hidden0 = hidden0.astype(WIDE)
    for k in range(middle + 1, teams):
        tables[k] = moved(later_table, "dp", k)
    norm_vals = wide_triple[:, triple_columns : triple_columns + norm_rows].astype(WIDE).T
    bias_vals = wide_triple[
        :, triple_columns + norm_rows : triple_columns + norm_rows + bias_rows
    ]
    bias_vals = bias_vals.astype(WIDE).reshape(-1)
    triple_bias = bias_vals[:triple_columns].reshape(span, heads_here, 3, head_dim)
    triple_bias = triple_bias.transpose(0, 2, 1, 3).reshape(1, triple_columns)

    normal0, inverse0 = standardize(hidden0)
    normed_one = (normal0 * norm_vals[0] + norm_vals[1]).astype(LOW)
    normed_two = (normal0 * norm_vals[2] + norm_vals[3]).astype(LOW)
    positions = sp_index * stretch + jnp.arange(stretch)
    angles = turn_tables(positions, turn_packs(span, wide), 3, wide, head_dim)
    packed = project_queries(normed_one, wide_triple, triple_bias, angles, span, seq_here, wide)
    triple = lax.all_to_all(packed, "sp", split_axis=0, concat_axis=0, tiled=True)
    triple, tables, later_table = lax.optimization_barrier((triple, tables, later_table))
    far_last = moved(later_table[half:], "dp", middle)
    attended_heads, log_totals = attend_forward(triple, heads_here, ATTEND_ROWS, scale)
    attended = lax.all_to_all(attended_heads, "sp", split_axis=0, concat_axis=0, tiled=True)
    attended, far_last = lax.optimization_barrier((attended, far_last))
    tables[middle] = jnp.concatenate([far_first, far_last], axis=0)
    tables = [own_table] + [tables[k] for k in range(1, teams)]
    attended = attended.reshape(span, tokens_here, wide).transpose(1, 0, 2).reshape(tokens_here, width)
    up_values = (
        jnp.dot(normed_two, wide_up, preferred_element_type=WIDE)
        + bias_vals[triple_columns:in_columns]
    )
    act_f, pull_gelu = jax.vjp(gelu_exact, up_values)
    joined = jnp.concatenate([attended, act_f.astype(LOW)], axis=-1)
    hidden1 = (
        hidden0 + jnp.dot(joined, wide_out, preferred_element_type=WIDE) + bias_vals[in_columns:]
    )
    normal1, inverse1 = standardize(hidden1)
    final = (normal1 * norm_vals[4] + norm_vals[5]).astype(LOW)
    final = turned(final, teams, dp_index)
    rows_all = lax.all_gather(final.reshape(seq_here, stretch, width), "sp", axis=1, tiled=True)
    rows_all = rows_all.reshape(-1, width)
    grand = rows_all.shape[0]
    labels = targets.reshape(-1, 1) - offset
    powers, stats, lines = head_forward(rows_all, tables, labels, vocab_local)
    merged = lax.all_gather(lines[0:3], "sp")
    highest = jnp.max(merged[:, 0], axis=0)
    summed = jnp.sum(merged[:, 1] * jnp.exp(merged[:, 0] - highest), axis=0)
    log_sum = highest + jnp.log(summed)
    token_loss = (log_sum - jnp.sum(merged[:, 2], axis=0)).reshape(seq_here, length)
    weight_all = 1.0 + (REPLAY_WEIGHT - 1.0) * stream_ids.astype(WIDE)
    total_weight = jnp.sum(weight_all)
    seq_weight = lax.dynamic_slice_in_dim(weight_all, dp_index * seq_here, seq_here, 0)
    loss_local = jnp.sum(seq_weight * jnp.mean(token_loss, axis=1))
    token_scale = jnp.broadcast_to(
        (seq_weight / (total_weight * length))[:, None], (seq_here, length)
    ).reshape(-1)
    guide = jnp.concatenate(
        [log_sum[None], token_scale[None], jnp.zeros((6, grand), WIDE)], axis=0
    )
    slopes, grad_rows = head_backward(stats, guide, labels, powers, tables)
    final_grad = lax.psum_scatter(
        grad_rows.reshape(seq_here, length, width), "sp", scatter_dimension=1, tiled=True
    ).astype(WIDE)
    final_grad = final_grad.reshape(tokens_here, width)
    share = width // teams
    inner = rows_all[:, share : (middle + 1) * share]
    outer = jnp.concatenate([rows_all[:, :share], rows_all[:, (middle + 1) * share :]], axis=1)
    inner, outer = [
        lax.dot_general(
            slopes, side, (((0,), (0,)), ((), ())), preferred_element_type=WIDE
        ).astype(LOW)
        for side in (inner, outer)
    ]
    arrived = [
        moved(inner[:, (k - 1) * share : k * share], "dp", teams - k) for k in range(1, middle)
    ]
    far = inner[:, (middle - 1) * share :]
    quarter = vocab_padded // 4
    far = [far[q * quarter : (q + 1) * quarter] for q in range(4)]
    far[0] = moved(far[0], "dp", middle)
    final_grad, inner, outer = lax.optimization_barrier((final_grad, inner, outer))
    final_grad = turned(final_grad, teams, dp_index)

    g_gain_final = jnp.sum(final_grad * normal1, axis=0)
    g_shift_final = jnp.sum(final_grad, axis=0)
    d_hidden1 = standardize_pull(final_grad * norm_vals[4], normal1, inverse1)
    d_branch = d_hidden1.astype(LOW)
    g_out = lax.dot_general(
        joined, d_branch, (((0,), (0,)), ((), ())), preferred_element_type=WIDE
    ).astype(LOW)
    g_bias_out = jnp.sum(d_branch.astype(WIDE), axis=0)
    contract_last = (((1,), (1,)), ((), ()))
    d_attended = lax.dot_general(
        d_branch, wide_out[:width], contract_last, preferred_element_type=WIDE
    ).astype(LOW)
    d_attended = d_attended.reshape(seq_here, stretch, span, wide).transpose(2, 0, 1, 3)
    d_heads = lax.all_to_all(d_attended, "sp", split_axis=0, concat_axis=0, tiled=True)
    d_act = lax.dot_general(d_branch, wide_out[width:], contract_last, preferred_element_type=WIDE)
    d_up = pull_gelu(d_act)[0].astype(LOW)
    g_up = lax.dot_general(
        normed_two, d_up, (((0,), (0,)), ((), ())), preferred_element_type=WIDE
    ).astype(LOW)
    d_normed_two = lax.dot_general(
        d_up, wide_up, contract_last, preferred_element_type=WIDE
    )
    d_heads, g_out, g_up, d_normed_two, arrived, far = lax.optimization_barrier(
        (d_heads, g_out, g_up, d_normed_two, arrived, far)
    )
    far[1] = moved(far[1], "dp", middle)
    r_out = scattered(g_out)
    r_up = scattered(g_up)
    d_triple = attend_backward(
        triple, attended_heads, d_heads, log_totals, heads_here, ATTEND_ROWS, scale
    )
    d_triple, far = lax.optimization_barrier((d_triple, far))
    far[2] = moved(far[2], "dp", middle)
    d_triple = lax.all_to_all(d_triple, "sp", split_axis=0, concat_axis=0, tiled=True)
    d_joint = unturn(d_triple, angles)
    g_triple = lax.dot_general(
        normed_one, d_joint, (((0,), (0,)), ((), ())), preferred_element_type=WIDE
    ).astype(LOW)
    d_normed_one = lax.dot_general(
        d_joint, wide_triple[:, :triple_columns], contract_last, preferred_element_type=WIDE
    )
    d_normed_one, far, outer = lax.optimization_barrier((d_normed_one, far, outer))
    own_part = outer[:, :share]
    late = [
        (k, outer[:, (k - middle) * share : (k - middle + 1) * share])
        for k in range(middle + 1, teams)
    ]
    late_first = [moved(part[:half], "dp", teams - k) for k, part in late]
    g_gain_one = jnp.sum(d_normed_one * normal0, axis=0)
    g_shift_one = jnp.sum(d_normed_one, axis=0)
    g_gain_two = jnp.sum(d_normed_two * normal0, axis=0)
    g_shift_two = jnp.sum(d_normed_two, axis=0)
    d_sum = d_normed_one * norm_vals[0] + d_normed_two * norm_vals[2]
    d_hidden0 = (d_hidden1 + standardize_pull(d_sum, normal0, inverse0)).astype(LOW)
    grad_all = lax.all_to_all(d_hidden0, "dp", split_axis=1, concat_axis=0, tiled=True)
    late_rest = [part[half:] for k, part in late]
    grad_all, r_out, r_up, late_first, late_rest = lax.optimization_barrier(
        (grad_all, r_out, r_up, late_first, late_rest)
    )
    late_rest = [moved(late_rest[j], "dp", teams - late[j][0]) for j in range(len(late))]
    grad_all = lax.all_gather(grad_all, "sp", axis=0, tiled=True)
    grad_all, late_rest, far = lax.optimization_barrier((grad_all, late_rest, far))
    far[3] = moved(far[3], "dp", middle)
    target_ids = jnp.where(in_slice, local_ids, vocab_local)
    r_embed = (
        jnp.zeros(embed_table.shape, WIDE).at[target_ids].add(grad_all.astype(WIDE), mode="drop")
    )

    g_bias_triple = jnp.sum(d_joint.astype(WIDE), axis=0).reshape(span, 3, heads_here, head_dim)
    g_bias = jnp.concatenate(
        [
            g_bias_triple.transpose(0, 2, 1, 3).reshape(-1),
            jnp.sum(d_up.astype(WIDE), axis=0),
            g_bias_out,
        ]
    )
    g_norm = jnp.stack(
        [g_gain_one, g_shift_one, g_gain_two, g_shift_two, g_gain_final, g_shift_final], axis=1
    )
    g_extra = jnp.concatenate([g_norm, g_bias.reshape(width, bias_rows)], axis=1).astype(LOW)
    g_extra = jnp.pad(g_extra, ((0, 0), (0, LANES - g_extra.shape[1])))
    r_triple = scattered(jnp.concatenate([g_triple, g_extra], axis=1))
    r_triple, r_up, r_out = joined_teams(r_triple), joined_teams(r_up), joined_teams(r_out)
    r_embed, far, late_first, late_rest, arrived, r_out, own_part = lax.optimization_barrier(
        (r_embed, far, late_first, late_rest, arrived, r_out, own_part)
    )
    late = [jnp.concatenate(pair, axis=0) for pair in zip(late_first, late_rest)]
    r_unembed = [own_part, *arrived, *late, jnp.concatenate(far, axis=0)]
    r_norm = r_triple[:, triple_columns : triple_columns + norm_rows].T
    r_bias = r_triple[
        :, triple_columns + norm_rows : triple_columns + norm_rows + bias_rows
    ].reshape(-1)
    r_triple = r_triple[:, :triple_columns].reshape(slab, span, 3, heads_here, head_dim)
    r_triple = r_triple.transpose(0, 1, 3, 2, 4).reshape(slab, triple_columns)
    r_in = jnp.concatenate([r_triple, r_up], axis=1)
    r_unembed = sum(part[:vocab_local].astype(WIDE) for part in r_unembed).T

    reduced = (r_embed, r_unembed, r_in, r_out, r_norm, r_bias)
    squares = jnp.float32(0.0)
    for grad_piece in reduced:
        squares = squares + jnp.sum(grad_piece * grad_piece)
    loss_term = jnp.where(sp_index == 0, loss_local, 0.0)
    totals = summed_over(jnp.stack([squares, loss_term]), ("sp", "dp"))
    squares_total, loss_total = totals[0], totals[1]
    grad_norm = jnp.sqrt(squares_total)
    mean_loss = loss_total / total_weight
    clip_factor = jnp.minimum(1.0, CLIP_LEVEL / (grad_norm + 1e-06))
    masters = (embed_table, unembed, proj_in, proj_out, norm_params, biases)
    firsts = (embed_first, unembed_first, proj_in_first, proj_out_first, norm_first, bias_first)
    seconds = (
        embed_second,
        unembed_second,
        proj_in_second,
        proj_out_second,
        norm_second,
        bias_second,
    )
    rates = (1.0, 0.05, 0.05, 0.1, 0.5, 0.5)
    decays = (WEIGHT_DECAY, WEIGHT_DECAY, WEIGHT_DECAY, WEIGHT_DECAY, 0.0, 0.0)
    results = []
    for index in range(6):
        results.extend(
            adam_update(
                masters[index],
                firsts[index],
                seconds[index],
                reduced[index],
                clip_factor,
                rates[index],
                decays[index],
            )
        )
    return (
        mean_loss,
        grad_norm,
        results[0],
        results[1],
        results[2],
        results[3],
        results[4],
        results[5],
        results[6],
        results[7],
        results[8],
        results[9],
        results[10],
        results[11],
        results[12],
        results[13],
        results[14],
        results[15],
        results[16],
        results[17],
    )


def solution(mesh):
    in_specs = (
        P("dp", None),
        P("dp", None),
        P(),
        P("sp", "dp"),
        P("sp", "dp"),
        P("sp", "dp"),
        P("dp", "sp"),
        P("dp", "sp"),
        P("dp", "sp"),
        P(("dp", "sp"), None),
        P(("dp", "sp"), None),
        P(("dp", "sp"), None),
        P(("dp", "sp"), None),
        P(("dp", "sp"), None),
        P(("dp", "sp"), None),
        P(None, ("dp", "sp")),
        P(None, ("dp", "sp")),
        P(None, ("dp", "sp")),
        P(("dp", "sp")),
        P(("dp", "sp")),
        P(("dp", "sp")),
    )
    out_specs = (
        P(),
        P(),
        P("sp", "dp"),
        P("sp", "dp"),
        P("sp", "dp"),
        P("dp", "sp"),
        P("dp", "sp"),
        P("dp", "sp"),
        P(("dp", "sp"), None),
        P(("dp", "sp"), None),
        P(("dp", "sp"), None),
        P(("dp", "sp"), None),
        P(("dp", "sp"), None),
        P(("dp", "sp"), None),
        P(None, ("dp", "sp")),
        P(None, ("dp", "sp")),
        P(None, ("dp", "sp")),
        P(("dp", "sp")),
        P(("dp", "sp")),
        P(("dp", "sp")),
    )
    return jax.shard_map(local, mesh=mesh, in_specs=in_specs, out_specs=out_specs, check_vma=False)
```

```python
from functools import partial

import jax
import jax.numpy as jnp
from jax import lax
from jax.experimental import pallas as pl
from jax.experimental.pallas import tpu as pltpu
from jax.sharding import PartitionSpec as P

HEADS = 16
ROT = 16
STEP_COUNT = 10


NORM_EPS = 1e-05
BETA_ONE = 0.9
BETA_TWO = 0.95
ADAM_EPS = 1e-08
WEIGHT_DECAY = 0.01
CLIP_LEVEL = 0.01
REPLAY_WEIGHT = 4.0
NEGATIVE_FILL = -1e30
LOW = jnp.bfloat16
WIDE = jnp.float32
CHUNKS = 5
LANES = 128
HEAD_ROWS = 512
ATTEND_ROWS = 1024
VMEM_LIMIT = 60 * 1024 * 1024


def lane_of(shape):
    return lax.broadcasted_iota(jnp.int32, shape, 1)


def fetch_table(parts, table_ref, arrivals):
    @pl.when(pl.program_id(0) == 0)
    def _():
        share = table_ref.shape[1] // len(parts)
        copies = [
            pltpu.make_async_copy(
                parts[k], table_ref.at[:, k * share : (k + 1) * share], arrivals.at[k]
            )
            for k in range(len(parts))
        ]
        for copy in copies:
            copy.start()
        for copy in copies:
            copy.wait()


def head_forward_kernel(teams, real, rows_ref, label_ref, *refs):
    powers_ref, stats_ref, lines_ref, table_ref, arrivals = refs[teams:]
    fetch_table(refs[:teams], table_ref, arrivals)
    padded = table_ref.shape[0]
    part = padded // CHUNKS
    rows = rows_ref[...]
    count = rows.shape[0]
    label = label_ref[...]
    lane = lane_of((count, LANES))
    stats = jnp.zeros((count, LANES), WIDE)
    tops, sums = [], []
    chosen = jnp.zeros((count, 1), WIDE)
    for c in range(CHUNKS):
        logits = lax.dot_general(
            rows,
            table_ref[c * part : (c + 1) * part, :],
            (((1,), (1,)), ((), ())),
            preferred_element_type=WIDE,
        )
        column = lane_of(logits.shape) + c * part
        chosen = chosen + jnp.sum(jnp.where(column == label, logits, 0.0), axis=1, keepdims=True)
        if (c + 1) * part > real:
            logits = jnp.where(column < real, logits, NEGATIVE_FILL)
        top = jnp.max(logits, axis=1, keepdims=True)
        powers = jnp.exp(logits - top)
        sums.append(jnp.sum(powers, axis=1, keepdims=True))
        tops.append(top)
        powers_ref[:, c * part : (c + 1) * part] = powers.astype(LOW)
        stats = jnp.where(lane == 8 + c, top, stats)
    highest = tops[0]
    for c in range(1, CHUNKS):
        highest = jnp.maximum(highest, tops[c])
    total = jnp.zeros((count, 1), WIDE)
    for c in range(CHUNKS):
        total = total + sums[c] * jnp.exp(tops[c] - highest)
    stats = jnp.where(lane == 0, highest, stats)
    stats = jnp.where(lane == 1, total, stats)
    stats = jnp.where(lane == 2, chosen, stats)
    stats_ref[...] = stats
    lines_ref[...] = jnp.transpose(stats)[0:8, :]


def head_forward(rows, tables, label, real):
    total, width = rows.shape
    padded = tables[0].shape[0]
    teams = len(tables)
    count = min(HEAD_ROWS, total)
    return pl.pallas_call(
        partial(head_forward_kernel, teams, real),
        grid=(total // count,),
        in_specs=[
            pl.BlockSpec((count, width), lambda i: (i, 0)),
            pl.BlockSpec((count, 1), lambda i: (i, 0)),
        ]
        + [pl.BlockSpec(memory_space=pl.ANY)] * teams,
        out_specs=[
            pl.BlockSpec((count, padded), lambda i: (i, 0)),
            pl.BlockSpec((count, LANES), lambda i: (i, 0)),
            pl.BlockSpec((8, count), lambda i: (0, i)),
        ],
        out_shape=[
            jax.ShapeDtypeStruct((total, padded), LOW),
            jax.ShapeDtypeStruct((total, LANES), WIDE),
            jax.ShapeDtypeStruct((8, total), WIDE),
        ],
        scratch_shapes=[pltpu.VMEM((padded, width), LOW), pltpu.SemaphoreType.DMA((teams,))],
        cost_estimate=pl.CostEstimate(
            flops=2 * total * width * padded,
            bytes_accessed=2 * (total * (width + padded) + width * padded),
            transcendentals=total * padded,
        ),
        compiler_params=pltpu.CompilerParams(vmem_limit_bytes=VMEM_LIMIT),
        name="head_forward",
    )(rows, label, *tables)


def head_backward_kernel(teams, stats_ref, lines_ref, label_ref, powers_ref, *refs):
    slope_ref, grad_ref, table_ref, arrivals = refs[teams:]
    fetch_table(refs[:teams], table_ref, arrivals)
    padded = table_ref.shape[0]
    part = padded // CHUNKS
    stats = stats_ref[...]
    label = label_ref[...]
    lines = lines_ref[...]
    lines = jnp.transpose(jnp.concatenate([lines] * (LANES // 8), axis=0))
    lse = lines[:, 0:1]
    scale = lines[:, 1:2]
    total = None
    for c in range(CHUNKS):
        ratio = scale * jnp.exp(stats[:, 8 + c : 9 + c] - lse)
        slope = powers_ref[:, c * part : (c + 1) * part].astype(WIDE) * ratio
        column = lane_of(slope.shape) + c * part
        slope = jnp.where(column == label, slope - scale, slope).astype(LOW)
        slope_ref[:, c * part : (c + 1) * part] = slope
        piece = jnp.dot(
            slope, table_ref[c * part : (c + 1) * part, :], preferred_element_type=WIDE
        )
        total = piece if total is None else total + piece
    grad_ref[...] = total.astype(LOW)


def head_backward(stats, lines, label, powers, tables):
    total, padded = powers.shape
    teams = len(tables)
    width = teams * tables[0].shape[1]
    count = min(HEAD_ROWS, total)
    return pl.pallas_call(
        partial(head_backward_kernel, teams),
        grid=(total // count,),
        in_specs=[
            pl.BlockSpec((count, LANES), lambda i: (i, 0)),
            pl.BlockSpec((8, count), lambda i: (0, i)),
            pl.BlockSpec((count, 1), lambda i: (i, 0)),
            pl.BlockSpec((count, padded), lambda i: (i, 0)),
        ]
        + [pl.BlockSpec(memory_space=pl.ANY)] * teams,
        out_specs=[
            pl.BlockSpec((count, padded), lambda i: (i, 0)),
            pl.BlockSpec((count, width), lambda i: (i, 0)),
        ],
        out_shape=[
            jax.ShapeDtypeStruct((total, padded), LOW),
            jax.ShapeDtypeStruct((total, width), LOW),
        ],
        scratch_shapes=[pltpu.VMEM((padded, width), LOW), pltpu.SemaphoreType.DMA((teams,))],
        cost_estimate=pl.CostEstimate(
            flops=2 * total * width * padded,
            bytes_accessed=2 * (total * (width + 2 * padded) + width * padded),
            transcendentals=0,
        ),
        compiler_params=pltpu.CompilerParams(vmem_limit_bytes=VMEM_LIMIT),
        name="head_backward",
    )(stats, lines, label, powers, *tables)


def attend_forward_kernel(heads, scale, query_ref, key_ref, value_ref, out_ref, lse_ref):
    pieces, stretch, wide = query_ref.shape
    block = pieces * stretch
    head = wide // heads
    index = pl.program_id(1)
    query = query_ref[...].reshape(block, wide) * jnp.asarray(scale, LOW)
    lane = lane_of((block, wide))
    mine = [(lane >= h * head) & (lane < (h + 1) * head) for h in range(heads)]
    own = [jnp.where(mine[h], query, jnp.zeros_like(query)) for h in range(heads)]

    def step(c, state, masked):
        spots = pl.ds(c * pieces, pieces)
        keys = key_ref[spots].reshape(block, wide)
        values = value_ref[spots].reshape(block, wide)
        fresh = []
        for h in range(heads):
            top, total, summed = state[h]
            scores = lax.dot_general(
                own[h], keys, (((1,), (1,)), ((), ())), preferred_element_type=WIDE
            )
            if masked:
                here = lax.broadcasted_iota(jnp.int32, scores.shape, 0)
                scores = jnp.where(here >= lane_of(scores.shape), scores, NEGATIVE_FILL)
            higher = jnp.maximum(top, jnp.max(scores, axis=1, keepdims=True))
            powers = jnp.exp(scores - higher)
            shrink = jnp.exp(top - higher)
            total = total * shrink + jnp.sum(powers, axis=1, keepdims=True)
            summed = summed * shrink + jnp.dot(
                powers.astype(LOW), values, preferred_element_type=WIDE
            )
            fresh.append((higher, total, summed))
        return tuple(fresh)

    state = tuple(
        (
            jnp.full((block, 1), NEGATIVE_FILL, WIDE),
            jnp.zeros((block, 1), WIDE),
            jnp.zeros((block, wide), WIDE),
        )
        for _ in range(heads)
    )
    state = lax.fori_loop(0, index, lambda c, s: step(c, s, False), state)
    state = step(index, state, True)
    result = None
    spot = lane_of((block, LANES))
    logs = jnp.zeros((block, LANES), WIDE)
    for h in range(heads):
        top, total, summed = state[h]
        piece = summed / total
        result = piece if result is None else jnp.where(mine[h], piece, result)
        logs = jnp.where(spot == h, top + jnp.log(total), logs)
    out_ref[...] = result.astype(LOW).reshape(pieces, stretch, wide)
    lse_ref[...] = jnp.transpose(logs)[0:8, :]


def attend_specs(triple, block):
    span, _, seqs, stretch, wide = triple.shape
    pieces = min(block, span * stretch) // stretch
    part = pl.BlockSpec((pieces, None, stretch, wide), lambda s, i: (i, s, 0, 0))
    query = pl.BlockSpec((pieces, None, None, stretch, wide), lambda s, i: (i, 0, s, 0, 0))
    keys = pl.BlockSpec((span, None, None, stretch, wide), lambda s, i: (0, 1, s, 0, 0))
    values = pl.BlockSpec((span, None, None, stretch, wide), lambda s, i: (0, 2, s, 0, 0))
    logs = pl.BlockSpec((None, 8, pieces * stretch), lambda s, i: (s, 0, i))
    return (seqs, span // pieces), part, query, keys, values, logs


def attend_forward(triple, heads, block, scale):
    span, _, seqs, stretch, wide = triple.shape
    length = span * stretch
    grid, part, query, keys, values, logs = attend_specs(triple, block)
    pairs = seqs * heads * length * length // 2
    return pl.pallas_call(
        partial(attend_forward_kernel, heads, scale),
        grid=grid,
        in_specs=[query, keys, values],
        out_specs=[part, logs],
        out_shape=[
            jax.ShapeDtypeStruct((span, seqs, stretch, wide), LOW),
            jax.ShapeDtypeStruct((seqs, 8, length), WIDE),
        ],
        cost_estimate=pl.CostEstimate(
            flops=pairs, bytes_accessed=seqs * length * wide, transcendentals=0
        ),
        compiler_params=pltpu.CompilerParams(vmem_limit_bytes=VMEM_LIMIT),
        name="attend_forward",
    )(triple, triple, triple)


def attend_backward_kernel(
    heads, scale, query_ref, key_ref, value_ref, out_ref, grad_ref, lse_ref, triple_ref, dk_sum, dv_sum
):
    pieces, stretch, wide = query_ref.shape
    block = pieces * stretch
    span = key_ref.shape[0]
    head = wide // heads
    index = pl.program_id(1)

    @pl.when(index == 0)
    def _():
        dk_sum[...] = jnp.zeros_like(dk_sum)
        dv_sum[...] = jnp.zeros_like(dv_sum)

    query = query_ref[...].reshape(block, wide) * jnp.asarray(scale, LOW)
    grad = grad_ref[...].reshape(block, wide)
    lane = lane_of((block, wide))
    mine = [(lane >= h * head) & (lane < (h + 1) * head) for h in range(heads)]
    zero = jnp.zeros_like(query)
    own_query = [jnp.where(mine[h], query, zero) for h in range(heads)]
    own_grad = [jnp.where(mine[h], grad, zero) for h in range(heads)]
    product = out_ref[...].reshape(block, wide).astype(WIDE) * grad.astype(WIDE)
    spot = lane_of((block, LANES))
    centres = jnp.zeros((block, LANES), WIDE)
    for h in range(heads):
        centre = jnp.sum(jnp.where(mine[h], product, 0.0), axis=1, keepdims=True)
        centres = jnp.where(spot == h, centre, centres)
    centres = jnp.transpose(centres)
    logs = lse_ref[...]

    def step(c, state, masked):
        spots = pl.ds(c * pieces, pieces)
        rows = pl.ds(pl.multiple_of(c * block, block), block)
        keys = key_ref[spots].reshape(block, wide)
        values = value_ref[spots].reshape(block, wide)
        fresh = []
        key_part, value_part = None, None
        for h in range(heads):
            scores = lax.dot_general(
                keys, own_query[h], (((1,), (1,)), ((), ())), preferred_element_type=WIDE
            )
            probs = jnp.exp(scores - logs[h : h + 1, :])
            if masked:
                here = lax.broadcasted_iota(jnp.int32, scores.shape, 0)
                probs = jnp.where(here <= lane_of(scores.shape), probs, 0.0)
            grad_probs = lax.dot_general(
                values, own_grad[h], (((1,), (1,)), ((), ())), preferred_element_type=WIDE
            )
            slope = (probs * (grad_probs - centres[h : h + 1, :])).astype(LOW)
            a = jnp.dot(slope, own_query[h], preferred_element_type=WIDE)
            b = jnp.dot(probs.astype(LOW), own_grad[h], preferred_element_type=WIDE)
            key_part = a if key_part is None else key_part + a
            value_part = b if value_part is None else value_part + b
            fresh.append(
                state[h]
                + lax.dot_general(slope, keys, (((0,), (0,)), ((), ())), preferred_element_type=WIDE)
            )
        dk_sum[rows, :] += key_part
        dv_sum[rows, :] += value_part
        return tuple(fresh)

    state = tuple(jnp.zeros((block, wide), WIDE) for _ in range(heads))
    state = lax.fori_loop(0, index, lambda c, s: step(c, s, False), state)
    state = step(index, state, True)
    result = state[0]
    for h in range(1, heads):
        result = jnp.where(mine[h], state[h], result)
    triple_ref[pl.ds(index * pieces, pieces), 0] = (
        (result * scale).astype(LOW).reshape(pieces, stretch, wide)
    )

    @pl.when(index == pl.num_programs(1) - 1)
    def _():
        triple_ref[:, 1] = dk_sum[...].astype(LOW).reshape(span, stretch, wide)
        triple_ref[:, 2] = dv_sum[...].astype(LOW).reshape(span, stretch, wide)


def attend_backward(triple, attended, grad, lse, heads, block, scale):
    span, _, seqs, stretch, wide = triple.shape
    length = span * stretch
    grid, part, query, keys, values, logs = attend_specs(triple, block)
    pairs = seqs * heads * length * length // 2
    return pl.pallas_call(
        partial(attend_backward_kernel, heads, scale),
        grid=grid,
        in_specs=[query, keys, values, part, part, logs],
        out_specs=pl.BlockSpec((span, 3, None, stretch, wide), lambda s, i: (0, 0, s, 0, 0)),
        out_shape=jax.ShapeDtypeStruct((span, 3, seqs, stretch, wide), LOW),
        scratch_shapes=[pltpu.VMEM((length, wide), WIDE), pltpu.VMEM((length, wide), WIDE)],
        cost_estimate=pl.CostEstimate(
            flops=pairs, bytes_accessed=seqs * length * wide, transcendentals=0
        ),
        compiler_params=pltpu.CompilerParams(vmem_limit_bytes=VMEM_LIMIT),
        name="attend_backward",
    )(triple, triple, triple, attended, grad, lse)


def turn_tables(positions, repeats, parts, wide, head):
    halfway = ROT // 2
    place = jnp.arange(parts * wide)
    entry = place % head
    turned = (place // wide < 2) & (entry < ROT)
    frequency = 10000.0 ** (-2.0 * (entry % halfway).astype(WIDE) / ROT)
    angles = positions.astype(WIDE)[:, None] * frequency[None, :]
    sine = jnp.where(turned, jnp.sin(angles), 0.0)
    cosine = jnp.where(turned, jnp.cos(angles), 1.0)
    later = jnp.where(entry < halfway, -sine, 0.0)
    earlier = jnp.where(entry < halfway, 0.0, sine)
    return tuple(jnp.tile(table, (1, repeats)) for table in (cosine, later, earlier))


def turn_packs(span, wide):
    return 1 if (3 * wide) % LANES == 0 else 2


def queries_kernel(seqs, wide, rows_ref, table_ref, bias_ref, cosine_ref, later_ref, earlier_ref, out_ref):
    halfway = ROT // 2
    columns = table_ref.shape[1]
    values = jnp.dot(rows_ref[...], table_ref[...], preferred_element_type=WIDE) + bias_ref[...]
    stretch = cosine_ref.shape[0]
    for s in range(seqs):
        part = values[s * stretch : (s + 1) * stretch]
        part = (
            part * cosine_ref[...]
            + pltpu.roll(part, columns - halfway, 1) * later_ref[...]
            + pltpu.roll(part, halfway, 1) * earlier_ref[...]
        ).astype(LOW)
        for j in range(columns // wide):
            out_ref[j // 3, j % 3, s] = part[:, j * wide : (j + 1) * wide]


def project_queries(rows, table, bias, tables, span, seqs, wide):
    total, width = rows.shape
    stretch = total // seqs
    packs = turn_packs(span, wide)
    columns = packs * 3 * wide
    fixed = pl.BlockSpec((stretch, columns), lambda g: (0, 0))
    return pl.pallas_call(
        partial(queries_kernel, seqs, wide),
        grid=(span // packs,),
        in_specs=[
            pl.BlockSpec((total, width), lambda g: (0, 0)),
            pl.BlockSpec((width, columns), lambda g: (0, g)),
            pl.BlockSpec((1, columns), lambda g: (0, g)),
            fixed,
            fixed,
            fixed,
        ],
        out_specs=pl.BlockSpec((packs, 3, seqs, stretch, wide), lambda g: (g, 0, 0, 0, 0)),
        out_shape=jax.ShapeDtypeStruct((span, 3, seqs, stretch, wide), LOW),
        cost_estimate=pl.CostEstimate(
            flops=2 * total * width * span * 3 * wide,
            bytes_accessed=2 * width * span * 3 * wide,
            transcendentals=0,
        ),
        compiler_params=pltpu.CompilerParams(vmem_limit_bytes=VMEM_LIMIT),
        name="project_queries",
    )(rows, table, bias, *tables)


def unturn_kernel(seqs, wide, triple_ref, cosine_ref, later_ref, earlier_ref, out_ref):
    halfway = ROT // 2
    columns = out_ref.shape[1]
    stretch = cosine_ref.shape[0]
    for s in range(seqs):
        part = jnp.concatenate(
            [triple_ref[j // 3, j % 3, s].astype(WIDE) for j in range(columns // wide)], axis=1
        )
        part = (
            part * cosine_ref[...]
            - pltpu.roll(part, columns - halfway, 1) * later_ref[...]
            - pltpu.roll(part, halfway, 1) * earlier_ref[...]
        )
        out_ref[s * stretch : (s + 1) * stretch, :] = part.astype(LOW)


def unturn(triple, tables):
    span, _, seqs, stretch, wide = triple.shape
    packs = turn_packs(span, wide)
    columns = packs * 3 * wide
    fixed = pl.BlockSpec((stretch, columns), lambda g: (0, 0))
    return pl.pallas_call(
        partial(unturn_kernel, seqs, wide),
        grid=(span // packs,),
        in_specs=[
            pl.BlockSpec((packs, 3, seqs, stretch, wide), lambda g: (g, 0, 0, 0, 0)),
            fixed,
            fixed,
            fixed,
        ],
        out_specs=pl.BlockSpec((seqs * stretch, columns), lambda g: (0, g)),
        out_shape=jax.ShapeDtypeStruct((seqs * stretch, span * 3 * wide), LOW),
        compiler_params=pltpu.CompilerParams(vmem_limit_bytes=VMEM_LIMIT),
        name="unturn",
    )(triple, *tables)


def gelu_exact(values):
    return jax.nn.gelu(values, approximate=False)


def standardize(values):
    average = jnp.mean(values, axis=-1, keepdims=True)
    centered = values - average
    variance = jnp.mean(centered * centered, axis=-1, keepdims=True)
    inverse = lax.rsqrt(variance + NORM_EPS)
    return centered * inverse, inverse


def standardize_pull(scaled, normal, inverse):
    return inverse * (
        scaled
        - jnp.mean(scaled, axis=-1, keepdims=True)
        - normal * jnp.mean(scaled * normal, axis=-1, keepdims=True)
    )


def adam_update(weight, first, second, grad, clip_factor, rate, decay):
    grad = grad * clip_factor
    first_new = BETA_ONE * first + (1.0 - BETA_ONE) * grad
    second_new = BETA_TWO * second + (1.0 - BETA_TWO) * grad * grad
    fix_one = 1.0 - BETA_ONE**STEP_COUNT
    fix_two = 1.0 - BETA_TWO**STEP_COUNT
    direction = first_new / fix_one / (jnp.sqrt(second_new / fix_two) + ADAM_EPS)
    return (weight - rate * (direction + decay * weight), first_new, second_new)


def summed_over(vector, axes):
    for axis in axes:
        vector = jnp.sum(lax.all_gather(vector, axis), axis=0)
    return vector


def turned_blocks(blocks, team, axis):
    teams = len(blocks)
    order = [blocks[(teams - 1 - m) % teams] for m in range(2 * teams - 1)]
    share = blocks[0].shape[axis]
    joined = jnp.concatenate(order, axis=axis)
    return lax.dynamic_slice_in_dim(joined, (teams - 1 - team) * share, teams * share, axis)


def team_rows(shard):
    teams = lax.axis_size("dp")
    blocks = [shard] + [moved(shard, "dp", k) for k in range(1, teams)]
    rows = turned_blocks(blocks, lax.axis_index("dp"), 0)
    return rows.reshape(teams, *shard.shape)


def gathered(rows):
    rows = lax.all_gather(rows, "sp", axis=1, tiled=True)
    return rows.reshape(-1, rows.shape[-1])


def scattered(gradient):
    dp, sp = lax.axis_size("dp"), lax.axis_size("sp")
    rows, columns = gradient.shape
    gradient = gradient.reshape(dp, sp, rows // (dp * sp), columns).transpose(1, 0, 2, 3)
    gradient = gradient.reshape(rows, columns)
    return lax.psum_scatter(gradient, "sp", scatter_dimension=0, tiled=True)


def joined_teams(gradient):
    return lax.psum_scatter(gradient, "dp", scatter_dimension=0, tiled=True)


def moved(array, axis, step):
    size = lax.axis_size(axis)
    return lax.ppermute(array, axis, [(i, (i + step) % size) for i in range(size)])


def turned(values, teams, team):
    share = values.shape[1] // teams
    blocks = [values[:, b * share : (b + 1) * share] for b in range(teams)]
    return turned_blocks(blocks, team, 1)


def local(
    token_ids,
    targets,
    stream_ids,
    embed_table,
    embed_first,
    embed_second,
    unembed,
    unembed_first,
    unembed_second,
    proj_in,
    proj_in_first,
    proj_in_second,
    proj_out,
    proj_out_first,
    proj_out_second,
    norm_params,
    norm_first,
    norm_second,
    biases,
    bias_first,
    bias_second,
):
    span = lax.axis_size("sp")
    teams = lax.axis_size("dp")
    sp_index = lax.axis_index("sp")
    dp_index = lax.axis_index("dp")
    seq_here, length = token_ids.shape
    stretch = length // span
    vocab_local = embed_table.shape[0]
    slab, in_columns = proj_in.shape
    width = proj_out.shape[1]
    triple_columns = 3 * width
    hidden_units = in_columns - triple_columns
    heads_here = HEADS // span
    head_dim = width // HEADS
    wide = heads_here * head_dim
    scale = head_dim ** (-0.5)
    tokens_here = seq_here * stretch
    offset = sp_index * vocab_local

    bias_rows = biases.shape[0] // slab
    norm_rows = norm_params.shape[0]
    shard_triple = proj_in[:, :triple_columns].astype(LOW)
    shard_triple = shard_triple.reshape(slab, span, heads_here, 3, head_dim).transpose(0, 1, 3, 2, 4)
    shard_triple = shard_triple.reshape(slab, triple_columns)
    extras = jnp.concatenate([norm_params.T, biases.reshape(slab, bias_rows)], axis=1).astype(LOW)
    extras = jnp.pad(extras, ((0, 0), (0, LANES - extras.shape[1])))
    shard_triple = jnp.concatenate([shard_triple, extras], axis=1)
    vocab_step = CHUNKS * LANES
    vocab_padded = -(-vocab_local // vocab_step) * vocab_step
    own_table = jnp.pad(unembed.T.astype(LOW), ((0, vocab_padded - vocab_local), (0, 0)))
    shard_up, shard_out = proj_in[:, triple_columns:].astype(LOW), proj_out.astype(LOW)
    token_ids, shard_triple = lax.optimization_barrier((token_ids, shard_triple))
    wide_triple = lax.all_gather(shard_triple, ("dp", "sp"), axis=0, tiled=True)
    half = vocab_padded // 2
    middle = teams // 2
    ids_all = lax.all_gather(token_ids, "dp")
    ids_all, own_table, shard_up, shard_out = lax.optimization_barrier(
        (ids_all, own_table, shard_up, shard_out)
    )
    quarter = vocab_padded // 4
    far_first = moved(own_table[:quarter], "dp", middle)
    rows_up, rows_out = team_rows(shard_up), team_rows(shard_out)
    ids_all = ids_all.reshape(teams, seq_here, span, stretch).transpose(2, 0, 1, 3).reshape(-1)
    local_ids = ids_all - offset
    in_slice = (local_ids >= 0) & (local_ids < vocab_local)
    safe_ids = jnp.clip(local_ids, 0, vocab_local - 1)
    picked = jnp.where(
        in_slice[:, None],
        embed_table.astype(LOW).at[safe_ids].get(mode="promise_in_bounds"),
        jnp.zeros((), LOW),
    )
    picked, wide_triple, far_first, own_table, rows_up, rows_out = lax.optimization_barrier(
        (picked, wide_triple, far_first, own_table, rows_up, rows_out)
    )
    tables = {k: moved(own_table, "dp", k) for k in range(1, middle)}
    hidden0 = lax.psum_scatter(picked, "sp", scatter_dimension=0, tiled=True)
    hidden0, tables, rows_up, rows_out = lax.optimization_barrier(
        (hidden0, tables, rows_up, rows_out)
    )
    wide_up = gathered(rows_up)
    wide_out = gathered(rows_out)
    hidden0 = lax.all_to_all(hidden0, "dp", split_axis=0, concat_axis=1, tiled=True)
    hidden0, later_table = lax.optimization_barrier((hidden0, own_table))
    hidden0 = hidden0.astype(WIDE)
    for k in range(middle + 1, teams):
        tables[k] = moved(later_table, "dp", k)
    norm_vals = wide_triple[:, triple_columns : triple_columns + norm_rows].astype(WIDE).T
    bias_vals = wide_triple[
        :, triple_columns + norm_rows : triple_columns + norm_rows + bias_rows
    ]
    bias_vals = bias_vals.astype(WIDE).reshape(-1)
    triple_bias = bias_vals[:triple_columns].reshape(span, heads_here, 3, head_dim)
    triple_bias = triple_bias.transpose(0, 2, 1, 3).reshape(1, triple_columns)

    normal0, inverse0 = standardize(hidden0)
    normed_one = (normal0 * norm_vals[0] + norm_vals[1]).astype(LOW)
    normed_two = (normal0 * norm_vals[2] + norm_vals[3]).astype(LOW)
    positions = sp_index * stretch + jnp.arange(stretch)
    angles = turn_tables(positions, turn_packs(span, wide), 3, wide, head_dim)
    packed = project_queries(normed_one, wide_triple, triple_bias, angles, span, seq_here, wide)
    triple = lax.all_to_all(packed, "sp", split_axis=0, concat_axis=0, tiled=True)
    triple, tables, later_table = lax.optimization_barrier((triple, tables, later_table))
    far_next = moved(later_table[quarter:half], "dp", middle)
    attended_heads, log_totals = attend_forward(triple, heads_here, ATTEND_ROWS, scale)
    attended = lax.all_to_all(attended_heads, "sp", split_axis=0, concat_axis=0, tiled=True)
    attended, far_next, later_table = lax.optimization_barrier((attended, far_next, later_table))
    far_last = moved(later_table[half:], "dp", middle)
    attended = attended.reshape(span, tokens_here, wide).transpose(1, 0, 2).reshape(tokens_here, width)
    up_values = (
        jnp.dot(normed_two, wide_up, preferred_element_type=WIDE)
        + bias_vals[triple_columns:in_columns]
    )
    act_f, pull_gelu = jax.vjp(gelu_exact, up_values)
    joined = jnp.concatenate([attended, act_f.astype(LOW)], axis=-1)
    hidden1 = (
        hidden0 + jnp.dot(joined, wide_out, preferred_element_type=WIDE) + bias_vals[in_columns:]
    )
    normal1, inverse1 = standardize(hidden1)
    final = (normal1 * norm_vals[4] + norm_vals[5]).astype(LOW)
    final = turned(final, teams, dp_index)
    rows_all = lax.all_gather(final.reshape(seq_here, stretch, width), "sp", axis=1, tiled=True)
    rows_all, far_last = lax.optimization_barrier((rows_all, far_last))
    tables[middle] = jnp.concatenate([far_first, far_next, far_last], axis=0)
    tables = [own_table] + [tables[k] for k in range(1, teams)]
    rows_all = rows_all.reshape(-1, width)
    grand = rows_all.shape[0]
    labels = targets.reshape(-1, 1) - offset
    powers, stats, lines = head_forward(rows_all, tables, labels, vocab_local)
    merged = lax.all_gather(lines[0:3], "sp")
    highest = jnp.max(merged[:, 0], axis=0)
    summed = jnp.sum(merged[:, 1] * jnp.exp(merged[:, 0] - highest), axis=0)
    log_sum = highest + jnp.log(summed)
    token_loss = (log_sum - jnp.sum(merged[:, 2], axis=0)).reshape(seq_here, length)
    weight_all = 1.0 + (REPLAY_WEIGHT - 1.0) * stream_ids.astype(WIDE)
    total_weight = jnp.sum(weight_all)
    seq_weight = lax.dynamic_slice_in_dim(weight_all, dp_index * seq_here, seq_here, 0)
    loss_local = jnp.sum(seq_weight * jnp.mean(token_loss, axis=1))
    token_scale = jnp.broadcast_to(
        (seq_weight / (total_weight * length))[:, None], (seq_here, length)
    ).reshape(-1)
    guide = jnp.concatenate(
        [log_sum[None], token_scale[None], jnp.zeros((6, grand), WIDE)], axis=0
    )
    slopes, grad_rows = head_backward(stats, guide, labels, powers, tables)
    final_grad = lax.psum_scatter(
        grad_rows.reshape(seq_here, length, width), "sp", scatter_dimension=1, tiled=True
    ).astype(WIDE)
    final_grad = final_grad.reshape(tokens_here, width)
    share = width // teams
    inner = rows_all[:, share : (middle + 1) * share]
    outer = jnp.concatenate([rows_all[:, :share], rows_all[:, (middle + 1) * share :]], axis=1)
    inner, outer = [
        lax.dot_general(
            slopes, side, (((0,), (0,)), ((), ())), preferred_element_type=WIDE
        ).astype(LOW)
        for side in (inner, outer)
    ]
    arrived = [
        moved(inner[:, (k - 1) * share : k * share], "dp", teams - k) for k in range(1, middle)
    ]
    far = inner[:, (middle - 1) * share :]
    far = [far[q * quarter : (q + 1) * quarter] for q in range(4)]
    far[0] = moved(far[0], "dp", middle)
    final_grad, inner, outer = lax.optimization_barrier((final_grad, inner, outer))
    final_grad = turned(final_grad, teams, dp_index)

    g_gain_final = jnp.sum(final_grad * normal1, axis=0)
    g_shift_final = jnp.sum(final_grad, axis=0)
    d_hidden1 = standardize_pull(final_grad * norm_vals[4], normal1, inverse1)
    d_branch = d_hidden1.astype(LOW)
    g_out = lax.dot_general(
        joined, d_branch, (((0,), (0,)), ((), ())), preferred_element_type=WIDE
    ).astype(LOW)
    g_bias_out = jnp.sum(d_branch.astype(WIDE), axis=0)
    contract_last = (((1,), (1,)), ((), ()))
    d_attended = lax.dot_general(
        d_branch, wide_out[:width], contract_last, preferred_element_type=WIDE
    ).astype(LOW)
    d_attended = d_attended.reshape(seq_here, stretch, span, wide).transpose(2, 0, 1, 3)
    d_heads = lax.all_to_all(d_attended, "sp", split_axis=0, concat_axis=0, tiled=True)
    d_act = lax.dot_general(d_branch, wide_out[width:], contract_last, preferred_element_type=WIDE)
    d_up = pull_gelu(d_act)[0].astype(LOW)
    g_up = lax.dot_general(
        normed_two, d_up, (((0,), (0,)), ((), ())), preferred_element_type=WIDE
    ).astype(LOW)
    d_normed_two = lax.dot_general(
        d_up, wide_up, contract_last, preferred_element_type=WIDE
    )
    d_heads, g_out, g_up, d_normed_two, arrived, far = lax.optimization_barrier(
        (d_heads, g_out, g_up, d_normed_two, arrived, far)
    )
    far[1] = moved(far[1], "dp", middle)
    r_out = scattered(g_out)
    r_up = scattered(g_up)
    d_triple = attend_backward(
        triple, attended_heads, d_heads, log_totals, heads_here, ATTEND_ROWS, scale
    )
    d_triple, far, outer = lax.optimization_barrier((d_triple, far, outer))
    far[2] = moved(far[2], "dp", middle)
    late = [
        (k, outer[:, (k - middle) * share : (k - middle + 1) * share])
        for k in range(middle + 1, teams)
    ]
    late_first = [moved(part[:half], "dp", teams - k) for k, part in late]
    d_triple = lax.all_to_all(d_triple, "sp", split_axis=0, concat_axis=0, tiled=True)
    d_joint = unturn(d_triple, angles)
    g_triple = lax.dot_general(
        normed_one, d_joint, (((0,), (0,)), ((), ())), preferred_element_type=WIDE
    ).astype(LOW)
    d_normed_one = lax.dot_general(
        d_joint, wide_triple[:, :triple_columns], contract_last, preferred_element_type=WIDE
    )
    late_rest = [part[half:] for k, part in late]
    d_normed_one, far, outer, late_first, late_rest = lax.optimization_barrier(
        (d_normed_one, far, outer, late_first, late_rest)
    )
    own_part = outer[:, :share]
    late_rest = [moved(late_rest[j], "dp", teams - late[j][0]) for j in range(len(late))]
    g_gain_one = jnp.sum(d_normed_one * normal0, axis=0)
    g_shift_one = jnp.sum(d_normed_one, axis=0)
    g_gain_two = jnp.sum(d_normed_two * normal0, axis=0)
    g_shift_two = jnp.sum(d_normed_two, axis=0)
    d_sum = d_normed_one * norm_vals[0] + d_normed_two * norm_vals[2]
    d_hidden0 = (d_hidden1 + standardize_pull(d_sum, normal0, inverse0)).astype(LOW)
    grad_all = lax.all_to_all(d_hidden0, "dp", split_axis=1, concat_axis=0, tiled=True)
    grad_all, r_out, r_up = lax.optimization_barrier((grad_all, r_out, r_up))
    grad_all = lax.all_gather(grad_all, "sp", axis=0, tiled=True)
    grad_all, late_rest, far, r_out, r_up = lax.optimization_barrier(
        (grad_all, late_rest, far, r_out, r_up)
    )
    far[3] = moved(far[3], "dp", middle)
    target_ids = jnp.where(in_slice, local_ids, vocab_local)
    g_bias_triple = jnp.sum(d_joint.astype(WIDE), axis=0).reshape(span, 3, heads_here, head_dim)
    g_bias = jnp.concatenate(
        [
            g_bias_triple.transpose(0, 2, 1, 3).reshape(-1),
            jnp.sum(d_up.astype(WIDE), axis=0),
            g_bias_out,
        ]
    )
    g_norm = jnp.stack(
        [g_gain_one, g_shift_one, g_gain_two, g_shift_two, g_gain_final, g_shift_final], axis=1
    )
    g_extra = jnp.concatenate([g_norm, g_bias.reshape(width, bias_rows)], axis=1).astype(LOW)
    g_extra = jnp.pad(g_extra, ((0, 0), (0, LANES - g_extra.shape[1])))
    r_triple = scattered(jnp.concatenate([g_triple, g_extra], axis=1))
    grad_all, r_triple = lax.optimization_barrier((grad_all, r_triple))
    r_embed = (
        jnp.zeros(embed_table.shape, WIDE).at[target_ids].add(grad_all.astype(WIDE), mode="drop")
    )
    r_triple, r_up, r_out = joined_teams(r_triple), joined_teams(r_up), joined_teams(r_out)
    r_embed, far, late_first, late_rest, arrived, own_part, r_triple, r_up, r_out = (
        lax.optimization_barrier(
            (r_embed, far, late_first, late_rest, arrived, own_part, r_triple, r_up, r_out)
        )
    )
    r_triple, r_up, r_out = r_triple.astype(WIDE), r_up.astype(WIDE), r_out.astype(WIDE)
    late = [jnp.concatenate(pair, axis=0) for pair in zip(late_first, late_rest)]
    r_unembed = [own_part, *arrived, *late, jnp.concatenate(far, axis=0)]
    r_norm = r_triple[:, triple_columns : triple_columns + norm_rows].T
    r_bias = r_triple[
        :, triple_columns + norm_rows : triple_columns + norm_rows + bias_rows
    ].reshape(-1)
    r_triple = r_triple[:, :triple_columns].reshape(slab, span, 3, heads_here, head_dim)
    r_triple = r_triple.transpose(0, 1, 3, 2, 4).reshape(slab, triple_columns)
    r_in = jnp.concatenate([r_triple, r_up], axis=1)
    r_unembed = sum(part[:vocab_local].astype(WIDE) for part in r_unembed).T

    reduced = (r_embed, r_unembed, r_in, r_out, r_norm, r_bias)
    squares = jnp.float32(0.0)
    for grad_piece in reduced:
        squares = squares + jnp.sum(grad_piece * grad_piece)
    loss_term = jnp.where(sp_index == 0, loss_local, 0.0)
    totals = summed_over(jnp.stack([squares, loss_term]), ("sp", "dp"))
    squares_total, loss_total = totals[0], totals[1]
    grad_norm = jnp.sqrt(squares_total)
    mean_loss = loss_total / total_weight
    clip_factor = jnp.minimum(1.0, CLIP_LEVEL / (grad_norm + 1e-06))
    masters = (embed_table, unembed, proj_in, proj_out, norm_params, biases)
    firsts = (embed_first, unembed_first, proj_in_first, proj_out_first, norm_first, bias_first)
    seconds = (
        embed_second,
        unembed_second,
        proj_in_second,
        proj_out_second,
        norm_second,
        bias_second,
    )
    rates = (1.0, 0.05, 0.05, 0.1, 0.5, 0.5)
    decays = (WEIGHT_DECAY, WEIGHT_DECAY, WEIGHT_DECAY, WEIGHT_DECAY, 0.0, 0.0)
    results = []
    for index in range(6):
        results.extend(
            adam_update(
                masters[index],
                firsts[index],
                seconds[index],
                reduced[index],
                clip_factor,
                rates[index],
                decays[index],
            )
        )
    return (
        mean_loss,
        grad_norm,
        results[0],
        results[1],
        results[2],
        results[3],
        results[4],
        results[5],
        results[6],
        results[7],
        results[8],
        results[9],
        results[10],
        results[11],
        results[12],
        results[13],
        results[14],
        results[15],
        results[16],
        results[17],
    )


def solution(mesh):
    in_specs = (
        P("dp", None),
        P("dp", None),
        P(),
        P("sp", "dp"),
        P("sp", "dp"),
        P("sp", "dp"),
        P("dp", "sp"),
        P("dp", "sp"),
        P("dp", "sp"),
        P(("dp", "sp"), None),
        P(("dp", "sp"), None),
        P(("dp", "sp"), None),
        P(("dp", "sp"), None),
        P(("dp", "sp"), None),
        P(("dp", "sp"), None),
        P(None, ("dp", "sp")),
        P(None, ("dp", "sp")),
        P(None, ("dp", "sp")),
        P(("dp", "sp")),
        P(("dp", "sp")),
        P(("dp", "sp")),
    )
    out_specs = (
        P(),
        P(),
        P("sp", "dp"),
        P("sp", "dp"),
        P("sp", "dp"),
        P("dp", "sp"),
        P("dp", "sp"),
        P("dp", "sp"),
        P(("dp", "sp"), None),
        P(("dp", "sp"), None),
        P(("dp", "sp"), None),
        P(("dp", "sp"), None),
        P(("dp", "sp"), None),
        P(("dp", "sp"), None),
        P(None, ("dp", "sp")),
        P(None, ("dp", "sp")),
        P(None, ("dp", "sp")),
        P(("dp", "sp")),
        P(("dp", "sp")),
        P(("dp", "sp")),
    )
    return jax.shard_map(local, mesh=mesh, in_specs=in_specs, out_specs=out_specs, check_vma=False)
```

```python
from functools import partial

import jax
import jax.numpy as jnp
from jax import lax
from jax.experimental import pallas as pl
from jax.experimental.pallas import tpu as pltpu
from jax.sharding import PartitionSpec as P

HEADS = 16
ROT = 16
STEP_COUNT = 10


NORM_EPS = 1e-05
BETA_ONE = 0.9
BETA_TWO = 0.95
ADAM_EPS = 1e-08
WEIGHT_DECAY = 0.01
CLIP_LEVEL = 0.01
REPLAY_WEIGHT = 4.0
NEGATIVE_FILL = -1e30
LOW = jnp.bfloat16
WIDE = jnp.float32
CHUNKS = 5
LANES = 128
HEAD_ROWS = 512
ATTEND_ROWS = 1024
VMEM_LIMIT = 60 * 1024 * 1024


def lane_of(shape):
    return lax.broadcasted_iota(jnp.int32, shape, 1)


def fetch_table(parts, table_ref, arrivals):
    @pl.when(pl.program_id(0) == 0)
    def _():
        share = table_ref.shape[1] // len(parts)
        copies = [
            pltpu.make_async_copy(
                parts[k], table_ref.at[:, k * share : (k + 1) * share], arrivals.at[k]
            )
            for k in range(len(parts))
        ]
        for copy in copies:
            copy.start()
        for copy in copies:
            copy.wait()


def head_forward_kernel(teams, real, rows_ref, label_ref, *refs):
    powers_ref, stats_ref, lines_ref, table_ref, arrivals = refs[teams:]
    fetch_table(refs[:teams], table_ref, arrivals)
    padded = table_ref.shape[0]
    part = padded // CHUNKS
    rows = rows_ref[...]
    count = rows.shape[0]
    label = label_ref[...]
    lane = lane_of((count, LANES))
    stats = jnp.zeros((count, LANES), WIDE)
    tops, sums = [], []
    chosen = jnp.zeros((count, 1), WIDE)
    for c in range(CHUNKS):
        logits = lax.dot_general(
            rows,
            table_ref[c * part : (c + 1) * part, :],
            (((1,), (1,)), ((), ())),
            preferred_element_type=WIDE,
        )
        column = lane_of(logits.shape) + c * part
        chosen = chosen + jnp.sum(jnp.where(column == label, logits, 0.0), axis=1, keepdims=True)
        if (c + 1) * part > real:
            logits = jnp.where(column < real, logits, NEGATIVE_FILL)
        top = jnp.max(logits, axis=1, keepdims=True)
        powers = jnp.exp(logits - top)
        sums.append(jnp.sum(powers, axis=1, keepdims=True))
        tops.append(top)
        powers_ref[:, c * part : (c + 1) * part] = powers.astype(LOW)
        stats = jnp.where(lane == 8 + c, top, stats)
    highest = tops[0]
    for c in range(1, CHUNKS):
        highest = jnp.maximum(highest, tops[c])
    total = jnp.zeros((count, 1), WIDE)
    for c in range(CHUNKS):
        total = total + sums[c] * jnp.exp(tops[c] - highest)
    stats = jnp.where(lane == 0, highest, stats)
    stats = jnp.where(lane == 1, total, stats)
    stats = jnp.where(lane == 2, chosen, stats)
    stats_ref[...] = stats
    lines_ref[...] = jnp.transpose(stats)[0:8, :]


def head_forward(rows, tables, label, real):
    total, width = rows.shape
    padded = tables[0].shape[0]
    teams = len(tables)
    count = min(HEAD_ROWS, total)
    return pl.pallas_call(
        partial(head_forward_kernel, teams, real),
        grid=(total // count,),
        in_specs=[
            pl.BlockSpec((count, width), lambda i: (i, 0)),
            pl.BlockSpec((count, 1), lambda i: (i, 0)),
        ]
        + [pl.BlockSpec(memory_space=pl.ANY)] * teams,
        out_specs=[
            pl.BlockSpec((count, padded), lambda i: (i, 0)),
            pl.BlockSpec((count, LANES), lambda i: (i, 0)),
            pl.BlockSpec((8, count), lambda i: (0, i)),
        ],
        out_shape=[
            jax.ShapeDtypeStruct((total, padded), LOW),
            jax.ShapeDtypeStruct((total, LANES), WIDE),
            jax.ShapeDtypeStruct((8, total), WIDE),
        ],
        scratch_shapes=[pltpu.VMEM((padded, width), LOW), pltpu.SemaphoreType.DMA((teams,))],
        cost_estimate=pl.CostEstimate(
            flops=2 * total * width * padded,
            bytes_accessed=2 * (total * (width + padded) + width * padded),
            transcendentals=total * padded,
        ),
        compiler_params=pltpu.CompilerParams(vmem_limit_bytes=VMEM_LIMIT),
        name="head_forward",
    )(rows, label, *tables)


def head_backward_kernel(teams, stats_ref, lines_ref, label_ref, powers_ref, *refs):
    slope_ref, grad_ref, table_ref, arrivals = refs[teams:]
    fetch_table(refs[:teams], table_ref, arrivals)
    padded = table_ref.shape[0]
    part = padded // CHUNKS
    stats = stats_ref[...]
    label = label_ref[...]
    lines = lines_ref[...]
    lines = jnp.transpose(jnp.concatenate([lines] * (LANES // 8), axis=0))
    lse = lines[:, 0:1]
    scale = lines[:, 1:2]
    total = None
    for c in range(CHUNKS):
        ratio = scale * jnp.exp(stats[:, 8 + c : 9 + c] - lse)
        slope = powers_ref[:, c * part : (c + 1) * part].astype(WIDE) * ratio
        column = lane_of(slope.shape) + c * part
        slope = jnp.where(column == label, slope - scale, slope).astype(LOW)
        slope_ref[:, c * part : (c + 1) * part] = slope
        piece = jnp.dot(
            slope, table_ref[c * part : (c + 1) * part, :], preferred_element_type=WIDE
        )
        total = piece if total is None else total + piece
    grad_ref[...] = total.astype(LOW)


def head_backward(stats, lines, label, powers, tables):
    total, padded = powers.shape
    teams = len(tables)
    width = teams * tables[0].shape[1]
    count = min(HEAD_ROWS, total)
    return pl.pallas_call(
        partial(head_backward_kernel, teams),
        grid=(total // count,),
        in_specs=[
            pl.BlockSpec((count, LANES), lambda i: (i, 0)),
            pl.BlockSpec((8, count), lambda i: (0, i)),
            pl.BlockSpec((count, 1), lambda i: (i, 0)),
            pl.BlockSpec((count, padded), lambda i: (i, 0)),
        ]
        + [pl.BlockSpec(memory_space=pl.ANY)] * teams,
        out_specs=[
            pl.BlockSpec((count, padded), lambda i: (i, 0)),
            pl.BlockSpec((count, width), lambda i: (i, 0)),
        ],
        out_shape=[
            jax.ShapeDtypeStruct((total, padded), LOW),
            jax.ShapeDtypeStruct((total, width), LOW),
        ],
        scratch_shapes=[pltpu.VMEM((padded, width), LOW), pltpu.SemaphoreType.DMA((teams,))],
        cost_estimate=pl.CostEstimate(
            flops=2 * total * width * padded,
            bytes_accessed=2 * (total * (width + 2 * padded) + width * padded),
            transcendentals=0,
        ),
        compiler_params=pltpu.CompilerParams(vmem_limit_bytes=VMEM_LIMIT),
        name="head_backward",
    )(stats, lines, label, powers, *tables)


def attend_forward_kernel(heads, scale, query_ref, key_ref, value_ref, out_ref, lse_ref):
    pieces, stretch, wide = query_ref.shape
    block = pieces * stretch
    head = wide // heads
    index = pl.program_id(1)
    query = query_ref[...].reshape(block, wide) * jnp.asarray(scale, LOW)
    lane = lane_of((block, wide))
    mine = [(lane >= h * head) & (lane < (h + 1) * head) for h in range(heads)]
    own = [jnp.where(mine[h], query, jnp.zeros_like(query)) for h in range(heads)]

    def step(c, state, masked):
        spots = pl.ds(c * pieces, pieces)
        keys = key_ref[spots].reshape(block, wide)
        values = value_ref[spots].reshape(block, wide)
        fresh = []
        for h in range(heads):
            top, total, summed = state[h]
            scores = lax.dot_general(
                own[h], keys, (((1,), (1,)), ((), ())), preferred_element_type=WIDE
            )
            if masked:
                here = lax.broadcasted_iota(jnp.int32, scores.shape, 0)
                scores = jnp.where(here >= lane_of(scores.shape), scores, NEGATIVE_FILL)
            higher = jnp.maximum(top, jnp.max(scores, axis=1, keepdims=True))
            powers = jnp.exp(scores - higher)
            shrink = jnp.exp(top - higher)
            total = total * shrink + jnp.sum(powers, axis=1, keepdims=True)
            summed = summed * shrink + jnp.dot(
                powers.astype(LOW), values, preferred_element_type=WIDE
            )
            fresh.append((higher, total, summed))
        return tuple(fresh)

    state = tuple(
        (
            jnp.full((block, 1), NEGATIVE_FILL, WIDE),
            jnp.zeros((block, 1), WIDE),
            jnp.zeros((block, wide), WIDE),
        )
        for _ in range(heads)
    )
    state = lax.fori_loop(0, index, lambda c, s: step(c, s, False), state)
    state = step(index, state, True)
    result = None
    spot = lane_of((block, LANES))
    logs = jnp.zeros((block, LANES), WIDE)
    for h in range(heads):
        top, total, summed = state[h]
        piece = summed / total
        result = piece if result is None else jnp.where(mine[h], piece, result)
        logs = jnp.where(spot == h, top + jnp.log(total), logs)
    out_ref[...] = result.astype(LOW).reshape(pieces, stretch, wide)
    lse_ref[...] = jnp.transpose(logs)[0:8, :]


def attend_specs(triple, block):
    span, _, seqs, stretch, wide = triple.shape
    pieces = min(block, span * stretch) // stretch
    part = pl.BlockSpec((pieces, None, stretch, wide), lambda s, i: (i, s, 0, 0))
    query = pl.BlockSpec((pieces, None, None, stretch, wide), lambda s, i: (i, 0, s, 0, 0))
    keys = pl.BlockSpec((span, None, None, stretch, wide), lambda s, i: (0, 1, s, 0, 0))
    values = pl.BlockSpec((span, None, None, stretch, wide), lambda s, i: (0, 2, s, 0, 0))
    logs = pl.BlockSpec((None, 8, pieces * stretch), lambda s, i: (s, 0, i))
    return (seqs, span // pieces), part, query, keys, values, logs


def attend_forward(triple, heads, block, scale):
    span, _, seqs, stretch, wide = triple.shape
    length = span * stretch
    grid, part, query, keys, values, logs = attend_specs(triple, block)
    pairs = seqs * heads * length * length // 2
    return pl.pallas_call(
        partial(attend_forward_kernel, heads, scale),
        grid=grid,
        in_specs=[query, keys, values],
        out_specs=[part, logs],
        out_shape=[
            jax.ShapeDtypeStruct((span, seqs, stretch, wide), LOW),
            jax.ShapeDtypeStruct((seqs, 8, length), WIDE),
        ],
        cost_estimate=pl.CostEstimate(
            flops=pairs, bytes_accessed=seqs * length * wide, transcendentals=0
        ),
        compiler_params=pltpu.CompilerParams(vmem_limit_bytes=VMEM_LIMIT),
        name="attend_forward",
    )(triple, triple, triple)


def attend_backward_kernel(
    heads, scale, query_ref, key_ref, value_ref, out_ref, grad_ref, lse_ref, triple_ref, dk_sum, dv_sum
):
    pieces, stretch, wide = query_ref.shape
    block = pieces * stretch
    span = key_ref.shape[0]
    head = wide // heads
    index = pl.program_id(1)

    @pl.when(index == 0)
    def _():
        dk_sum[...] = jnp.zeros_like(dk_sum)
        dv_sum[...] = jnp.zeros_like(dv_sum)

    query = query_ref[...].reshape(block, wide) * jnp.asarray(scale, LOW)
    grad = grad_ref[...].reshape(block, wide)
    lane = lane_of((block, wide))
    mine = [(lane >= h * head) & (lane < (h + 1) * head) for h in range(heads)]
    zero = jnp.zeros_like(query)
    own_query = [jnp.where(mine[h], query, zero) for h in range(heads)]
    own_grad = [jnp.where(mine[h], grad, zero) for h in range(heads)]
    product = out_ref[...].reshape(block, wide).astype(WIDE) * grad.astype(WIDE)
    spot = lane_of((block, LANES))
    centres = jnp.zeros((block, LANES), WIDE)
    for h in range(heads):
        centre = jnp.sum(jnp.where(mine[h], product, 0.0), axis=1, keepdims=True)
        centres = jnp.where(spot == h, centre, centres)
    centres = jnp.transpose(centres)
    logs = lse_ref[...]

    def step(c, state, masked):
        spots = pl.ds(c * pieces, pieces)
        rows = pl.ds(pl.multiple_of(c * block, block), block)
        keys = key_ref[spots].reshape(block, wide)
        values = value_ref[spots].reshape(block, wide)
        fresh = []
        key_part, value_part = None, None
        for h in range(heads):
            scores = lax.dot_general(
                keys, own_query[h], (((1,), (1,)), ((), ())), preferred_element_type=WIDE
            )
            probs = jnp.exp(scores - logs[h : h + 1, :])
            if masked:
                here = lax.broadcasted_iota(jnp.int32, scores.shape, 0)
                probs = jnp.where(here <= lane_of(scores.shape), probs, 0.0)
            grad_probs = lax.dot_general(
                values, own_grad[h], (((1,), (1,)), ((), ())), preferred_element_type=WIDE
            )
            slope = (probs * (grad_probs - centres[h : h + 1, :])).astype(LOW)
            a = jnp.dot(slope, own_query[h], preferred_element_type=WIDE)
            b = jnp.dot(probs.astype(LOW), own_grad[h], preferred_element_type=WIDE)
            key_part = a if key_part is None else key_part + a
            value_part = b if value_part is None else value_part + b
            fresh.append(
                state[h]
                + lax.dot_general(slope, keys, (((0,), (0,)), ((), ())), preferred_element_type=WIDE)
            )
        dk_sum[rows, :] += key_part
        dv_sum[rows, :] += value_part
        return tuple(fresh)

    state = tuple(jnp.zeros((block, wide), WIDE) for _ in range(heads))
    state = lax.fori_loop(0, index, lambda c, s: step(c, s, False), state)
    state = step(index, state, True)
    result = state[0]
    for h in range(1, heads):
        result = jnp.where(mine[h], state[h], result)
    triple_ref[pl.ds(index * pieces, pieces), 0] = (
        (result * scale).astype(LOW).reshape(pieces, stretch, wide)
    )

    @pl.when(index == pl.num_programs(1) - 1)
    def _():
        triple_ref[:, 1] = dk_sum[...].astype(LOW).reshape(span, stretch, wide)
        triple_ref[:, 2] = dv_sum[...].astype(LOW).reshape(span, stretch, wide)


def attend_backward(triple, attended, grad, lse, heads, block, scale):
    span, _, seqs, stretch, wide = triple.shape
    length = span * stretch
    grid, part, query, keys, values, logs = attend_specs(triple, block)
    pairs = seqs * heads * length * length // 2
    return pl.pallas_call(
        partial(attend_backward_kernel, heads, scale),
        grid=grid,
        in_specs=[query, keys, values, part, part, logs],
        out_specs=pl.BlockSpec((span, 3, None, stretch, wide), lambda s, i: (0, 0, s, 0, 0)),
        out_shape=jax.ShapeDtypeStruct((span, 3, seqs, stretch, wide), LOW),
        scratch_shapes=[pltpu.VMEM((length, wide), WIDE), pltpu.VMEM((length, wide), WIDE)],
        cost_estimate=pl.CostEstimate(
            flops=pairs, bytes_accessed=seqs * length * wide, transcendentals=0
        ),
        compiler_params=pltpu.CompilerParams(vmem_limit_bytes=VMEM_LIMIT),
        name="attend_backward",
    )(triple, triple, triple, attended, grad, lse)


def turn_tables(positions, repeats, parts, wide, head):
    halfway = ROT // 2
    place = jnp.arange(parts * wide)
    entry = place % head
    turned = (place // wide < 2) & (entry < ROT)
    frequency = 10000.0 ** (-2.0 * (entry % halfway).astype(WIDE) / ROT)
    angles = positions.astype(WIDE)[:, None] * frequency[None, :]
    sine = jnp.where(turned, jnp.sin(angles), 0.0)
    cosine = jnp.where(turned, jnp.cos(angles), 1.0)
    later = jnp.where(entry < halfway, -sine, 0.0)
    earlier = jnp.where(entry < halfway, 0.0, sine)
    return tuple(jnp.tile(table, (1, repeats)) for table in (cosine, later, earlier))


def turn_packs(span, wide):
    return 1 if (3 * wide) % LANES == 0 else 2


def queries_kernel(seqs, wide, rows_ref, table_ref, bias_ref, cosine_ref, later_ref, earlier_ref, out_ref):
    halfway = ROT // 2
    columns = table_ref.shape[1]
    values = jnp.dot(rows_ref[...], table_ref[...], preferred_element_type=WIDE) + bias_ref[...]
    stretch = cosine_ref.shape[0]
    for s in range(seqs):
        part = values[s * stretch : (s + 1) * stretch]
        part = (
            part * cosine_ref[...]
            + pltpu.roll(part, columns - halfway, 1) * later_ref[...]
            + pltpu.roll(part, halfway, 1) * earlier_ref[...]
        ).astype(LOW)
        for j in range(columns // wide):
            out_ref[j // 3, j % 3, s] = part[:, j * wide : (j + 1) * wide]


def project_queries(rows, table, bias, tables, span, seqs, wide):
    total, width = rows.shape
    stretch = total // seqs
    packs = turn_packs(span, wide)
    columns = packs * 3 * wide
    fixed = pl.BlockSpec((stretch, columns), lambda g: (0, 0))
    return pl.pallas_call(
        partial(queries_kernel, seqs, wide),
        grid=(span // packs,),
        in_specs=[
            pl.BlockSpec((total, width), lambda g: (0, 0)),
            pl.BlockSpec((width, columns), lambda g: (0, g)),
            pl.BlockSpec((1, columns), lambda g: (0, g)),
            fixed,
            fixed,
            fixed,
        ],
        out_specs=pl.BlockSpec((packs, 3, seqs, stretch, wide), lambda g: (g, 0, 0, 0, 0)),
        out_shape=jax.ShapeDtypeStruct((span, 3, seqs, stretch, wide), LOW),
        cost_estimate=pl.CostEstimate(
            flops=2 * total * width * span * 3 * wide,
            bytes_accessed=2 * width * span * 3 * wide,
            transcendentals=0,
        ),
        compiler_params=pltpu.CompilerParams(vmem_limit_bytes=VMEM_LIMIT),
        name="project_queries",
    )(rows, table, bias, *tables)


def unturn_kernel(seqs, wide, triple_ref, cosine_ref, later_ref, earlier_ref, out_ref):
    halfway = ROT // 2
    columns = out_ref.shape[1]
    stretch = cosine_ref.shape[0]
    for s in range(seqs):
        part = jnp.concatenate(
            [triple_ref[j // 3, j % 3, s].astype(WIDE) for j in range(columns // wide)], axis=1
        )
        part = (
            part * cosine_ref[...]
            - pltpu.roll(part, columns - halfway, 1) * later_ref[...]
            - pltpu.roll(part, halfway, 1) * earlier_ref[...]
        )
        out_ref[s * stretch : (s + 1) * stretch, :] = part.astype(LOW)


def unturn(triple, tables):
    span, _, seqs, stretch, wide = triple.shape
    packs = turn_packs(span, wide)
    columns = packs * 3 * wide
    fixed = pl.BlockSpec((stretch, columns), lambda g: (0, 0))
    return pl.pallas_call(
        partial(unturn_kernel, seqs, wide),
        grid=(span // packs,),
        in_specs=[
            pl.BlockSpec((packs, 3, seqs, stretch, wide), lambda g: (g, 0, 0, 0, 0)),
            fixed,
            fixed,
            fixed,
        ],
        out_specs=pl.BlockSpec((seqs * stretch, columns), lambda g: (0, g)),
        out_shape=jax.ShapeDtypeStruct((seqs * stretch, span * 3 * wide), LOW),
        compiler_params=pltpu.CompilerParams(vmem_limit_bytes=VMEM_LIMIT),
        name="unturn",
    )(triple, *tables)


def gelu_exact(values):
    return jax.nn.gelu(values, approximate=False)


def standardize(values):
    average = jnp.mean(values, axis=-1, keepdims=True)
    centered = values - average
    variance = jnp.mean(centered * centered, axis=-1, keepdims=True)
    inverse = lax.rsqrt(variance + NORM_EPS)
    return centered * inverse, inverse


def standardize_pull(scaled, normal, inverse):
    return inverse * (
        scaled
        - jnp.mean(scaled, axis=-1, keepdims=True)
        - normal * jnp.mean(scaled * normal, axis=-1, keepdims=True)
    )


def adam_update(weight, first, second, grad, clip_factor, rate, decay):
    grad = grad * clip_factor
    first_new = BETA_ONE * first + (1.0 - BETA_ONE) * grad
    second_new = BETA_TWO * second + (1.0 - BETA_TWO) * grad * grad
    fix_one = 1.0 - BETA_ONE**STEP_COUNT
    fix_two = 1.0 - BETA_TWO**STEP_COUNT
    direction = first_new / fix_one / (jnp.sqrt(second_new / fix_two) + ADAM_EPS)
    return (weight - rate * (direction + decay * weight), first_new, second_new)


def summed_over(vector, axes):
    for axis in axes:
        vector = jnp.sum(lax.all_gather(vector, axis), axis=0)
    return vector


def turned_blocks(blocks, team, axis):
    teams = len(blocks)
    order = [blocks[(teams - 1 - m) % teams] for m in range(2 * teams - 1)]
    share = blocks[0].shape[axis]
    joined = jnp.concatenate(order, axis=axis)
    return lax.dynamic_slice_in_dim(joined, (teams - 1 - team) * share, teams * share, axis)


def team_rows(shard):
    teams = lax.axis_size("dp")
    blocks = [shard] + [moved(shard, "dp", k) for k in range(1, teams)]
    rows = turned_blocks(blocks, lax.axis_index("dp"), 0)
    return rows.reshape(teams, *shard.shape)


def gathered(rows):
    rows = lax.all_gather(rows, "sp", axis=1, tiled=True)
    return rows.reshape(-1, rows.shape[-1])


def scattered(gradient):
    dp, sp = lax.axis_size("dp"), lax.axis_size("sp")
    rows, columns = gradient.shape
    gradient = gradient.reshape(dp, sp, rows // (dp * sp), columns).transpose(1, 0, 2, 3)
    gradient = gradient.reshape(rows, columns)
    return lax.psum_scatter(gradient, "sp", scatter_dimension=0, tiled=True)


def joined_teams(gradient):
    return lax.psum_scatter(gradient, "dp", scatter_dimension=0, tiled=True)


def moved(array, axis, step):
    size = lax.axis_size(axis)
    return lax.ppermute(array, axis, [(i, (i + step) % size) for i in range(size)])


def turned(values, teams, team):
    share = values.shape[1] // teams
    blocks = [values[:, b * share : (b + 1) * share] for b in range(teams)]
    return turned_blocks(blocks, team, 1)


def local(
    token_ids,
    targets,
    stream_ids,
    embed_table,
    embed_first,
    embed_second,
    unembed,
    unembed_first,
    unembed_second,
    proj_in,
    proj_in_first,
    proj_in_second,
    proj_out,
    proj_out_first,
    proj_out_second,
    norm_params,
    norm_first,
    norm_second,
    biases,
    bias_first,
    bias_second,
):
    span = lax.axis_size("sp")
    teams = lax.axis_size("dp")
    sp_index = lax.axis_index("sp")
    dp_index = lax.axis_index("dp")
    seq_here, length = token_ids.shape
    stretch = length // span
    vocab_local = embed_table.shape[0]
    slab, in_columns = proj_in.shape
    width = proj_out.shape[1]
    triple_columns = 3 * width
    hidden_units = in_columns - triple_columns
    heads_here = HEADS // span
    head_dim = width // HEADS
    wide = heads_here * head_dim
    scale = head_dim ** (-0.5)
    tokens_here = seq_here * stretch
    offset = sp_index * vocab_local

    bias_rows = biases.shape[0] // slab
    norm_rows = norm_params.shape[0]
    shard_triple = proj_in[:, :triple_columns].astype(LOW)
    shard_triple = shard_triple.reshape(slab, span, heads_here, 3, head_dim).transpose(0, 1, 3, 2, 4)
    shard_triple = shard_triple.reshape(slab, triple_columns)
    extras = jnp.concatenate([norm_params.T, biases.reshape(slab, bias_rows)], axis=1).astype(LOW)
    extras = jnp.pad(extras, ((0, 0), (0, LANES - extras.shape[1])))
    shard_triple = jnp.concatenate([shard_triple, extras], axis=1)
    vocab_step = CHUNKS * LANES
    vocab_padded = -(-vocab_local // vocab_step) * vocab_step
    own_table = jnp.pad(unembed.T.astype(LOW), ((0, vocab_padded - vocab_local), (0, 0)))
    shard_up, shard_out = proj_in[:, triple_columns:].astype(LOW), proj_out.astype(LOW)
    token_ids, shard_triple = lax.optimization_barrier((token_ids, shard_triple))
    wide_triple = lax.all_gather(shard_triple, ("dp", "sp"), axis=0, tiled=True)
    half = vocab_padded // 2
    middle = teams // 2
    ids_all = lax.all_gather(token_ids, "dp")
    ids_all, own_table, shard_up, shard_out = lax.optimization_barrier(
        (ids_all, own_table, shard_up, shard_out)
    )
    quarter = vocab_padded // 4
    far_first = moved(own_table[:quarter], "dp", middle)
    rows_up, rows_out = team_rows(shard_up), team_rows(shard_out)
    ids_all = ids_all.reshape(teams, seq_here, span, stretch).transpose(2, 0, 1, 3).reshape(-1)
    local_ids = ids_all - offset
    in_slice = (local_ids >= 0) & (local_ids < vocab_local)
    safe_ids = jnp.clip(local_ids, 0, vocab_local - 1)
    picked = jnp.where(
        in_slice[:, None],
        embed_table.astype(LOW).at[safe_ids].get(mode="promise_in_bounds"),
        jnp.zeros((), LOW),
    )
    picked, wide_triple, far_first, own_table, rows_up, rows_out = lax.optimization_barrier(
        (picked, wide_triple, far_first, own_table, rows_up, rows_out)
    )
    tables = {k: moved(own_table, "dp", k) for k in range(1, middle)}
    hidden0 = lax.psum_scatter(picked, "sp", scatter_dimension=0, tiled=True)
    hidden0, tables, rows_up, rows_out = lax.optimization_barrier(
        (hidden0, tables, rows_up, rows_out)
    )
    wide_up = gathered(rows_up)
    wide_out = gathered(rows_out)
    hidden0 = lax.all_to_all(hidden0, "dp", split_axis=0, concat_axis=1, tiled=True)
    hidden0, later_table = lax.optimization_barrier((hidden0, own_table))
    hidden0 = hidden0.astype(WIDE)
    for k in range(middle + 1, teams):
        tables[k] = moved(later_table, "dp", k)
    norm_vals = wide_triple[:, triple_columns : triple_columns + norm_rows].astype(WIDE).T
    bias_vals = wide_triple[
        :, triple_columns + norm_rows : triple_columns + norm_rows + bias_rows
    ]
    bias_vals = bias_vals.astype(WIDE).reshape(-1)
    triple_bias = bias_vals[:triple_columns].reshape(span, heads_here, 3, head_dim)
    triple_bias = triple_bias.transpose(0, 2, 1, 3).reshape(1, triple_columns)

    normal0, inverse0 = standardize(hidden0)
    normed_one = (normal0 * norm_vals[0] + norm_vals[1]).astype(LOW)
    normed_two = (normal0 * norm_vals[2] + norm_vals[3]).astype(LOW)
    positions = sp_index * stretch + jnp.arange(stretch)
    angles = turn_tables(positions, turn_packs(span, wide), 3, wide, head_dim)
    packed = project_queries(normed_one, wide_triple, triple_bias, angles, span, seq_here, wide)
    triple = lax.all_to_all(packed, "sp", split_axis=0, concat_axis=0, tiled=True)
    triple, tables, later_table = lax.optimization_barrier((triple, tables, later_table))
    far_next = moved(later_table[quarter:half], "dp", middle)
    attended_heads, log_totals = attend_forward(triple, heads_here, ATTEND_ROWS, scale)
    attended = lax.all_to_all(attended_heads, "sp", split_axis=0, concat_axis=0, tiled=True)
    attended = attended.reshape(span, tokens_here, wide).transpose(1, 0, 2).reshape(tokens_here, width)
    up_values = (
        jnp.dot(normed_two, wide_up, preferred_element_type=WIDE)
        + bias_vals[triple_columns:in_columns]
    )
    act_f, pull_gelu = jax.vjp(gelu_exact, up_values)
    act, far_next, later_table = lax.optimization_barrier((act_f.astype(LOW), far_next, later_table))
    far_third = moved(later_table[half : half + quarter], "dp", middle)
    joined = jnp.concatenate([attended, act], axis=-1)
    hidden1 = (
        hidden0 + jnp.dot(joined, wide_out, preferred_element_type=WIDE) + bias_vals[in_columns:]
    )
    normal1, inverse1 = standardize(hidden1)
    final = (normal1 * norm_vals[4] + norm_vals[5]).astype(LOW)
    final = turned(final, teams, dp_index)
    final, far_third, later_table = lax.optimization_barrier((final, far_third, later_table))
    far_last = moved(later_table[half + quarter :], "dp", middle)
    rows_all = lax.all_gather(final.reshape(seq_here, stretch, width), "sp", axis=1, tiled=True)
    rows_all, far_last = lax.optimization_barrier((rows_all, far_last))
    tables[middle] = jnp.concatenate([far_first, far_next, far_third, far_last], axis=0)
    tables = [own_table] + [tables[k] for k in range(1, teams)]
    rows_all = rows_all.reshape(-1, width)
    grand = rows_all.shape[0]
    labels = targets.reshape(-1, 1) - offset
    powers, stats, lines = head_forward(rows_all, tables, labels, vocab_local)
    merged = lax.all_gather(lines[0:3], "sp")
    highest = jnp.max(merged[:, 0], axis=0)
    summed = jnp.sum(merged[:, 1] * jnp.exp(merged[:, 0] - highest), axis=0)
    log_sum = highest + jnp.log(summed)
    token_loss = (log_sum - jnp.sum(merged[:, 2], axis=0)).reshape(seq_here, length)
    weight_all = 1.0 + (REPLAY_WEIGHT - 1.0) * stream_ids.astype(WIDE)
    total_weight = jnp.sum(weight_all)
    seq_weight = lax.dynamic_slice_in_dim(weight_all, dp_index * seq_here, seq_here, 0)
    loss_local = jnp.sum(seq_weight * jnp.mean(token_loss, axis=1))
    token_scale = jnp.broadcast_to(
        (seq_weight / (total_weight * length))[:, None], (seq_here, length)
    ).reshape(-1)
    guide = jnp.concatenate(
        [log_sum[None], token_scale[None], jnp.zeros((6, grand), WIDE)], axis=0
    )
    slopes, grad_rows = head_backward(stats, guide, labels, powers, tables)
    final_grad = lax.psum_scatter(
        grad_rows.reshape(seq_here, length, width), "sp", scatter_dimension=1, tiled=True
    ).astype(WIDE)
    final_grad = final_grad.reshape(tokens_here, width)
    share = width // teams
    inner = rows_all[:, share : (middle + 1) * share]
    outer = jnp.concatenate([rows_all[:, :share], rows_all[:, (middle + 1) * share :]], axis=1)
    inner, outer = [
        lax.dot_general(
            slopes, side, (((0,), (0,)), ((), ())), preferred_element_type=WIDE
        ).astype(LOW)
        for side in (inner, outer)
    ]
    arrived = [
        moved(inner[:, (k - 1) * share : k * share], "dp", teams - k) for k in range(1, middle)
    ]
    far = inner[:, (middle - 1) * share :]
    far = [far[q * quarter : (q + 1) * quarter] for q in range(4)]
    final_grad, inner, outer = lax.optimization_barrier((final_grad, inner, outer))
    final_grad = turned(final_grad, teams, dp_index)

    g_gain_final = jnp.sum(final_grad * normal1, axis=0)
    g_shift_final = jnp.sum(final_grad, axis=0)
    d_hidden1 = standardize_pull(final_grad * norm_vals[4], normal1, inverse1)
    d_branch = d_hidden1.astype(LOW)
    g_out = lax.dot_general(
        joined, d_branch, (((0,), (0,)), ((), ())), preferred_element_type=WIDE
    ).astype(LOW)
    g_bias_out = jnp.sum(d_branch.astype(WIDE), axis=0)
    contract_last = (((1,), (1,)), ((), ()))
    d_attended = lax.dot_general(
        d_branch, wide_out[:width], contract_last, preferred_element_type=WIDE
    ).astype(LOW)
    d_attended = d_attended.reshape(seq_here, stretch, span, wide).transpose(2, 0, 1, 3)
    d_heads = lax.all_to_all(d_attended, "sp", split_axis=0, concat_axis=0, tiled=True)
    d_act = lax.dot_general(d_branch, wide_out[width:], contract_last, preferred_element_type=WIDE)
    d_up = pull_gelu(d_act)[0].astype(LOW)
    g_up = lax.dot_general(
        normed_two, d_up, (((0,), (0,)), ((), ())), preferred_element_type=WIDE
    ).astype(LOW)
    d_normed_two = lax.dot_general(
        d_up, wide_up, contract_last, preferred_element_type=WIDE
    )
    d_heads, g_out, g_up, d_normed_two, arrived, far = lax.optimization_barrier(
        (d_heads, g_out, g_up, d_normed_two, arrived, far)
    )
    far[1] = moved(far[1], "dp", middle)
    r_out = scattered(g_out)
    r_up = scattered(g_up)
    d_triple = attend_backward(
        triple, attended_heads, d_heads, log_totals, heads_here, ATTEND_ROWS, scale
    )
    d_triple, far, outer = lax.optimization_barrier((d_triple, far, outer))
    far[0] = moved(far[0], "dp", middle)
    late = [
        (k, outer[:, (k - middle) * share : (k - middle + 1) * share])
        for k in range(middle + 1, teams)
    ]
    d_triple = lax.all_to_all(d_triple, "sp", split_axis=0, concat_axis=0, tiled=True)
    d_joint = unturn(d_triple, angles)
    g_triple = lax.dot_general(
        normed_one, d_joint, (((0,), (0,)), ((), ())), preferred_element_type=WIDE
    ).astype(LOW)
    d_normed_one = lax.dot_general(
        d_joint, wide_triple[:, :triple_columns], contract_last, preferred_element_type=WIDE
    )
    late_steps = [teams - k for k, part in late]
    late = [part for k, part in late]
    d_normed_one, far, outer, late = lax.optimization_barrier((d_normed_one, far, outer, late))
    own_part = outer[:, :share]
    late = [moved(part, "dp", step) for part, step in zip(late, late_steps)]
    far[2] = moved(far[2], "dp", middle)
    g_gain_one = jnp.sum(d_normed_one * normal0, axis=0)
    g_shift_one = jnp.sum(d_normed_one, axis=0)
    g_gain_two = jnp.sum(d_normed_two * normal0, axis=0)
    g_shift_two = jnp.sum(d_normed_two, axis=0)
    d_sum = d_normed_one * norm_vals[0] + d_normed_two * norm_vals[2]
    d_hidden0 = (d_hidden1 + standardize_pull(d_sum, normal0, inverse0)).astype(LOW)
    grad_all = lax.all_to_all(d_hidden0, "dp", split_axis=1, concat_axis=0, tiled=True)
    grad_all, r_out, r_up = lax.optimization_barrier((grad_all, r_out, r_up))
    grad_all = lax.all_gather(grad_all, "sp", axis=0, tiled=True)
    grad_all, late, far, r_out, r_up = lax.optimization_barrier(
        (grad_all, late, far, r_out, r_up)
    )
    far[3] = moved(far[3], "dp", middle)
    target_ids = jnp.where(in_slice, local_ids, vocab_local)
    g_bias_triple = jnp.sum(d_joint.astype(WIDE), axis=0).reshape(span, 3, heads_here, head_dim)
    g_bias = jnp.concatenate(
        [
            g_bias_triple.transpose(0, 2, 1, 3).reshape(-1),
            jnp.sum(d_up.astype(WIDE), axis=0),
            g_bias_out,
        ]
    )
    g_norm = jnp.stack(
        [g_gain_one, g_shift_one, g_gain_two, g_shift_two, g_gain_final, g_shift_final], axis=1
    )
    g_extra = jnp.concatenate([g_norm, g_bias.reshape(width, bias_rows)], axis=1).astype(LOW)
    g_extra = jnp.pad(g_extra, ((0, 0), (0, LANES - g_extra.shape[1])))
    r_triple = scattered(jnp.concatenate([g_triple, g_extra], axis=1))
    grad_all, r_triple = lax.optimization_barrier((grad_all, r_triple))
    r_embed = (
        jnp.zeros(embed_table.shape, WIDE).at[target_ids].add(grad_all.astype(WIDE), mode="drop")
    )
    team_parts = [part.reshape(teams, slab, -1) for part in (r_triple, r_up, r_out)]
    r_layer = joined_teams(jnp.concatenate(team_parts, axis=2).reshape(teams * slab, -1))
    r_embed, far, late, arrived, own_part, r_layer = lax.optimization_barrier(
        (r_embed, far, late, arrived, own_part, r_layer)
    )
    r_layer = r_layer.astype(WIDE)
    up_start = triple_columns + LANES
    out_start = up_start + hidden_units
    r_up = r_layer[:, up_start:out_start]
    r_out = r_layer[:, out_start:].reshape(-1, width)
    r_triple = r_layer[:, :up_start]
    r_unembed = [own_part, *arrived, *late, jnp.concatenate(far, axis=0)]
    r_norm = r_triple[:, triple_columns : triple_columns + norm_rows].T
    r_bias = r_triple[
        :, triple_columns + norm_rows : triple_columns + norm_rows + bias_rows
    ].reshape(-1)
    r_triple = r_triple[:, :triple_columns].reshape(slab, span, 3, heads_here, head_dim)
    r_triple = r_triple.transpose(0, 1, 3, 2, 4).reshape(slab, triple_columns)
    r_in = jnp.concatenate([r_triple, r_up], axis=1)
    r_unembed = sum(part[:vocab_local].astype(WIDE) for part in r_unembed).T

    reduced = (r_embed, r_unembed, r_in, r_out, r_norm, r_bias)
    squares = jnp.float32(0.0)
    for grad_piece in reduced:
        squares = squares + jnp.sum(grad_piece * grad_piece)
    loss_term = jnp.where(sp_index == 0, loss_local, 0.0)
    totals = summed_over(jnp.stack([squares, loss_term]), ("sp", "dp"))
    squares_total, loss_total = totals[0], totals[1]
    grad_norm = jnp.sqrt(squares_total)
    mean_loss = loss_total / total_weight
    clip_factor = jnp.minimum(1.0, CLIP_LEVEL / (grad_norm + 1e-06))
    masters = (embed_table, unembed, proj_in, proj_out, norm_params, biases)
    firsts = (embed_first, unembed_first, proj_in_first, proj_out_first, norm_first, bias_first)
    seconds = (
        embed_second,
        unembed_second,
        proj_in_second,
        proj_out_second,
        norm_second,
        bias_second,
    )
    rates = (1.0, 0.05, 0.05, 0.1, 0.5, 0.5)
    decays = (WEIGHT_DECAY, WEIGHT_DECAY, WEIGHT_DECAY, WEIGHT_DECAY, 0.0, 0.0)
    results = []
    for index in range(6):
        results.extend(
            adam_update(
                masters[index],
                firsts[index],
                seconds[index],
                reduced[index],
                clip_factor,
                rates[index],
                decays[index],
            )
        )
    return (
        mean_loss,
        grad_norm,
        results[0],
        results[1],
        results[2],
        results[3],
        results[4],
        results[5],
        results[6],
        results[7],
        results[8],
        results[9],
        results[10],
        results[11],
        results[12],
        results[13],
        results[14],
        results[15],
        results[16],
        results[17],
    )


def solution(mesh):
    in_specs = (
        P("dp", None),
        P("dp", None),
        P(),
        P("sp", "dp"),
        P("sp", "dp"),
        P("sp", "dp"),
        P("dp", "sp"),
        P("dp", "sp"),
        P("dp", "sp"),
        P(("dp", "sp"), None),
        P(("dp", "sp"), None),
        P(("dp", "sp"), None),
        P(("dp", "sp"), None),
        P(("dp", "sp"), None),
        P(("dp", "sp"), None),
        P(None, ("dp", "sp")),
        P(None, ("dp", "sp")),
        P(None, ("dp", "sp")),
        P(("dp", "sp")),
        P(("dp", "sp")),
        P(("dp", "sp")),
    )
    out_specs = (
        P(),
        P(),
        P("sp", "dp"),
        P("sp", "dp"),
        P("sp", "dp"),
        P("dp", "sp"),
        P("dp", "sp"),
        P("dp", "sp"),
        P(("dp", "sp"), None),
        P(("dp", "sp"), None),
        P(("dp", "sp"), None),
        P(("dp", "sp"), None),
        P(("dp", "sp"), None),
        P(("dp", "sp"), None),
        P(None, ("dp", "sp")),
        P(None, ("dp", "sp")),
        P(None, ("dp", "sp")),
        P(("dp", "sp")),
        P(("dp", "sp")),
        P(("dp", "sp")),
    )
    return jax.shard_map(local, mesh=mesh, in_specs=in_specs, out_specs=out_specs, check_vma=False)
```
